32 devices in a mesh: wide: 8 (over z, x), head: 4 (over y, core).
Axes of the slice: x: 2, y: 2, z: 4, core: 2. Of those that a mesh axis runs over, the one named last changes fastest.
Arguments:
- hidden_in: bfloat16 [2048, 2048], P('wide'), may hold values from -6 to 6
- out_cotangent: bfloat16 [2048, 2048], P('wide'), may hold values from -6 to 6
- doc_lengths: int32 [8], replicated, may hold values from 1 to 1024, 2048 in all
- query_weight: bfloat16 [2048, 2048], P('wide', 'head'), may hold values from -0.125 to 0.125
- key_matrix: bfloat16 [2048, 1024], P('wide', 'head'), may hold values from -0.125 to 0.125
- value_matrix: bfloat16 [2048, 1024], P('wide', 'head'), may hold values from -0.125 to 0.125
- gate_weight: bfloat16 [2048, 2048], P('wide', 'head'), may hold values from -0.125 to 0.125
- out_weight: bfloat16 [2048, 2048], P('wide', 'head'), may hold values from -6 to 6
- ffn_gate_weight: bfloat16 [2048, 6144], P('wide', 'head'), may hold values from -0.125 to 0.125
- ffn_up_weight: bfloat16 [2048, 6144], P('wide', 'head'), may hold values from -0.125 to 0.125
- ffn_down_weight: bfloat16 [2048, 6144], P('wide', 'head'), may hold values from -0.078125 to 0.078125
- attn_gain: float32 [2048], replicated, may hold values from 0.5 to 2
- ffn_gain: float32 [2048], replicated, may hold values from 0.5 to 2
- query_gain: float32 [128], replicated, may hold values from 0.5 to 2
- key_gain: float32 [128], replicated, may hold values from 0.5 to 2
Outputs:
- layer_out: bfloat16 [2048, 2048], P('wide')
- input_grad: bfloat16 [2048, 2048], P('wide')
- query_weight_grad: float32 [2048, 2048], P('wide', 'head')
- key_weight_grad: float32 [2048, 1024], P('wide', 'head')
- value_weight_grad: float32 [2048, 1024], P('wide', 'head')
- gate_weight_grad: float32 [2048, 2048], P('wide', 'head')
- out_weight_grad: float32 [2048, 2048], P('wide', 'head')
- ffn_gate_weight_grad: float32 [2048, 6144], P('wide', 'head')
- ffn_up_weight_grad: float32 [2048, 6144], P('wide', 'head')
- ffn_down_weight_grad: float32 [2048, 6144], P('wide', 'head')
- attn_gain_grad: float32 [2048], replicated
- ffn_gain_grad: float32 [2048], replicated
- query_gain_grad: float32 [128], replicated
- key_gain_grad: float32 [128], replicated
The draws below stay inside these ranges and needn't reach their ends.
Inputs may be any that keep to these rules, and one draw needn't show every extreme that they name: `doc_lengths`: 8 documents packed in order fill the row of 2048 tokens; their lengths sum to 2048 and the longest has exactly 1024 tokens.
All inputs are finite; a program needn't handle non-finite values.
Results may differ from the reference program's by a relative error of at most 0.03.
Values may be sent and summed in bfloat16 or wider, within the bound.
No kernel may reach another device: no remote copies, remote signals or barrier semaphores. Data moves between devices by JAX's collectives and lax.ppermute only.
A program may use at most 128 MiB of HBM per device.

```python
import math
import jax
import jax.numpy as jnp
import numpy as np
from jax import lax

MODEL_WIDTH = 2048
QUERY_HEAD_COUNT = 16
KEY_VALUE_HEADS = 8
HEAD_WIDTH = 128
FF = 6144
DOCS = 8
PACKED_TOKENS = 2048
MOST = 1024


def strengthened(array, rng, source, target, shards_of, factor):
    def block_of(position):
        return (jnp.arange(array.shape[position]) // (array.shape[position] // shards_of)).reshape((-1,) + (1,) * (array.ndim - 1 - position))

    one_side = jax.random.permutation(rng, shards_of)[block_of(target)]
    far = (block_of(target) + shards_of // 2) % shards_of
    return jnp.where((block_of(source) == one_side) | (block_of(source) == far), factor * array, array)


def levels(own_key, dims, split, low, high):
    loudness = 1.0
    for dim, parts in split:
        draws = jax.random.uniform(jax.random.fold_in(jax.random.fold_in(own_key, 6), dim), (parts,), jnp.float32, low / len(split), high / len(split))
        loudness = loudness * jnp.repeat(jnp.exp(draws), dims[dim] // parts).reshape((-1,) + (1,) * (len(dims) - 1 - dim))
    return loudness


def profile(amount, total, reach, slope):
    weights = [(1 << 20) // math.isqrt(standing ** slope) + 1 for standing in range(2, amount + 1)]
    spare, given = total - reach - (amount - 1), [1] * (amount - 1)
    while spare > 0:
        candidates = [i for i in range(amount - 1) if given[i] < reach]
        pool, budget = sum([weights[i] for i in candidates]), spare
        for i in candidates:
            more = min(reach - given[i], max(1, budget * weights[i] // pool), spare)
            given[i] = given[i] + more
            spare = spare - more
    return np.array([reach] + given)


def ragged(key, number_of, total, bound, lean):
    if number_of == 2:
        one = jax.random.randint(key, (), max(1, total - bound), min(bound, total - 1) + 1)
        return jnp.stack([one, total - one])
    sizes = jnp.asarray(profile(number_of, total, bound, lean), jnp.int32)
    pairs = (number_of - 1) // 2
    giver, receiver = sizes[1:1 + 2 * pairs:2], sizes[2:2 + 2 * pairs:2]
    room = jnp.minimum(giver - 1, bound - receiver)
    passed = jax.random.randint(jax.random.fold_in(key, 1), (pairs,), 0, 1 << 20) % (room + 1)
    sizes = sizes.at[1:1 + 2 * pairs:2].set(giver - passed).at[2:2 + 2 * pairs:2].set(receiver + passed)
    return sizes[jax.random.permutation(jax.random.fold_in(key, 2), number_of)]


def noise(own_key, dims, spread, limit, shards=(), kind=jnp.bfloat16):
    factor_of = levels(own_key, dims, shards, -0.22, 0.18) if shards else 1.0
    array = jax.random.normal(own_key, dims, jnp.float32) * spread * factor_of
    return jnp.minimum(jnp.maximum(array, -limit), limit).astype(kind)


def bell_draw_with(own_key, extent, deviation, reach, cuts, heavy, held_as=jnp.bfloat16):
    array = deviation * jax.random.normal(own_key, extent, jnp.float32)
    if cuts:
        array = array * levels(own_key, extent, cuts, -0.22, 0.18)
    return jnp.clip(strengthened(array, jax.random.fold_in(own_key, 3), *heavy), -reach, reach).astype(held_as)


def setup_inputs(seed: int = 0) -> dict:
    streams_of = jax.random.split(jax.random.key(seed), 16)
    hidden_in = bell_draw_with(streams_of[0], (PACKED_TOKENS, MODEL_WIDTH), 1.0, 6.0, ((0, 8),), (0, 1, 8, 2.0))
    out_cotangent = bell_draw_with(streams_of[1], (PACKED_TOKENS, MODEL_WIDTH), 1.0, 6.0, ((0, 8),), (0, 1, 8, 2.0))
    doc_lengths = ragged(streams_of[2], DOCS, PACKED_TOKENS, MOST, 2).astype(jnp.int32)
    query_weight = noise(streams_of[3], (MODEL_WIDTH, QUERY_HEAD_COUNT * HEAD_WIDTH), MODEL_WIDTH ** -0.5, 0.125, ((0, 8), (1, 4)))
    key_matrix = noise(streams_of[4], (MODEL_WIDTH, KEY_VALUE_HEADS * HEAD_WIDTH), MODEL_WIDTH ** -0.5, 0.125, ((0, 8), (1, 4)))
    value_matrix = noise(streams_of[5], (MODEL_WIDTH, KEY_VALUE_HEADS * HEAD_WIDTH), MODEL_WIDTH ** -0.5, 0.125, ((0, 8), (1, 4)))
    gate_weight = noise(streams_of[6], (MODEL_WIDTH, QUERY_HEAD_COUNT * HEAD_WIDTH), MODEL_WIDTH ** -0.5, 0.125, ((0, 8), (1, 4)))
    out_weight = noise(streams_of[7], (MODEL_WIDTH, QUERY_HEAD_COUNT * HEAD_WIDTH), 1.0 ** -0.5, 6.0, ((0, 8), (1, 4)))
    ffn_gate_weight = noise(streams_of[8], (MODEL_WIDTH, FF), MODEL_WIDTH ** -0.5, 0.125, ((0, 8), (1, 4)))
    ffn_up_weight = noise(streams_of[9], (MODEL_WIDTH, FF), MODEL_WIDTH ** -0.5, 0.125, ((0, 8), (1, 4)))
    ffn_down_weight = noise(streams_of[10], (MODEL_WIDTH, FF), FF ** -0.5, 0.078125, ((0, 8), (1, 4)))
    attn_gain = jnp.clip(jax.random.uniform(streams_of[11], (MODEL_WIDTH,), jnp.float32, 0.5, 2.0), 0.5, 2.0)
    ffn_gain = jnp.clip(jax.random.uniform(streams_of[12], (MODEL_WIDTH,), jnp.float32, 0.5, 2.0), 0.5, 2.0)
    query_gain = jnp.clip(jax.random.uniform(streams_of[13], (HEAD_WIDTH,), jnp.float32, 0.5, 2.0), 0.5, 2.0)
    key_gain = jnp.clip(jax.random.uniform(streams_of[14], (HEAD_WIDTH,), jnp.float32, 0.5, 2.0), 0.5, 2.0)
    return dict(hidden_in=hidden_in, out_cotangent=out_cotangent, doc_lengths=doc_lengths, query_weight=query_weight, key_matrix=key_matrix, value_matrix=value_matrix, gate_weight=gate_weight, out_weight=out_weight, ffn_gate_weight=ffn_gate_weight, ffn_up_weight=ffn_up_weight, ffn_down_weight=ffn_down_weight, attn_gain=attn_gain, ffn_gain=ffn_gain, query_gain=query_gain, key_gain=key_gain)


@jax.custom_vjp
def reduced_precision(v):
    return lax.optimization_barrier(v.astype(jnp.bfloat16)).astype(jnp.float32)

@jax.custom_vjp
def reduced_backward(v):
    return v

def low_keep(v):
    return (reduced_precision(v), None)

def low_pass(kept, grad):
    return (grad,)

def back_keep(v):
    return (v, None)

def back_low(kept, grad):
    return (reduced_precision(grad),)
reduced_precision.defvjp(low_keep, low_pass)
reduced_backward.defvjp(back_keep, back_low)
epsilon = 1e-06
rope_base = 1000000.0
highest = lax.Precision.HIGHEST

def segment_of(lengths, token_ids):
    doc_ends = jnp.cumsum(lengths).astype(jnp.int32)
    return lax.optimization_barrier(jnp.sum((token_ids[:, None] >= doc_ends[None, :]).astype(jnp.int32), axis=1)).astype(jnp.int32)

def doc_tables(lengths, token_ids):
    doc_ends = jnp.cumsum(lengths).astype(jnp.int32)
    starts = (doc_ends - lengths).astype(jnp.int32)
    segment = segment_of(lengths, token_ids)
    labels = jnp.arange(lengths.shape[0], dtype=jnp.int32)
    doc_begin = lax.optimization_barrier(jnp.sum(jnp.where(segment[:, None] == labels[None, :], starts[None, :], 0), axis=1)).astype(jnp.int32)
    return (segment, (token_ids - doc_begin).astype(jnp.int32))

def rope_tables(positions, head_size):
    half_size = head_size // 2
    frequency = rope_base ** (-2.0 * jnp.arange(half_size, dtype=jnp.float32) / head_size)
    angles = positions.astype(jnp.float32)[:, None] * frequency[None, :]
    cosine = jnp.cos(angles)
    sine_table = jnp.sin(angles)
    return (jnp.concatenate([cosine, cosine], axis=1), jnp.concatenate([sine_table, sine_table], axis=1))

def rotate_half(values):
    half_size = values.shape[-1] // 2
    return jnp.concatenate([-values[..., half_size:], values[..., :half_size]], axis=-1)

def apply_rope(values, cos_table, sin_table):
    return values * cos_table[:, None, :] + rotate_half(values) * sin_table[:, None, :]

def rms_norm(values, gain):
    return values * lax.rsqrt(lax.optimization_barrier(jnp.mean(values * values, axis=-1, keepdims=True)) + epsilon) * gain

def matrix_product(left, right):
    return jnp.dot(left, right, precision=highest, preferred_element_type=jnp.float32)

def matmul_t(left, right):
    return lax.dot_general(left, right, (((1,), (1,)), ((), ())), precision=highest, preferred_element_type=jnp.float32)

def attend_block(query_block, key_head, value_head, query_seg, query_ids, key_seg, key_ids):
    score_scale = HEAD_WIDTH ** (-0.5)
    scores = jnp.einsum('gqd,kd->gqk', query_block, key_head, precision=highest) * score_scale
    scores = reduced_backward(scores)
    allowed = (query_seg[:, None] == key_seg[None, :]) & (key_ids[None, :] <= query_ids[:, None])
    scores = jnp.where(allowed[None], scores, -1e+30)
    weights = jax.nn.softmax(scores, axis=-1)
    return jnp.einsum('gqk,kd->gqd', reduced_precision(weights), value_head, precision=highest)

def attention(rotated_queries, keys_rot, every_value, segment, token_ids):
    group_width = QUERY_HEAD_COUNT // KEY_VALUE_HEADS
    query_tile_rows = 1024 if PACKED_TOKENS % 1024 == 0 else PACKED_TOKENS
    block_list = PACKED_TOKENS // query_tile_rows
    grouped_rows = rotated_queries.reshape(block_list, query_tile_rows, KEY_VALUE_HEADS, group_width, HEAD_WIDTH).transpose(2, 0, 3, 1, 4)
    seg_blocks = segment.reshape(block_list, query_tile_rows)
    id_blocks = token_ids.reshape(block_list, query_tile_rows)
    key_heads = keys_rot.transpose(1, 0, 2)
    value_heads = every_value.transpose(1, 0, 2)
    block_fn = jax.checkpoint(attend_block)

    def per_head(head_items):
        head_queries, key_head, value_head = head_items

        def per_block(block_parts):
            query_block, query_seg, query_ids = block_parts
            return block_fn(query_block, key_head, value_head, query_seg, query_ids, segment, token_ids)
        return lax.map(per_block, (head_queries, seg_blocks, id_blocks))
    result = lax.map(per_head, (grouped_rows, key_heads, value_heads))
    return result.transpose(1, 3, 0, 2, 4).reshape(PACKED_TOKENS, QUERY_HEAD_COUNT, HEAD_WIDTH)

def layer(hidden, query_weight, key_matrix, value_matrix, gate_weight, out_weight, ffn_gate_weight, ffn_up_weight, ffn_down_weight, attn_gain, ffn_gain, query_gain, key_gain, segment, token_ids, cos_table, sin_table):
    normed_input = reduced_precision(rms_norm(hidden, attn_gain))
    query_pre = reduced_backward(matrix_product(normed_input, query_weight)).reshape(PACKED_TOKENS, QUERY_HEAD_COUNT, HEAD_WIDTH)
    key_before_norm = reduced_backward(matrix_product(normed_input, key_matrix)).reshape(PACKED_TOKENS, KEY_VALUE_HEADS, HEAD_WIDTH)
    every_value = reduced_backward(reduced_precision(matrix_product(normed_input, value_matrix))).reshape(PACKED_TOKENS, KEY_VALUE_HEADS, HEAD_WIDTH)
    gate_pre = reduced_backward(matrix_product(normed_input, gate_weight))
    rotated_queries = reduced_backward(reduced_precision(apply_rope(rms_norm(query_pre, query_gain), cos_table, sin_table)))
    keys_rot = reduced_backward(reduced_precision(apply_rope(rms_norm(key_before_norm, key_gain), cos_table, sin_table)))
    attended = reduced_backward(attention(rotated_queries, keys_rot, every_value, segment, token_ids)).reshape(PACKED_TOKENS, QUERY_HEAD_COUNT * HEAD_WIDTH)
    gated = reduced_precision(attended * jax.nn.sigmoid(gate_pre))
    branch = reduced_backward(matmul_t(gated, out_weight))
    middle = hidden + branch
    normed_two = reduced_precision(rms_norm(middle, ffn_gain))
    ffn_gate_pre = reduced_backward(matrix_product(normed_two, ffn_gate_weight))
    ffn_up_pre = reduced_backward(matrix_product(normed_two, ffn_up_weight))
    hidden_act = reduced_precision(jax.nn.silu(ffn_gate_pre) * ffn_up_pre)
    return middle + matmul_t(hidden_act, ffn_down_weight)

def reference(hidden_in, out_cotangent, doc_lengths, query_weight, key_matrix, value_matrix, gate_weight, out_weight, ffn_gate_weight, ffn_up_weight, ffn_down_weight, attn_gain, ffn_gain, query_gain, key_gain):
    token_ids = jnp.arange(PACKED_TOKENS, dtype=jnp.int32)
    segment, positions = doc_tables(doc_lengths, token_ids)
    cos_table, sin_table = rope_tables(positions, HEAD_WIDTH)

    def forward(hidden, wquery, wkey, wvalue, wgate, wout, wfgate, wfup, wfdown, gain_one, gain_two, gain_query, gain_key):
        return layer(hidden, wquery, wkey, wvalue, wgate, wout, wfgate, wfup, wfdown, gain_one, gain_two, gain_query, gain_key, segment, token_ids, cos_table, sin_table)
    output, pullback = jax.vjp(forward, hidden_in.astype(jnp.float32), query_weight.astype(jnp.float32), key_matrix.astype(jnp.float32), value_matrix.astype(jnp.float32), gate_weight.astype(jnp.float32), out_weight.astype(jnp.float32), ffn_gate_weight.astype(jnp.float32), ffn_up_weight.astype(jnp.float32), ffn_down_weight.astype(jnp.float32), attn_gain, ffn_gain, query_gain, key_gain)
    grads = pullback(out_cotangent.astype(jnp.float32))
    return (output.astype(jnp.bfloat16), grads[0].astype(jnp.bfloat16), grads[1], grads[2], grads[3], grads[4], grads[5], grads[6], grads[7], grads[8], grads[9], grads[10], grads[11], grads[12])
```

```python
import jax
import jax.numpy as jnp
from jax import lax
from jax.sharding import Mesh
from jax.sharding import PartitionSpec as P

HEAD_WIDTH = 128


epsilon = 1e-06
rope_base = 1000000.0
masked_score = -1e30


def segment_of(lengths, token_ids):
    doc_ends = jnp.cumsum(lengths)
    return jnp.sum((token_ids[:, None] >= doc_ends[None, :]).astype(jnp.int32), axis=1)


def doc_tables(lengths, token_ids):
    doc_ends = jnp.cumsum(lengths)
    starts = doc_ends - lengths
    segment = segment_of(lengths, token_ids)
    labels = jnp.arange(lengths.shape[0], dtype=jnp.int32)
    doc_begin = jnp.sum(jnp.where(segment[:, None] == labels[None, :], starts[None, :], 0), axis=1)
    return (segment, token_ids - doc_begin)


def rope_tables(positions, head_size):
    half_size = head_size // 2
    frequency = rope_base ** (-2.0 * jnp.arange(half_size, dtype=jnp.float32) / head_size)
    angles = positions.astype(jnp.float32)[:, None] * frequency[None, :]
    cosine = jnp.cos(angles)
    sine_table = jnp.sin(angles)
    return (
        jnp.concatenate([cosine, cosine], axis=1),
        jnp.concatenate([sine_table, sine_table], axis=1),
    )


def rotate_half(values):
    half_size = values.shape[-1] // 2
    return jnp.concatenate([-values[..., half_size:], values[..., :half_size]], axis=-1)


def rotate_back(values):
    half_size = values.shape[-1] // 2
    return jnp.concatenate([values[..., half_size:], -values[..., :half_size]], axis=-1)


def apply_rope(values, cos_table, sin_table):
    return values * cos_table[:, None, :] + rotate_half(values) * sin_table[:, None, :]


def rope_back(grads, cos_table, sin_table):
    return grads * cos_table[:, None, :] + rotate_back(grads * sin_table[:, None, :])


def contract_last(left, right):
    return lax.dot_general(
        left, right, (((1,), (1,)), ((), ())), preferred_element_type=jnp.float32
    )


def contract_first(left, right):
    return lax.dot_general(
        left, right, (((0,), (0,)), ((), ())), preferred_element_type=jnp.float32
    )


def norm_back(grad_out, inputs, inv_root, gain):
    scaled = grad_out * gain
    return inv_root * scaled - inputs * inv_root**3 * jnp.mean(
        scaled * inputs, axis=-1, keepdims=True
    )


def on_device(
    hidden_in,
    out_cotangent,
    doc_lengths,
    query_weight,
    key_matrix,
    value_matrix,
    gate_weight,
    out_weight,
    ffn_gate_weight,
    ffn_up_weight,
    ffn_down_weight,
    attn_gain,
    ffn_gain,
    query_gain,
    key_gain,
):
    tok_rows = hidden_in.shape[0]
    row_length = tok_rows * lax.axis_size("wide")
    first_row = lax.axis_index("wide") * tok_rows
    token_ids = first_row + jnp.arange(tok_rows, dtype=jnp.int32)
    segment, positions = doc_tables(doc_lengths, token_ids)
    shard_begin = first_row - positions[0]
    shard_last = first_row + tok_rows - 1
    cos_table, sin_table = rope_tables(positions, HEAD_WIDTH)
    local_heads = query_weight.shape[1] // HEAD_WIDTH
    kv_heads = key_matrix.shape[1] // HEAD_WIDTH
    group_width = local_heads // kv_heads
    query_rows = group_width * tok_rows
    score_scale = HEAD_WIDTH ** (-0.5)
    (
        full_query,
        full_key,
        full_value,
        full_gate,
        full_out,
        full_ffn_gate,
        full_ffn_up,
        full_ffn_down,
    ) = (
        lax.all_gather(query_weight, "wide", axis=0, tiled=True),
        lax.all_gather(key_matrix, "wide", axis=0, tiled=True),
        lax.all_gather(value_matrix, "wide", axis=0, tiled=True),
        lax.all_gather(gate_weight, "wide", axis=0, tiled=True),
        lax.all_gather(out_weight, "wide", axis=0, tiled=True),
        lax.all_gather(ffn_gate_weight, "wide", axis=0, tiled=True),
        lax.all_gather(ffn_up_weight, "wide", axis=0, tiled=True),
        lax.all_gather(ffn_down_weight, "wide", axis=0, tiled=True),
    )
    hidden32 = hidden_in.astype(jnp.float32)
    inv_one = lax.rsqrt(jnp.mean(hidden32 * hidden32, axis=1, keepdims=True) + epsilon)
    normed_input = (hidden32 * inv_one * attn_gain).astype(jnp.bfloat16)
    query_pre = jnp.dot(normed_input, full_query, preferred_element_type=jnp.float32).reshape(
        tok_rows, local_heads, HEAD_WIDTH
    )
    key_before_norm = jnp.dot(normed_input, full_key, preferred_element_type=jnp.float32).reshape(
        tok_rows, kv_heads, HEAD_WIDTH
    )
    value_rows = jnp.dot(normed_input, full_value, preferred_element_type=jnp.float32).astype(
        jnp.bfloat16
    )
    gate_pre = jnp.dot(normed_input, full_gate, preferred_element_type=jnp.float32)
    inv_query = lax.rsqrt(jnp.mean(query_pre * query_pre, axis=-1, keepdims=True) + epsilon)
    inv_key = lax.rsqrt(
        jnp.mean(key_before_norm * key_before_norm, axis=-1, keepdims=True) + epsilon
    )
    query_unit = query_pre * inv_query
    key_unit = key_before_norm * inv_key
    query_rot = apply_rope(query_unit * query_gain, cos_table, sin_table).astype(jnp.bfloat16)
    key_rows = (
        apply_rope(key_unit * key_gain, cos_table, sin_table)
        .astype(jnp.bfloat16)
        .reshape(tok_rows, kv_heads * HEAD_WIDTH)
    )
    query_heads = (
        query_rot.reshape(tok_rows, kv_heads, group_width, HEAD_WIDTH)
        .transpose(1, 2, 0, 3)
        .reshape(kv_heads, query_rows, HEAD_WIDTH)
    )
    query_seg = jnp.tile(segment, group_width)
    query_ids = jnp.tile(token_ids, group_width)
    start_state = (
        jnp.full((kv_heads, query_rows), masked_score, jnp.float32),
        jnp.zeros((kv_heads, query_rows), jnp.float32),
        jnp.zeros((kv_heads, query_rows, HEAD_WIDTH), jnp.float32),
    )
    key_piece = lax.all_gather(key_rows, "wide", axis=0, tiled=True)
    value_piece = lax.all_gather(value_rows, "wide", axis=0, tiled=True)
    count = key_piece.shape[0]
    step_rows = 512
    steps_count = count // step_rows
    key_ids = jnp.arange(count, dtype=jnp.int32)
    key_seg = segment_of(doc_lengths, key_ids)
    key_blocks = key_piece.reshape(steps_count, step_rows, kv_heads, HEAD_WIDTH).transpose(
        0, 2, 1, 3
    )
    value_blocks = value_piece.reshape(steps_count, step_rows, kv_heads, HEAD_WIDTH).transpose(
        0, 2, 1, 3
    )

    def inner(state, block):
        key_block, value_block, block_seg, block_ids = block

        def inner_work(state_in):
            scores = (
                jnp.einsum(
                    "hqd,hkd->hqk", query_heads, key_block, preferred_element_type=jnp.float32
                )
                * score_scale
            )
            allowed = (
                (query_seg[:, None] == block_seg[None, :])
                & (block_ids[None, :] <= query_ids[:, None])
            )[None]
            scores = jnp.where(allowed, scores, masked_score)
            running, total, accum = state_in
            newest = jnp.maximum(running, jnp.max(scores, axis=-1))
            factor = jnp.exp(running - newest)
            weights = jnp.where(allowed, jnp.exp(scores - newest[..., None]), 0.0)
            total = total * factor + jnp.sum(weights, axis=-1)
            accum = accum * factor[..., None] + jnp.einsum(
                "hqk,hkd->hqd",
                weights.astype(jnp.bfloat16),
                value_block,
                preferred_element_type=jnp.float32,
            )
            return (newest, total, accum)

        useful = (block_ids[0] <= shard_last) & (block_ids[step_rows - 1] >= shard_begin)
        return (lax.cond(useful, inner_work, lambda state_in: state_in, state), None)

    state, unused = lax.scan(
        inner,
        start_state,
        (
            key_blocks,
            value_blocks,
            key_seg.reshape(steps_count, step_rows),
            key_ids.reshape(steps_count, step_rows),
        ),
    )
    running, total, accum = state
    attended_heads = accum / total[..., None]
    log_total = running + jnp.log(total)
    attended = (
        attended_heads.reshape(kv_heads, group_width, tok_rows, HEAD_WIDTH)
        .transpose(2, 0, 1, 3)
        .reshape(tok_rows, local_heads * HEAD_WIDTH)
    )
    gate_sig = jax.nn.sigmoid(gate_pre)
    gated = (attended * gate_sig).astype(jnp.bfloat16)
    branch = lax.psum(contract_last(gated, full_out).astype(jnp.bfloat16), "head").astype(
        jnp.float32
    )
    middle = hidden32 + branch
    inv_two = lax.rsqrt(jnp.mean(middle * middle, axis=1, keepdims=True) + epsilon)
    normed_two = (middle * inv_two * ffn_gain).astype(jnp.bfloat16)
    ffn_gate_pre = jnp.dot(normed_two, full_ffn_gate, preferred_element_type=jnp.float32)
    ffn_up_pre = jnp.dot(normed_two, full_ffn_up, preferred_element_type=jnp.float32)
    gate_act = jax.nn.sigmoid(ffn_gate_pre)
    silu_gate = ffn_gate_pre * gate_act
    hidden_act = (silu_gate * ffn_up_pre).astype(jnp.bfloat16)
    ffn_out = lax.psum(
        contract_last(hidden_act, full_ffn_down).astype(jnp.bfloat16), "head"
    ).astype(jnp.float32)
    layer_out = (middle + ffn_out).astype(jnp.bfloat16)
    grad32 = out_cotangent.astype(jnp.float32)
    grad_hidden = jnp.dot(out_cotangent, full_ffn_down, preferred_element_type=jnp.float32)
    grad_ffn_gate = (
        grad_hidden * ffn_up_pre * gate_act * (1.0 + ffn_gate_pre * (1.0 - gate_act))
    ).astype(jnp.bfloat16)
    grad_ffn_up = (grad_hidden * silu_gate).astype(jnp.bfloat16)
    grad_normed_two = lax.psum(
        (
            contract_last(grad_ffn_gate, full_ffn_gate) + contract_last(grad_ffn_up, full_ffn_up)
        ).astype(jnp.bfloat16),
        "head",
    ).astype(jnp.float32)
    grad_middle = grad32 + norm_back(grad_normed_two, middle, inv_two, ffn_gain)
    grad_branch = grad_middle.astype(jnp.bfloat16)
    grad_gated = jnp.dot(grad_branch, full_out, preferred_element_type=jnp.float32)
    grad_attended = (grad_gated * gate_sig).astype(jnp.bfloat16)
    grad_gate_pre = (grad_gated * attended * gate_sig * (1.0 - gate_sig)).astype(jnp.bfloat16)
    grad_heads = (
        grad_attended.reshape(tok_rows, kv_heads, group_width, HEAD_WIDTH)
        .transpose(1, 2, 0, 3)
        .reshape(kv_heads, query_rows, HEAD_WIDTH)
    )
    delta = jnp.sum(grad_heads.astype(jnp.float32) * attended_heads, axis=-1)
    all_keys, all_values = key_piece, value_piece
    key_step = 512
    key_count = row_length // key_step
    all_ids = jnp.arange(row_length, dtype=jnp.int32)
    all_seg = segment_of(doc_lengths, all_ids)
    key_blocks = all_keys.reshape(key_count, key_step, kv_heads, HEAD_WIDTH).transpose(0, 2, 1, 3)
    value_blocks = all_values.reshape(key_count, key_step, kv_heads, HEAD_WIDTH).transpose(
        0, 2, 1, 3
    )
    key_scan_items = (
        key_blocks,
        value_blocks,
        all_seg.reshape(key_count, key_step),
        all_ids.reshape(key_count, key_step),
    )
    zero_query = jnp.zeros((kv_heads, query_rows, HEAD_WIDTH), jnp.float32)

    def block_terms(key_block, value_block, block_seg, block_ids):
        scores = (
            jnp.einsum("hqd,hkd->hqk", query_heads, key_block, preferred_element_type=jnp.float32)
            * score_scale
        )
        allowed = (
            (query_seg[:, None] == block_seg[None, :]) & (block_ids[None, :] <= query_ids[:, None])
        )[None]
        weights = jnp.where(
            allowed, jnp.exp(jnp.where(allowed, scores, masked_score) - log_total[..., None]), 0.0
        )
        grad_weights = jnp.einsum(
            "hqd,hkd->hqk", grad_heads, value_block, preferred_element_type=jnp.float32
        )
        grad_scores = (weights * (grad_weights - delta[..., None])).astype(jnp.bfloat16)
        return (weights, grad_scores)

    def block_useful(block_ids):
        return (block_ids[0] <= shard_last) & (block_ids[key_step - 1] >= shard_begin)

    def back_block(grad_query, block):
        key_block, value_block, block_seg, block_ids = block

        def back_work(grad_in):
            weights, grad_scores = block_terms(key_block, value_block, block_seg, block_ids)
            grad_out = (
                grad_in
                + jnp.einsum(
                    "hqk,hkd->hqd", grad_scores, key_block, preferred_element_type=jnp.float32
                )
                * score_scale
            )
            grad_key = (
                jnp.einsum(
                    "hqk,hqd->hkd", grad_scores, query_heads, preferred_element_type=jnp.float32
                )
                * score_scale
            )
            grad_value = jnp.einsum(
                "hqk,hqd->hkd",
                weights.astype(jnp.bfloat16),
                grad_heads,
                preferred_element_type=jnp.float32,
            )
            return (grad_out, (grad_key, grad_value))

        def skip(grad_in):
            nothing = jnp.zeros((kv_heads, key_step, HEAD_WIDTH), jnp.float32)
            return (grad_in, (nothing, nothing))

        return lax.cond(block_useful(block_ids), back_work, skip, grad_query)

    grad_query, (key_parts, value_parts) = lax.scan(back_block, zero_query, key_scan_items)
    key_grad_rows = key_parts.transpose(0, 2, 1, 3).reshape(row_length, kv_heads * HEAD_WIDTH)
    value_grad_rows = value_parts.transpose(0, 2, 1, 3).reshape(row_length, kv_heads * HEAD_WIDTH)
    key_total, value_total = (
        lax.psum_scatter(
            key_grad_rows.astype(jnp.bfloat16), "wide", scatter_dimension=0, tiled=True
        ).astype(jnp.float32),
        lax.psum_scatter(
            value_grad_rows.astype(jnp.bfloat16), "wide", scatter_dimension=0, tiled=True
        ).astype(jnp.float32),
    )
    grad_values = value_total.astype(jnp.bfloat16)
    grad_key_rot = (
        key_total.astype(jnp.bfloat16).astype(jnp.float32).reshape(tok_rows, kv_heads, HEAD_WIDTH)
    )
    grad_query_rot = (
        grad_query.astype(jnp.bfloat16)
        .astype(jnp.float32)
        .reshape(kv_heads, group_width, tok_rows, HEAD_WIDTH)
        .transpose(2, 0, 1, 3)
        .reshape(tok_rows, local_heads, HEAD_WIDTH)
    )
    grad_query_unit = rope_back(grad_query_rot, cos_table, sin_table)
    grad_key_unit = rope_back(grad_key_rot, cos_table, sin_table)
    query_gain_part = jnp.sum(grad_query_unit * query_unit, axis=(0, 1))
    key_gain_part = jnp.sum(grad_key_unit * key_unit, axis=(0, 1))
    grad_query_pre = (
        norm_back(grad_query_unit, query_pre, inv_query, query_gain)
        .reshape(tok_rows, local_heads * HEAD_WIDTH)
        .astype(jnp.bfloat16)
    )
    grad_key_pre = (
        norm_back(grad_key_unit, key_before_norm, inv_key, key_gain)
        .reshape(tok_rows, kv_heads * HEAD_WIDTH)
        .astype(jnp.bfloat16)
    )
    grad_normed_part = (
        contract_last(grad_query_pre, full_query)
        + contract_last(grad_key_pre, full_key)
        + contract_last(grad_values, full_value)
        + contract_last(grad_gate_pre, full_gate)
    )
    grad_normed = lax.psum(grad_normed_part.astype(jnp.bfloat16), "head").astype(jnp.float32)
    input_grad = (grad_middle + norm_back(grad_normed, hidden32, inv_one, attn_gain)).astype(
        jnp.bfloat16
    )
    attn_gain_part = jnp.sum(grad_normed * hidden32 * inv_one, axis=0)
    ffn_gain_part = jnp.sum(grad_normed_two * middle * inv_two, axis=0)
    weight_grads = lax.psum_scatter(
        jnp.concatenate(
            [
                contract_first(normed_input, grad_query_pre),
                contract_first(normed_input, grad_key_pre),
                contract_first(normed_input, grad_values),
                contract_first(normed_input, grad_gate_pre),
                contract_first(grad_branch, gated),
                contract_first(normed_two, grad_ffn_gate),
                contract_first(normed_two, grad_ffn_up),
                contract_first(out_cotangent, hidden_act),
            ],
            axis=1,
        ).astype(jnp.bfloat16),
        "wide",
        scatter_dimension=0,
        tiled=True,
    ).astype(jnp.float32)
    col_widths = [
        query_weight.shape[1],
        key_matrix.shape[1],
        value_matrix.shape[1],
        gate_weight.shape[1],
        out_weight.shape[1],
        ffn_gate_weight.shape[1],
        ffn_up_weight.shape[1],
        ffn_down_weight.shape[1],
    ]
    pieces = []
    offset = 0
    for width in col_widths:
        pieces.append(weight_grads[:, offset : offset + width])
        offset = offset + width
    head_first = (lax.axis_index("head") == 0).astype(jnp.float32)
    attn_gain_grad, ffn_gain_grad, query_gain_grad, key_gain_grad = lax.psum(
        (attn_gain_part * head_first, ffn_gain_part * head_first, query_gain_part, key_gain_part),
        ("wide", "head"),
    )
    return (
        layer_out,
        input_grad,
        pieces[0],
        pieces[1],
        pieces[2],
        pieces[3],
        pieces[4],
        pieces[5],
        pieces[6],
        pieces[7],
        attn_gain_grad,
        ffn_gain_grad,
        query_gain_grad,
        key_gain_grad,
    )


PLANES = 4


def pair_swap(values, axis):
    return lax.ppermute(values, axis, [(0, 1), (1, 0)])


def plane_swap(values, step):
    return lax.ppermute(values, "z", [(i, i ^ step) for i in range(PLANES)])


def gather_chunks(chunk):
    columns = [chunk] + [plane_swap(chunk, step) for step in range(1, PLANES)]
    return jnp.concatenate(columns + [pair_swap(piece, "y") for piece in columns], axis=0)


def sum_chunks(parts):
    rows = parts.shape[0] // (2 * PLANES)
    total = None
    for step in (2, 3, 1, 0):
        other = PLANES + step
        got = pair_swap(parts[other * rows : (other + 1) * rows], "y")
        both = parts[step * rows : (step + 1) * rows].astype(jnp.float32) + got.astype(jnp.float32)
        if step:
            both = plane_swap(both.astype(jnp.bfloat16), step).astype(jnp.float32)
        total = both if total is None else total + both
    return total


def flip_if(values, axis, flag):
    return jnp.where(flag, jnp.flip(values, axis), values)


def to_own_first(values, flag):
    lead = values.shape[:-1]
    width = values.shape[-1]
    split = values.reshape(lead + (PLANES, 2, width // (2 * PLANES)))
    zero = split[..., 0, :].reshape(lead + (width // 2,))
    one = split[..., 1, :].reshape(lead + (width // 2,))
    return jnp.concatenate([jnp.where(flag, one, zero), jnp.where(flag, zero, one)], axis=-1)


def from_own_first(values, flag):
    lead = values.shape[:-1]
    width = values.shape[-1]
    block = width // (2 * PLANES)
    own = values[..., : width // 2].reshape(lead + (PLANES, block))
    other = values[..., width // 2 :].reshape(lead + (PLANES, block))
    pair = jnp.stack([jnp.where(flag, other, own), jnp.where(flag, own, other)], axis=-2)
    return pair.reshape(lead + (width,))


def spread_weight(local):
    rows, planes, width = local.shape
    mine = lax.all_to_all(
        local.reshape(rows, planes * width), "z", split_axis=1, concat_axis=0, tiled=True
    )
    mine = jnp.concatenate([mine, pair_swap(mine, "x")], axis=0)
    return mine, pair_swap(mine, "c")


def collect_grad(mine, other):
    half = mine.shape[0] // 2
    both = mine.astype(jnp.float32) + pair_swap(other, "c").astype(jnp.float32)
    both = both.astype(jnp.bfloat16)
    rows = both[:half].astype(jnp.float32) + pair_swap(both[half:], "x").astype(jnp.float32)
    back = lax.all_to_all(
        rows.astype(jnp.bfloat16), "z", split_axis=0, concat_axis=1, tiled=True
    )
    return back.reshape(half // PLANES, PLANES, mine.shape[1])


def head_norm(pre, gain):
    inverse = lax.rsqrt(jnp.mean(pre * pre, axis=-1, keepdims=True) + epsilon)
    unit = pre * inverse
    return inverse, unit, unit * gain


def on_slice_device(
    hidden_in,
    out_cotangent,
    doc_lengths,
    query_weight,
    key_matrix,
    value_matrix,
    gate_weight,
    out_weight,
    ffn_gate_weight,
    ffn_up_weight,
    ffn_down_weight,
    attn_gain,
    ffn_gain,
    query_gain,
    key_gain,
):
    bf16, f32 = jnp.bfloat16, jnp.float32
    block_rows, width = hidden_in.shape
    chunk_rows = block_rows // 4
    z, x, y, c = (lax.axis_index(name) for name in ("z", "x", "y", "c"))
    odd_x, odd_c = x == 1, c == 1
    score_scale = HEAD_WIDTH ** (-0.5)

    def by_head(weight, inner):
        return weight.reshape(block_rows, 2, inner, HEAD_WIDTH)

    queries, gates = by_head(query_weight, 2), by_head(gate_weight, 2)
    keys, vals = by_head(key_matrix, 1), by_head(value_matrix, 1)
    half_zero = jnp.concatenate([queries[:, :, 0], gates[:, :, 0], keys[:, :, 0]], axis=-1)
    half_one = jnp.concatenate([queries[:, :, 1], gates[:, :, 1], vals[:, :, 0]], axis=-1)
    kept = jnp.where(odd_c, half_one, half_zero)
    taken = pair_swap(jnp.where(odd_c, half_zero, half_one), "c")
    attn_local = jnp.concatenate(
        [jnp.where(odd_c, taken, kept), jnp.where(odd_c, kept, taken)], axis=1
    )
    attn_mine, attn_other = spread_weight(attn_local)

    chunk_start = (y * 2 + c) * chunk_rows
    own_hidden = lax.dynamic_slice_in_dim(hidden_in, chunk_start, chunk_rows, 0)
    own_cotangent = lax.dynamic_slice_in_dim(out_cotangent, chunk_start, chunk_rows, 0)
    hidden32 = to_own_first(own_hidden, odd_x).astype(f32)
    cotangent = to_own_first(own_cotangent, odd_x)
    gain_one = to_own_first(attn_gain, odd_x)
    gain_two = to_own_first(ffn_gain, odd_x)
    inv_one = lax.rsqrt(jnp.mean(hidden32 * hidden32, axis=1, keepdims=True) + epsilon)
    normed_chunk = (hidden32 * inv_one * gain_one).astype(bf16)
    normed = gather_chunks(normed_chunk)
    tokens = normed.shape[0]

    def ids_of(x_at, c_at):
        step = jnp.arange(2 * PLANES, dtype=jnp.int32)
        z_at, y_at = z ^ (step % PLANES), y ^ (step // PLANES)
        start = (z_at * 2 + x_at) * block_rows + (y_at * 2 + c_at) * chunk_rows
        return (start[:, None] + jnp.arange(chunk_rows, dtype=jnp.int32)[None, :]).reshape(-1)

    query_ids = ids_of(x, c)
    key_ids = jnp.concatenate([query_ids, ids_of(x ^ 1, c), ids_of(x, c ^ 1), ids_of(x ^ 1, c ^ 1)])
    query_seg, positions = doc_tables(doc_lengths, query_ids)
    key_seg = segment_of(doc_lengths, key_ids)
    cos_table, sin_table = rope_tables(positions, HEAD_WIDTH)
    cos_rows, sin_rows = cos_table, sin_table

    def turn(values):
        return values * cos_rows + rotate_half(values) * sin_rows

    def turn_back(grads):
        return grads * cos_rows + rotate_back(grads * sin_rows)

    mine = jnp.dot(normed, attn_mine, preferred_element_type=f32)
    other = jnp.dot(normed, attn_other, preferred_element_type=f32)
    low, high = HEAD_WIDTH, 2 * HEAD_WIDTH
    key_pre = jnp.where(odd_c, other[:, high:], mine[:, high:])
    value_rows = jnp.where(odd_c, mine[:, high:], other[:, high:]).astype(bf16)
    inv_key, key_unit, key_scaled = head_norm(key_pre, key_gain)
    key_rows = turn(key_scaled).astype(bf16)
    pair = jnp.concatenate([key_rows, value_rows], axis=1)
    pair_x = pair_swap(pair, "x")
    both_x = jnp.concatenate([pair, pair_x], axis=0)
    all_pairs = jnp.concatenate([both_x, pair_swap(both_x, "c")], axis=0)
    all_keys, all_values = all_pairs[:, :low], all_pairs[:, low:]

    query_pre = jnp.stack([mine[:, :low], other[:, :low]])
    gate_pre = jnp.stack([mine[:, low:high], other[:, low:high]])
    inv_query, query_unit, query_scaled = head_norm(query_pre, query_gain)
    query_rot = turn(query_scaled).astype(bf16)

    allowed = (query_seg[:, None] == key_seg[None, :]) & (key_ids[None, :] <= query_ids[:, None])
    scores = jnp.einsum("hqd,kd->hqk", query_rot, all_keys, preferred_element_type=f32) * score_scale
    scores = jnp.where(allowed[None], scores, masked_score)
    top = jnp.max(scores, axis=-1, keepdims=True)
    raised = jnp.exp(scores - top)
    total = jnp.sum(raised, axis=-1, keepdims=True)
    attended = (
        jnp.einsum("hqk,kd->hqd", raised.astype(bf16), all_values, preferred_element_type=f32)
        / total
    )
    log_total = top + jnp.log(total)
    gate_sig = jax.nn.sigmoid(gate_pre)
    gated = (attended * gate_sig).astype(bf16)

    out_rows = [out_weight] + [plane_swap(out_weight, step) for step in range(1, PLANES)]
    out_plane = jnp.zeros((PLANES * block_rows, out_weight.shape[1]), bf16)
    for step in range(PLANES):
        out_plane = lax.dynamic_update_slice_in_dim(
            out_plane, out_rows[step], (z ^ step) * block_rows, 0
        )
    out_here = jnp.concatenate([out_plane, pair_swap(out_plane, "x")], axis=0)
    out_y = pair_swap(out_here, "y")
    out_blocks = [[out_here, pair_swap(out_here, "c")], [out_y, pair_swap(out_y, "c")]]

    flip_hi, flip_lo = (z // 2) != c, (z % 2) == 1

    def to_blocks(pieces):
        tiles = pieces.reshape(2, 2, 2, chunk_rows, 2, HEAD_WIDTH)
        tiles = flip_if(flip_if(flip_if(tiles, 1, flip_hi), 2, flip_lo), 4, odd_c)
        return tiles.transpose(0, 1, 3, 2, 4, 5).reshape(2, 2, chunk_rows, 4 * HEAD_WIDTH)

    def from_blocks(blocks):
        tiles = blocks.reshape(2, 2, chunk_rows, 2, 2, HEAD_WIDTH).transpose(0, 1, 3, 2, 4, 5)
        tiles = flip_if(flip_if(flip_if(tiles, 1, flip_hi), 2, flip_lo), 4, odd_c)
        return tiles.reshape(2, PLANES, chunk_rows, 2 * HEAD_WIDTH)

    def to_owner(rows):
        tiles = rows.reshape(2, PLANES, chunk_rows, 2 * HEAD_WIDTH)
        tiles = jnp.stack(
            [tiles[:, 0]] + [plane_swap(tiles[:, step], step) for step in range(1, PLANES)], axis=1
        )
        return jnp.stack([tiles[0], pair_swap(tiles[1], "y")])

    def from_owner(tiles):
        tiles = jnp.stack([tiles[0], pair_swap(tiles[1], "y")])
        tiles = jnp.stack(
            [tiles[:, 0]] + [plane_swap(tiles[:, step], step) for step in range(1, PLANES)], axis=1
        )
        return tiles.reshape(tokens, 2 * HEAD_WIDTH)

    gated_rows = jnp.concatenate([gated[0], gated[1]], axis=1)
    gated_blocks = to_blocks(to_owner(gated_rows))
    branch = sum(
        contract_last(gated_blocks[i, j], out_blocks[i][j]) for i in range(2) for j in range(2)
    )
    middle = hidden32 + branch
    inv_two = lax.rsqrt(jnp.mean(middle * middle, axis=1, keepdims=True) + epsilon)
    normed_two_chunk = (middle * inv_two * gain_two).astype(bf16)
    normed_two = gather_chunks(normed_two_chunk)

    def by_plane(weight):
        return weight.reshape(block_rows, PLANES, weight.shape[1] // PLANES)

    ffn_gate = spread_weight(by_plane(ffn_gate_weight))
    ffn_up = spread_weight(by_plane(ffn_up_weight))
    ffn_down = spread_weight(by_plane(ffn_down_weight))
    all_cotangent = gather_chunks(cotangent)
    hidden_acts, grads_gate, grads_up = [], [], []
    for side in range(2):
        ffn_gate_pre = jnp.dot(normed_two, ffn_gate[side], preferred_element_type=f32)
        ffn_up_pre = jnp.dot(normed_two, ffn_up[side], preferred_element_type=f32)
        grad_act = jnp.dot(all_cotangent, ffn_down[side], preferred_element_type=f32)
        gate_act = jax.nn.sigmoid(ffn_gate_pre)
        silu_gate = ffn_gate_pre * gate_act
        hidden_acts.append((silu_gate * ffn_up_pre).astype(bf16))
        grads_gate.append(
            (grad_act * ffn_up_pre * gate_act * (1.0 + ffn_gate_pre * (1.0 - gate_act))).astype(bf16)
        )
        grads_up.append((grad_act * silu_gate).astype(bf16))
    grad_normed_two = sum_chunks(
        sum(
            contract_last(grads_gate[side], ffn_gate[side])
            + contract_last(grads_up[side], ffn_up[side])
            for side in range(2)
        ).astype(bf16)
    )
    ffn_out = sum_chunks(
        sum(contract_last(hidden_acts[side], ffn_down[side]) for side in range(2)).astype(bf16)
    )
    layer_chunk = (middle + ffn_out).astype(bf16)

    def whole_block(chunk):
        chunk = from_own_first(chunk, odd_x)
        by_core = jnp.stack([chunk, pair_swap(chunk, "c")])
        by_core = flip_if(by_core, 0, odd_c)
        by_y = jnp.stack([by_core, pair_swap(by_core, "y")])
        return flip_if(by_y, 0, y == 1).reshape(block_rows, width)

    layer_out = whole_block(layer_chunk)
    down_grad = collect_grad(
        *(contract_first(all_cotangent, act).astype(bf16) for act in hidden_acts)
    )
    gate_grad = collect_grad(*(contract_first(normed_two, g).astype(bf16) for g in grads_gate))
    up_grad = collect_grad(*(contract_first(normed_two, g).astype(bf16) for g in grads_up))

    grad_middle = cotangent.astype(f32) + norm_back(grad_normed_two, middle, inv_two, gain_two)
    grad_branch = grad_middle.astype(bf16)
    grad_blocks = jnp.stack(
        [
            jnp.stack(
                [
                    jnp.dot(grad_branch, out_blocks[i][j], preferred_element_type=f32).astype(bf16)
                    for j in range(2)
                ]
            )
            for i in range(2)
        ]
    )
    grad_gated_rows = from_owner(from_blocks(grad_blocks)).astype(f32)
    grad_gated = jnp.stack([grad_gated_rows[:, :low], grad_gated_rows[:, low:]])
    grad_attended = (grad_gated * gate_sig).astype(bf16)
    grad_gate_pre = (grad_gated * attended * gate_sig * (1.0 - gate_sig)).astype(bf16)
    all_grad_branch = gather_chunks(grad_branch)
    wo_gate_grad = collect_grad(
        *(
            jnp.concatenate(
                [
                    contract_first(all_grad_branch, gated[i]).astype(bf16),
                    contract_first(normed, grad_gate_pre[i]).astype(bf16),
                ],
                axis=1,
            )
            for i in range(2)
        )
    )

    delta = jnp.sum(grad_attended.astype(f32) * attended, axis=-1, keepdims=True)
    weights = jnp.exp(scores - log_total)
    grad_weights = jnp.einsum("hqd,kd->hqk", grad_attended, all_values, preferred_element_type=f32)
    grad_scores = (weights * (grad_weights - delta)).astype(bf16)
    grad_query_rot = (
        jnp.einsum("hqk,kd->hqd", grad_scores, all_keys, preferred_element_type=f32) * score_scale
    )
    grad_keys = (
        jnp.einsum("hqk,hqd->kd", grad_scores, query_rot, preferred_element_type=f32) * score_scale
    )
    grad_vals = jnp.einsum(
        "hqk,hqd->kd", weights.astype(bf16), grad_attended, preferred_element_type=f32
    )
    grad_pairs = jnp.concatenate([grad_keys, grad_vals], axis=1).astype(bf16)
    near = grad_pairs[: 2 * tokens].astype(f32) + pair_swap(grad_pairs[2 * tokens :], "c").astype(
        f32
    )
    near = near.astype(bf16)
    own_pair = near[:tokens].astype(f32) + pair_swap(near[tokens:], "x").astype(f32)
    grad_key_unit = turn_back(own_pair[:, :low].astype(bf16).astype(f32))
    grad_values = own_pair[:, low:].astype(bf16)
    grad_query_unit = turn_back(grad_query_rot.astype(bf16).astype(f32))
    query_gain_part = jnp.sum(grad_query_unit * query_unit, axis=(0, 1))
    key_gain_part = jnp.sum(grad_key_unit * key_unit, axis=0)
    grad_query_pre = norm_back(grad_query_unit, query_pre, inv_query, query_gain).astype(bf16)
    grad_key_pre = norm_back(grad_key_unit, key_pre, inv_key, key_gain).astype(bf16)
    key_or_value = [
        jnp.where(odd_c, grad_values, grad_key_pre),
        jnp.where(odd_c, grad_key_pre, grad_values),
    ]
    attn_sides = (attn_mine, attn_other)
    grad_pre = [
        jnp.concatenate([grad_query_pre[i], grad_gate_pre[i], key_or_value[i]], axis=1)
        for i in range(2)
    ]
    grad_normed = sum_chunks(
        sum(contract_last(grad_pre[i], attn_sides[i]) for i in range(2)).astype(bf16)
    )
    qk_grad = collect_grad(
        *(
            contract_first(
                normed, jnp.concatenate([grad_query_pre[i], key_or_value[i]], axis=1)
            ).astype(bf16)
            for i in range(2)
        )
    )
    input_chunk = (grad_middle + norm_back(grad_normed, hidden32, inv_one, gain_one)).astype(bf16)
    input_grad = whole_block(input_chunk)

    by_z = jnp.concatenate([wo_gate_grad, qk_grad], axis=-1)
    kept = jnp.where(odd_c, by_z[:, 2:], by_z[:, :2])
    taken = pair_swap(jnp.where(odd_c, by_z[:, :2], by_z[:, 2:]), "c")
    heads = jnp.stack([jnp.where(odd_c, taken, kept), jnp.where(odd_c, kept, taken)], axis=2)
    heads = heads.reshape(block_rows, 2, 2, 4, HEAD_WIDTH).astype(f32)

    def head_columns(which):
        return heads[:, :, :, which].reshape(block_rows, 4 * HEAD_WIDTH)

    out_weight_grad, gate_weight_grad, query_weight_grad = (head_columns(i) for i in range(3))
    key_weight_grad = heads[:, :, 0, 3].reshape(block_rows, 2 * HEAD_WIDTH)
    value_weight_grad = heads[:, :, 1, 3].reshape(block_rows, 2 * HEAD_WIDTH)

    gains = jnp.concatenate(
        [
            from_own_first(jnp.sum(grad_normed * hidden32 * inv_one, axis=0), odd_x),
            from_own_first(jnp.sum(grad_normed_two * middle * inv_two, axis=0), odd_x),
            query_gain_part,
            key_gain_part,
        ]
    )
    gains = (gains + plane_swap(gains, 1)) + (plane_swap(gains, 2) + plane_swap(gains, 3))
    for axis in ("x", "y", "c"):
        gains = gains + pair_swap(gains, axis)

    def flat(grad):
        return grad.reshape(block_rows, -1).astype(f32)

    return (
        layer_out,
        input_grad,
        query_weight_grad,
        key_weight_grad,
        value_weight_grad,
        gate_weight_grad,
        out_weight_grad,
        flat(gate_grad),
        flat(up_grad),
        flat(down_grad),
        gains[:width],
        gains[width : 2 * width],
        gains[2 * width : 2 * width + HEAD_WIDTH],
        gains[2 * width + HEAD_WIDTH :],
    )


def solution(mesh):
    wide, head = mesh.shape["wide"], mesh.shape["head"]
    if wide == 2 * PLANES and head == 4:
        devices = mesh.devices.reshape(PLANES, 2, 2, 2)
        mesh = Mesh(devices, ("z", "x", "y", "c"))
        program, rows, columns = on_slice_device, ("z", "x"), ("y", "c")
    else:
        program, rows, columns = on_device, "wide", "head"
    tokens, weight = P(rows, None), P(rows, columns)
    return jax.shard_map(
        program,
        mesh=mesh,
        in_specs=(tokens, tokens, P()) + (weight,) * 8 + (P(),) * 4,
        out_specs=(tokens, tokens) + (weight,) * 8 + (P(),) * 4,
        check_vma=False,
    )
```

```python
import jax
import jax.numpy as jnp
from jax import lax
from jax.sharding import Mesh
from jax.sharding import PartitionSpec as P

HEAD_WIDTH = 128


epsilon = 1e-06
rope_base = 1000000.0
masked_score = -1e30


def segment_of(lengths, token_ids):
    doc_ends = jnp.cumsum(lengths)
    return jnp.sum((token_ids[:, None] >= doc_ends[None, :]).astype(jnp.int32), axis=1)


def doc_tables(lengths, token_ids):
    doc_ends = jnp.cumsum(lengths)
    starts = doc_ends - lengths
    segment = segment_of(lengths, token_ids)
    labels = jnp.arange(lengths.shape[0], dtype=jnp.int32)
    doc_begin = jnp.sum(jnp.where(segment[:, None] == labels[None, :], starts[None, :], 0), axis=1)
    return (segment, token_ids - doc_begin)


def rope_tables(positions, head_size):
    half_size = head_size // 2
    frequency = rope_base ** (-2.0 * jnp.arange(half_size, dtype=jnp.float32) / head_size)
    angles = positions.astype(jnp.float32)[:, None] * frequency[None, :]
    cosine = jnp.cos(angles)
    sine_table = jnp.sin(angles)
    return (
        jnp.concatenate([cosine, cosine], axis=1),
        jnp.concatenate([sine_table, sine_table], axis=1),
    )


def rotate_half(values):
    half_size = values.shape[-1] // 2
    return jnp.concatenate([-values[..., half_size:], values[..., :half_size]], axis=-1)


def rotate_back(values):
    half_size = values.shape[-1] // 2
    return jnp.concatenate([values[..., half_size:], -values[..., :half_size]], axis=-1)


def apply_rope(values, cos_table, sin_table):
    return values * cos_table[:, None, :] + rotate_half(values) * sin_table[:, None, :]


def rope_back(grads, cos_table, sin_table):
    return grads * cos_table[:, None, :] + rotate_back(grads * sin_table[:, None, :])


def contract_last(left, right):
    return lax.dot_general(
        left, right, (((1,), (1,)), ((), ())), preferred_element_type=jnp.float32
    )


def contract_first(left, right):
    return lax.dot_general(
        left, right, (((0,), (0,)), ((), ())), preferred_element_type=jnp.float32
    )


def norm_back(grad_out, inputs, inv_root, gain):
    scaled = grad_out * gain
    return inv_root * scaled - inputs * inv_root**3 * jnp.mean(
        scaled * inputs, axis=-1, keepdims=True
    )


def on_device(
    hidden_in,
    out_cotangent,
    doc_lengths,
    query_weight,
    key_matrix,
    value_matrix,
    gate_weight,
    out_weight,
    ffn_gate_weight,
    ffn_up_weight,
    ffn_down_weight,
    attn_gain,
    ffn_gain,
    query_gain,
    key_gain,
):
    tok_rows = hidden_in.shape[0]
    row_length = tok_rows * lax.axis_size("wide")
    first_row = lax.axis_index("wide") * tok_rows
    token_ids = first_row + jnp.arange(tok_rows, dtype=jnp.int32)
    segment, positions = doc_tables(doc_lengths, token_ids)
    shard_begin = first_row - positions[0]
    shard_last = first_row + tok_rows - 1
    cos_table, sin_table = rope_tables(positions, HEAD_WIDTH)
    local_heads = query_weight.shape[1] // HEAD_WIDTH
    kv_heads = key_matrix.shape[1] // HEAD_WIDTH
    group_width = local_heads // kv_heads
    query_rows = group_width * tok_rows
    score_scale = HEAD_WIDTH ** (-0.5)
    (
        full_query,
        full_key,
        full_value,
        full_gate,
        full_out,
        full_ffn_gate,
        full_ffn_up,
        full_ffn_down,
    ) = (
        lax.all_gather(query_weight, "wide", axis=0, tiled=True),
        lax.all_gather(key_matrix, "wide", axis=0, tiled=True),
        lax.all_gather(value_matrix, "wide", axis=0, tiled=True),
        lax.all_gather(gate_weight, "wide", axis=0, tiled=True),
        lax.all_gather(out_weight, "wide", axis=0, tiled=True),
        lax.all_gather(ffn_gate_weight, "wide", axis=0, tiled=True),
        lax.all_gather(ffn_up_weight, "wide", axis=0, tiled=True),
        lax.all_gather(ffn_down_weight, "wide", axis=0, tiled=True),
    )
    hidden32 = hidden_in.astype(jnp.float32)
    inv_one = lax.rsqrt(jnp.mean(hidden32 * hidden32, axis=1, keepdims=True) + epsilon)
    normed_input = (hidden32 * inv_one * attn_gain).astype(jnp.bfloat16)
    query_pre = jnp.dot(normed_input, full_query, preferred_element_type=jnp.float32).reshape(
        tok_rows, local_heads, HEAD_WIDTH
    )
    key_before_norm = jnp.dot(normed_input, full_key, preferred_element_type=jnp.float32).reshape(
        tok_rows, kv_heads, HEAD_WIDTH
    )
    value_rows = jnp.dot(normed_input, full_value, preferred_element_type=jnp.float32).astype(
        jnp.bfloat16
    )
    gate_pre = jnp.dot(normed_input, full_gate, preferred_element_type=jnp.float32)
    inv_query = lax.rsqrt(jnp.mean(query_pre * query_pre, axis=-1, keepdims=True) + epsilon)
    inv_key = lax.rsqrt(
        jnp.mean(key_before_norm * key_before_norm, axis=-1, keepdims=True) + epsilon
    )
    query_unit = query_pre * inv_query
    key_unit = key_before_norm * inv_key
    query_rot = apply_rope(query_unit * query_gain, cos_table, sin_table).astype(jnp.bfloat16)
    key_rows = (
        apply_rope(key_unit * key_gain, cos_table, sin_table)
        .astype(jnp.bfloat16)
        .reshape(tok_rows, kv_heads * HEAD_WIDTH)
    )
    query_heads = (
        query_rot.reshape(tok_rows, kv_heads, group_width, HEAD_WIDTH)
        .transpose(1, 2, 0, 3)
        .reshape(kv_heads, query_rows, HEAD_WIDTH)
    )
    query_seg = jnp.tile(segment, group_width)
    query_ids = jnp.tile(token_ids, group_width)
    start_state = (
        jnp.full((kv_heads, query_rows), masked_score, jnp.float32),
        jnp.zeros((kv_heads, query_rows), jnp.float32),
        jnp.zeros((kv_heads, query_rows, HEAD_WIDTH), jnp.float32),
    )
    key_piece = lax.all_gather(key_rows, "wide", axis=0, tiled=True)
    value_piece = lax.all_gather(value_rows, "wide", axis=0, tiled=True)
    count = key_piece.shape[0]
    step_rows = 512
    steps_count = count // step_rows
    key_ids = jnp.arange(count, dtype=jnp.int32)
    key_seg = segment_of(doc_lengths, key_ids)
    key_blocks = key_piece.reshape(steps_count, step_rows, kv_heads, HEAD_WIDTH).transpose(
        0, 2, 1, 3
    )
    value_blocks = value_piece.reshape(steps_count, step_rows, kv_heads, HEAD_WIDTH).transpose(
        0, 2, 1, 3
    )

    def inner(state, block):
        key_block, value_block, block_seg, block_ids = block

        def inner_work(state_in):
            scores = (
                jnp.einsum(
                    "hqd,hkd->hqk", query_heads, key_block, preferred_element_type=jnp.float32
                )
                * score_scale
            )
            allowed = (
                (query_seg[:, None] == block_seg[None, :])
                & (block_ids[None, :] <= query_ids[:, None])
            )[None]
            scores = jnp.where(allowed, scores, masked_score)
            running, total, accum = state_in
            newest = jnp.maximum(running, jnp.max(scores, axis=-1))
            factor = jnp.exp(running - newest)
            weights = jnp.where(allowed, jnp.exp(scores - newest[..., None]), 0.0)
            total = total * factor + jnp.sum(weights, axis=-1)
            accum = accum * factor[..., None] + jnp.einsum(
                "hqk,hkd->hqd",
                weights.astype(jnp.bfloat16),
                value_block,
                preferred_element_type=jnp.float32,
            )
            return (newest, total, accum)

        useful = (block_ids[0] <= shard_last) & (block_ids[step_rows - 1] >= shard_begin)
        return (lax.cond(useful, inner_work, lambda state_in: state_in, state), None)

    state, unused = lax.scan(
        inner,
        start_state,
        (
            key_blocks,
            value_blocks,
            key_seg.reshape(steps_count, step_rows),
            key_ids.reshape(steps_count, step_rows),
        ),
    )
    running, total, accum = state
    attended_heads = accum / total[..., None]
    log_total = running + jnp.log(total)
    attended = (
        attended_heads.reshape(kv_heads, group_width, tok_rows, HEAD_WIDTH)
        .transpose(2, 0, 1, 3)
        .reshape(tok_rows, local_heads * HEAD_WIDTH)
    )
    gate_sig = jax.nn.sigmoid(gate_pre)
    gated = (attended * gate_sig).astype(jnp.bfloat16)
    branch = lax.psum(contract_last(gated, full_out).astype(jnp.bfloat16), "head").astype(
        jnp.float32
    )
    middle = hidden32 + branch
    inv_two = lax.rsqrt(jnp.mean(middle * middle, axis=1, keepdims=True) + epsilon)
    normed_two = (middle * inv_two * ffn_gain).astype(jnp.bfloat16)
    ffn_gate_pre = jnp.dot(normed_two, full_ffn_gate, preferred_element_type=jnp.float32)
    ffn_up_pre = jnp.dot(normed_two, full_ffn_up, preferred_element_type=jnp.float32)
    gate_act = jax.nn.sigmoid(ffn_gate_pre)
    silu_gate = ffn_gate_pre * gate_act
    hidden_act = (silu_gate * ffn_up_pre).astype(jnp.bfloat16)
    ffn_out = lax.psum(
        contract_last(hidden_act, full_ffn_down).astype(jnp.bfloat16), "head"
    ).astype(jnp.float32)
    layer_out = (middle + ffn_out).astype(jnp.bfloat16)
    grad32 = out_cotangent.astype(jnp.float32)
    grad_hidden = jnp.dot(out_cotangent, full_ffn_down, preferred_element_type=jnp.float32)
    grad_ffn_gate = (
        grad_hidden * ffn_up_pre * gate_act * (1.0 + ffn_gate_pre * (1.0 - gate_act))
    ).astype(jnp.bfloat16)
    grad_ffn_up = (grad_hidden * silu_gate).astype(jnp.bfloat16)
    grad_normed_two = lax.psum(
        (
            contract_last(grad_ffn_gate, full_ffn_gate) + contract_last(grad_ffn_up, full_ffn_up)
        ).astype(jnp.bfloat16),
        "head",
    ).astype(jnp.float32)
    grad_middle = grad32 + norm_back(grad_normed_two, middle, inv_two, ffn_gain)
    grad_branch = grad_middle.astype(jnp.bfloat16)
    grad_gated = jnp.dot(grad_branch, full_out, preferred_element_type=jnp.float32)
    grad_attended = (grad_gated * gate_sig).astype(jnp.bfloat16)
    grad_gate_pre = (grad_gated * attended * gate_sig * (1.0 - gate_sig)).astype(jnp.bfloat16)
    grad_heads = (
        grad_attended.reshape(tok_rows, kv_heads, group_width, HEAD_WIDTH)
        .transpose(1, 2, 0, 3)
        .reshape(kv_heads, query_rows, HEAD_WIDTH)
    )
    delta = jnp.sum(grad_heads.astype(jnp.float32) * attended_heads, axis=-1)
    all_keys, all_values = key_piece, value_piece
    key_step = 512
    key_count = row_length // key_step
    all_ids = jnp.arange(row_length, dtype=jnp.int32)
    all_seg = segment_of(doc_lengths, all_ids)
    key_blocks = all_keys.reshape(key_count, key_step, kv_heads, HEAD_WIDTH).transpose(0, 2, 1, 3)
    value_blocks = all_values.reshape(key_count, key_step, kv_heads, HEAD_WIDTH).transpose(
        0, 2, 1, 3
    )
    key_scan_items = (
        key_blocks,
        value_blocks,
        all_seg.reshape(key_count, key_step),
        all_ids.reshape(key_count, key_step),
    )
    zero_query = jnp.zeros((kv_heads, query_rows, HEAD_WIDTH), jnp.float32)

    def block_terms(key_block, value_block, block_seg, block_ids):
        scores = (
            jnp.einsum("hqd,hkd->hqk", query_heads, key_block, preferred_element_type=jnp.float32)
            * score_scale
        )
        allowed = (
            (query_seg[:, None] == block_seg[None, :]) & (block_ids[None, :] <= query_ids[:, None])
        )[None]
        weights = jnp.where(
            allowed, jnp.exp(jnp.where(allowed, scores, masked_score) - log_total[..., None]), 0.0
        )
        grad_weights = jnp.einsum(
            "hqd,hkd->hqk", grad_heads, value_block, preferred_element_type=jnp.float32
        )
        grad_scores = (weights * (grad_weights - delta[..., None])).astype(jnp.bfloat16)
        return (weights, grad_scores)

    def block_useful(block_ids):
        return (block_ids[0] <= shard_last) & (block_ids[key_step - 1] >= shard_begin)

    def back_block(grad_query, block):
        key_block, value_block, block_seg, block_ids = block

        def back_work(grad_in):
            weights, grad_scores = block_terms(key_block, value_block, block_seg, block_ids)
            grad_out = (
                grad_in
                + jnp.einsum(
                    "hqk,hkd->hqd", grad_scores, key_block, preferred_element_type=jnp.float32
                )
                * score_scale
            )
            grad_key = (
                jnp.einsum(
                    "hqk,hqd->hkd", grad_scores, query_heads, preferred_element_type=jnp.float32
                )
                * score_scale
            )
            grad_value = jnp.einsum(
                "hqk,hqd->hkd",
                weights.astype(jnp.bfloat16),
                grad_heads,
                preferred_element_type=jnp.float32,
            )
            return (grad_out, (grad_key, grad_value))

        def skip(grad_in):
            nothing = jnp.zeros((kv_heads, key_step, HEAD_WIDTH), jnp.float32)
            return (grad_in, (nothing, nothing))

        return lax.cond(block_useful(block_ids), back_work, skip, grad_query)

    grad_query, (key_parts, value_parts) = lax.scan(back_block, zero_query, key_scan_items)
    key_grad_rows = key_parts.transpose(0, 2, 1, 3).reshape(row_length, kv_heads * HEAD_WIDTH)
    value_grad_rows = value_parts.transpose(0, 2, 1, 3).reshape(row_length, kv_heads * HEAD_WIDTH)
    key_total, value_total = (
        lax.psum_scatter(
            key_grad_rows.astype(jnp.bfloat16), "wide", scatter_dimension=0, tiled=True
        ).astype(jnp.float32),
        lax.psum_scatter(
            value_grad_rows.astype(jnp.bfloat16), "wide", scatter_dimension=0, tiled=True
        ).astype(jnp.float32),
    )
    grad_values = value_total.astype(jnp.bfloat16)
    grad_key_rot = (
        key_total.astype(jnp.bfloat16).astype(jnp.float32).reshape(tok_rows, kv_heads, HEAD_WIDTH)
    )
    grad_query_rot = (
        grad_query.astype(jnp.bfloat16)
        .astype(jnp.float32)
        .reshape(kv_heads, group_width, tok_rows, HEAD_WIDTH)
        .transpose(2, 0, 1, 3)
        .reshape(tok_rows, local_heads, HEAD_WIDTH)
    )
    grad_query_unit = rope_back(grad_query_rot, cos_table, sin_table)
    grad_key_unit = rope_back(grad_key_rot, cos_table, sin_table)
    query_gain_part = jnp.sum(grad_query_unit * query_unit, axis=(0, 1))
    key_gain_part = jnp.sum(grad_key_unit * key_unit, axis=(0, 1))
    grad_query_pre = (
        norm_back(grad_query_unit, query_pre, inv_query, query_gain)
        .reshape(tok_rows, local_heads * HEAD_WIDTH)
        .astype(jnp.bfloat16)
    )
    grad_key_pre = (
        norm_back(grad_key_unit, key_before_norm, inv_key, key_gain)
        .reshape(tok_rows, kv_heads * HEAD_WIDTH)
        .astype(jnp.bfloat16)
    )
    grad_normed_part = (
        contract_last(grad_query_pre, full_query)
        + contract_last(grad_key_pre, full_key)
        + contract_last(grad_values, full_value)
        + contract_last(grad_gate_pre, full_gate)
    )
    grad_normed = lax.psum(grad_normed_part.astype(jnp.bfloat16), "head").astype(jnp.float32)
    input_grad = (grad_middle + norm_back(grad_normed, hidden32, inv_one, attn_gain)).astype(
        jnp.bfloat16
    )
    attn_gain_part = jnp.sum(grad_normed * hidden32 * inv_one, axis=0)
    ffn_gain_part = jnp.sum(grad_normed_two * middle * inv_two, axis=0)
    weight_grads = lax.psum_scatter(
        jnp.concatenate(
            [
                contract_first(normed_input, grad_query_pre),
                contract_first(normed_input, grad_key_pre),
                contract_first(normed_input, grad_values),
                contract_first(normed_input, grad_gate_pre),
                contract_first(grad_branch, gated),
                contract_first(normed_two, grad_ffn_gate),
                contract_first(normed_two, grad_ffn_up),
                contract_first(out_cotangent, hidden_act),
            ],
            axis=1,
        ).astype(jnp.bfloat16),
        "wide",
        scatter_dimension=0,
        tiled=True,
    ).astype(jnp.float32)
    col_widths = [
        query_weight.shape[1],
        key_matrix.shape[1],
        value_matrix.shape[1],
        gate_weight.shape[1],
        out_weight.shape[1],
        ffn_gate_weight.shape[1],
        ffn_up_weight.shape[1],
        ffn_down_weight.shape[1],
    ]
    pieces = []
    offset = 0
    for width in col_widths:
        pieces.append(weight_grads[:, offset : offset + width])
        offset = offset + width
    head_first = (lax.axis_index("head") == 0).astype(jnp.float32)
    attn_gain_grad, ffn_gain_grad, query_gain_grad, key_gain_grad = lax.psum(
        (attn_gain_part * head_first, ffn_gain_part * head_first, query_gain_part, key_gain_part),
        ("wide", "head"),
    )
    return (
        layer_out,
        input_grad,
        pieces[0],
        pieces[1],
        pieces[2],
        pieces[3],
        pieces[4],
        pieces[5],
        pieces[6],
        pieces[7],
        attn_gain_grad,
        ffn_gain_grad,
        query_gain_grad,
        key_gain_grad,
    )


PLANES = 4
PLANE = ("far", "x")


def pair_swap(values, axis):
    return lax.ppermute(values, axis, [(0, 1), (1, 0)])


def plane_swap(values, step):
    return lax.ppermute(values, PLANE, [(i, i ^ step) for i in range(PLANES)])


def side_swap(values, step):
    return lax.ppermute(values, ("x", "y"), [(i, i ^ step) for i in range(4)])


def after(values, *done):
    return lax.optimization_barrier((values, done))[0]


def gather_chunks(chunk):
    far = pair_swap(chunk, "far")
    near = [side_swap(chunk, step) for step in range(1, 4)]
    away = [side_swap(far, step) for step in range(1, 4)]
    pieces = [chunk, far]
    for pair in zip(near, away):
        pieces.extend(pair)
    return jnp.concatenate(pieces, axis=0)


def sum_sends(parts):
    rows = parts.shape[0] // 8

    def part(step, far):
        return parts[(2 * step + far) * rows : (2 * step + far + 1) * rows]

    return [
        [part(0, far)] + [side_swap(part(step, far), step) for step in range(1, 4)]
        for far in (1, 0)
    ]


def sum_pieces(pieces):
    total = pieces[0].astype(jnp.float32)
    for piece in pieces[1:]:
        total = total + piece.astype(jnp.float32)
    return total


def sum_sends_paired(parts):
    rows = parts.shape[0] // 4
    return [parts[:rows]] + [
        side_swap(parts[step * rows : (step + 1) * rows], step) for step in range(1, 4)
    ]


def sum_chunks(parts, *due):
    away, own = sum_sends(parts)
    away = sum_pieces(away).astype(jnp.bfloat16)
    if due:
        away = after(away, *due)
    return sum_pieces(own + [pair_swap(away, "far")])


def flip_if(values, axis, flag):
    return jnp.where(flag, jnp.flip(values, axis), values)


def to_own_first(values, flag):
    lead = values.shape[:-1]
    width = values.shape[-1]
    split = values.reshape(lead + (2, 2, width // 4))
    zero = split[..., 0, :].reshape(lead + (width // 2,))
    one = split[..., 1, :].reshape(lead + (width // 2,))
    return jnp.concatenate([jnp.where(flag, one, zero), jnp.where(flag, zero, one)], axis=-1)


def from_own_first(values, flag):
    lead = values.shape[:-1]
    width = values.shape[-1]
    own = values[..., : width // 2].reshape(lead + (2, width // 4))
    other = values[..., width // 2 :].reshape(lead + (2, width // 4))
    pair = jnp.stack([jnp.where(flag, other, own), jnp.where(flag, own, other)], axis=-2)
    return pair.reshape(lead + (width,))


def to_plane_owners(local):
    planes, rows, width = local.shape
    return lax.all_to_all(
        local.reshape(planes * rows, width), PLANE, split_axis=0, concat_axis=0, tiled=True
    )


def with_near_and_core(mine, other):
    mine = jnp.concatenate([mine, other], axis=0)
    return mine, pair_swap(mine, "c")


def core_sum(mine, other):
    both = mine.astype(jnp.float32) + pair_swap(other, "c").astype(jnp.float32)
    return both.astype(jnp.bfloat16)


def near_add(both, got):
    half = both.shape[0] // 2
    return (both[:half].astype(jnp.float32) + got.astype(jnp.float32)).astype(jnp.bfloat16)


def to_row_owners(rows):
    back = lax.all_to_all(rows, PLANE, split_axis=0, concat_axis=0, tiled=True)
    return back.reshape(PLANES, rows.shape[0] // PLANES, rows.shape[1])


def head_norm(pre, gain):
    inverse = lax.rsqrt(jnp.mean(pre * pre, axis=-1, keepdims=True) + epsilon)
    unit = pre * inverse
    return inverse, unit, unit * gain


def on_slice_device(
    hidden_in,
    out_cotangent,
    doc_lengths,
    query_weight,
    key_matrix,
    value_matrix,
    gate_weight,
    out_weight,
    ffn_gate_weight,
    ffn_up_weight,
    ffn_down_weight,
    attn_gain,
    ffn_gain,
    query_gain,
    key_gain,
):
    bf16, f32 = jnp.bfloat16, jnp.float32
    block_rows, width = hidden_in.shape
    chunk_rows = block_rows // 4
    far, near, x, y, c = (lax.axis_index(name) for name in ("far", "near", "x", "y", "c"))
    odd_near, odd_c = near == 1, c == 1
    score_scale = HEAD_WIDTH ** (-0.5)

    def heads_of(weight, which, group):
        width = weight.shape[1] // 2
        start = which * HEAD_WIDTH if group == 2 else 0
        return [weight[:, i * width + start : i * width + start + HEAD_WIDTH] for i in range(2)]

    def halves(which):
        third = key_matrix if which == 0 else value_matrix
        columns = [
            heads_of(query_weight, which, 2),
            heads_of(third, which, 1),
            heads_of(gate_weight, which, 2),
            heads_of(out_weight, which, 2),
        ]
        return jnp.stack([jnp.concatenate([col[i] for col in columns], axis=1) for i in range(2)])

    half_zero, half_one = halves(0), halves(1)
    kept = jnp.where(odd_c, half_one, half_zero)
    taken = pair_swap(jnp.where(odd_c, half_zero, half_one), "c")
    attn_local = jnp.concatenate(
        [jnp.where(odd_c, taken, kept), jnp.where(odd_c, kept, taken)], axis=0
    )
    low, high = HEAD_WIDTH, 2 * HEAD_WIDTH
    qk_half = to_plane_owners(attn_local[:, :, :high])
    qk_mine, qk_other = with_near_and_core(qk_half, pair_swap(qk_half, "near"))

    chunk_start = (y * 2 + c) * chunk_rows
    own_hidden = lax.dynamic_slice_in_dim(hidden_in, chunk_start, chunk_rows, 0)
    hidden32 = to_own_first(own_hidden, odd_near).astype(f32)
    gain_one = to_own_first(attn_gain, odd_near)
    inv_one = lax.rsqrt(jnp.mean(hidden32 * hidden32, axis=1, keepdims=True) + epsilon)
    normed_chunk = (hidden32 * inv_one * gain_one).astype(bf16)
    normed = gather_chunks(normed_chunk)

    (
        (out_cotangent, ffn_gain, doc_lengths, ffn_gate_weight, ffn_up_weight, ffn_down_weight),
        (far, near, x, y, c),
    ) = after(
        (
            (out_cotangent, ffn_gain, doc_lengths, ffn_gate_weight, ffn_up_weight, ffn_down_weight),
            (far, near, x, y, c),
        ),
        attn_local,
        normed_chunk,
    )
    odd_near, odd_c = near == 1, c == 1
    own_cotangent = lax.dynamic_slice_in_dim(
        out_cotangent, (y * 2 + c) * chunk_rows, chunk_rows, 0
    )
    cotangent = to_own_first(own_cotangent, odd_near)
    gain_two = to_own_first(ffn_gain, odd_near)
    tokens = normed.shape[0]

    def ids_of(near_at, c_at):
        step = jnp.arange(8, dtype=jnp.int32)
        x_at, y_at, far_at = x ^ (step // 4), y ^ (step // 2 % 2), far ^ (step % 2)
        start = ((far_at * 2 + near_at) * 2 + x_at) * block_rows + (y_at * 2 + c_at) * chunk_rows
        return (start[:, None] + jnp.arange(chunk_rows, dtype=jnp.int32)[None, :]).reshape(-1)

    query_ids = ids_of(near, c)
    key_ids = jnp.concatenate([query_ids, ids_of(near ^ 1, c), ids_of(near, c ^ 1), ids_of(near ^ 1, c ^ 1)])
    query_seg, positions = doc_tables(doc_lengths, query_ids)
    key_seg = segment_of(doc_lengths, key_ids)
    cos_table, sin_table = rope_tables(positions, HEAD_WIDTH)
    cos_rows, sin_rows = cos_table, sin_table

    def turn(values):
        return values * cos_rows + rotate_half(values) * sin_rows

    def turn_back(grads):
        return grads * cos_rows + rotate_back(grads * sin_rows)

    mine = jnp.dot(normed, qk_mine, preferred_element_type=f32)
    other = jnp.dot(normed, qk_other, preferred_element_type=f32)
    key_pre = jnp.where(odd_c, other[:, low:], mine[:, low:])
    value_rows = jnp.where(odd_c, mine[:, low:], other[:, low:]).astype(bf16)
    inv_key, key_unit, key_scaled = head_norm(key_pre, key_gain)
    key_rows = turn(key_scaled).astype(bf16)
    pair = jnp.concatenate([key_rows, value_rows], axis=1)
    pair_near = pair_swap(pair, "near")
    both_near = jnp.concatenate([pair, pair_near], axis=0)
    all_pairs = jnp.concatenate([both_near, pair_swap(both_near, "c")], axis=0)
    all_keys, all_values = all_pairs[:, :low], all_pairs[:, low:]

    def by_plane(*weights):
        step = weights[0].shape[1] // PLANES
        return jnp.stack(
            [
                jnp.concatenate([w[:, p * step : (p + 1) * step] for w in weights], axis=1)
                for p in range(PLANES)
            ]
        )

    units = ffn_gate_weight.shape[1] // PLANES
    og_half = to_plane_owners(after(attn_local[:, :, high:], qk_half))
    og_near = pair_swap(after(og_half, pair_near), "near")
    og_mine, og_other = with_near_and_core(og_half, og_near)
    gate_up_half = to_plane_owners(after(by_plane(ffn_gate_weight, ffn_up_weight), og_half, pair))
    cotangent_far = pair_swap(after(cotangent, qk_half), "far")
    cotangent_pair = after(jnp.concatenate([cotangent, cotangent_far], axis=0), pair_near)
    cotangent_pieces = [cotangent_pair] + [side_swap(cotangent_pair, i) for i in range(1, 4)]

    query_pre = jnp.stack([mine[:, :low], other[:, :low]])
    gate_pre = jnp.stack(
        [
            jnp.dot(normed, side[:, :low], preferred_element_type=f32)
            for side in (og_mine, og_other)
        ]
    )
    out_sides = (og_mine[:, low:], og_other[:, low:])
    inv_query, query_unit, query_scaled = head_norm(query_pre, query_gain)
    query_rot = turn(query_scaled).astype(bf16)

    allowed = (query_seg[:, None] == key_seg[None, :]) & (key_ids[None, :] <= query_ids[:, None])
    scores = jnp.einsum("hqd,kd->hqk", query_rot, all_keys, preferred_element_type=f32) * score_scale
    scores = jnp.where(allowed[None], scores, masked_score)
    top = jnp.max(scores, axis=-1, keepdims=True)
    raised = jnp.exp(scores - top)
    total = jnp.sum(raised, axis=-1, keepdims=True)
    attended = (
        jnp.einsum("hqk,kd->hqd", raised.astype(bf16), all_values, preferred_element_type=f32)
        / total
    )
    log_total = top + jnp.log(total)
    gate_sig = jax.nn.sigmoid(gate_pre)
    gated = (attended * gate_sig).astype(bf16)

    branch_parts = sum(contract_last(gated[i], out_sides[i]) for i in range(2)).astype(bf16)
    gate_up_near = pair_swap(after(gate_up_half, og_near, branch_parts), "near")
    down_half = to_plane_owners(after(by_plane(ffn_down_weight), gate_up_half))
    branch = sum_chunks(branch_parts, gate_up_half)
    middle = hidden32 + branch
    inv_two = lax.rsqrt(jnp.mean(middle * middle, axis=1, keepdims=True) + epsilon)
    normed_two_chunk = (middle * inv_two * gain_two).astype(bf16)
    normed_two_chunk, gate_up_near, down_half = after((normed_two_chunk, gate_up_near, down_half))
    normed_two = gather_chunks(normed_two_chunk)
    gate_up = with_near_and_core(gate_up_half, gate_up_near)
    ffn_down = with_near_and_core(down_half, pair_swap(down_half, "near"))
    ffn_gate = [part[:, :units] for part in gate_up]
    ffn_up = [part[:, units:] for part in gate_up]
    all_cotangent = jnp.concatenate(after(cotangent_pieces, normed_two_chunk), axis=0)

    hidden_acts, grads_gate, grads_up = [], [], []
    for side in range(2):
        ffn_gate_pre = jnp.dot(normed_two, ffn_gate[side], preferred_element_type=f32)
        ffn_up_pre = jnp.dot(normed_two, ffn_up[side], preferred_element_type=f32)
        grad_act = jnp.dot(all_cotangent, ffn_down[side], preferred_element_type=f32)
        gate_act = jax.nn.sigmoid(ffn_gate_pre)
        silu_gate = ffn_gate_pre * gate_act
        hidden_acts.append((silu_gate * ffn_up_pre).astype(bf16))
        grads_gate.append(
            (grad_act * ffn_up_pre * gate_act * (1.0 + ffn_gate_pre * (1.0 - gate_act))).astype(bf16)
        )
        grads_up.append((grad_act * silu_gate).astype(bf16))
    grad_ffn = [jnp.concatenate([grads_gate[i], grads_up[i]], axis=1) for i in range(2)]
    grad_two_parts = sum(contract_last(grad_ffn[i], gate_up[i]) for i in range(2)).astype(bf16)
    grad_normed_two = sum_chunks(grad_two_parts)
    hidden_acts, all_cotangent, grad_ffn = after(
        (hidden_acts, all_cotangent, grad_ffn), grad_two_parts
    )
    down_parts = sum(contract_last(hidden_acts[i], ffn_down[i]) for i in range(2)).astype(bf16)
    down_both = core_sum(*(contract_first(all_cotangent, act).astype(bf16) for act in hidden_acts))
    gate_up_both = core_sum(*(contract_first(normed_two, g).astype(bf16) for g in grad_ffn))

    def whole_block(chunk):
        chunk = from_own_first(chunk, odd_near)
        by_y = jnp.stack([chunk, pair_swap(chunk, "y")])
        by_core = jnp.stack([by_y, pair_swap(by_y, "c")], axis=1)
        return flip_if(flip_if(by_core, 1, odd_c), 0, y == 1).reshape(block_rows, width)

    grad_middle = cotangent.astype(f32) + norm_back(grad_normed_two, middle, inv_two, gain_two)
    grad_branch = grad_middle.astype(bf16)
    grad_branch, down_both, gate_up_both, down_parts = lax.optimization_barrier(
        (grad_branch, down_both, gate_up_both, down_parts)
    )
    all_grad_branch = gather_chunks(grad_branch)
    grad_gated = jnp.stack(
        [jnp.dot(all_grad_branch, side, preferred_element_type=f32) for side in out_sides]
    )
    down_pieces = sum_sends_paired(after(down_parts, all_grad_branch))
    gate_up_got = pair_swap(gate_up_both[gate_up_both.shape[0] // 2 :], "near")
    down_got = pair_swap(down_both[down_both.shape[0] // 2 :], "near")
    grad_attended = (grad_gated * gate_sig).astype(bf16)
    grad_gate_pre = (grad_gated * attended * gate_sig * (1.0 - gate_sig)).astype(bf16)

    delta = jnp.sum(grad_attended.astype(f32) * attended, axis=-1, keepdims=True)
    weights = jnp.exp(scores - log_total)
    grad_weights = jnp.einsum("hqd,kd->hqk", grad_attended, all_values, preferred_element_type=f32)
    grad_scores = (weights * (grad_weights - delta)).astype(bf16)
    grad_query_rot = (
        jnp.einsum("hqk,kd->hqd", grad_scores, all_keys, preferred_element_type=f32) * score_scale
    )
    grad_keys = (
        jnp.einsum("hqk,hqd->kd", grad_scores, query_rot, preferred_element_type=f32) * score_scale
    )
    grad_vals = jnp.einsum(
        "hqk,hqd->kd", weights.astype(bf16), grad_attended, preferred_element_type=f32
    )
    grad_pairs = jnp.concatenate([grad_keys, grad_vals], axis=1).astype(bf16)
    pair_other = pair_swap(grad_pairs[2 * tokens :], "c")
    down_pieces, gate_up_got, down_got, normed_late, branch_late = after(
        (down_pieces, gate_up_got, down_got, normed, all_grad_branch), grad_pairs
    )
    near_pairs = grad_pairs[: 2 * tokens].astype(f32) + pair_other.astype(f32)
    near_pairs = near_pairs.astype(bf16)
    pair_got = pair_swap(near_pairs[tokens:], "near")
    gate_up_rows, down_rows = near_add(gate_up_both, gate_up_got), near_add(down_both, down_got)
    gate_up_grad = to_row_owners(gate_up_rows)
    down_grad = to_row_owners(after(down_rows, gate_up_grad))
    down_sums = sum_pieces(down_pieces)
    ffn_out_far = pair_swap(down_sums[chunk_rows:].astype(bf16), "far")
    og_both = core_sum(
        *(
            jnp.concatenate(
                [
                    contract_first(normed_late, grad_gate_pre[i]).astype(bf16),
                    contract_first(branch_late, gated[i]).astype(bf16),
                ],
                axis=1,
            )
            for i in range(2)
        )
    )
    pair_got, gate_up_rows, down_rows, down_sums = after(
        (pair_got, gate_up_rows, down_rows, down_sums)
    )
    own_pair = near_pairs[:tokens].astype(f32) + pair_got.astype(f32)
    og_both = after(og_both, own_pair)
    og_got = pair_swap(og_both[og_both.shape[0] // 2 :], "near")
    grad_key_unit = turn_back(own_pair[:, :low].astype(bf16).astype(f32))
    grad_values = own_pair[:, low:].astype(bf16)
    grad_query_unit = turn_back(grad_query_rot.astype(bf16).astype(f32))
    query_gain_part = jnp.sum(grad_query_unit * query_unit, axis=(0, 1))
    key_gain_part = jnp.sum(grad_key_unit * key_unit, axis=0)
    grad_query_pre = norm_back(grad_query_unit, query_pre, inv_query, query_gain).astype(bf16)
    grad_key_pre = norm_back(grad_key_unit, key_pre, inv_key, key_gain).astype(bf16)
    key_or_value = [
        jnp.where(odd_c, grad_values, grad_key_pre),
        jnp.where(odd_c, grad_key_pre, grad_values),
    ]
    grad_qk = [
        jnp.concatenate([grad_query_pre[i], key_or_value[i]], axis=1) for i in range(2)
    ]
    normed_parts = sum(
        contract_last(grad_qk[i], side) + contract_last(grad_gate_pre[i], gate_side[:, :low])
        for i, (side, gate_side) in enumerate(((qk_mine, og_mine), (qk_other, og_other)))
    ).astype(bf16)
    normed_parts, gate_up_grad = after((normed_parts, gate_up_grad))
    grad_qk, grad_normed_two, middle, ffn_out_far, og_got, gain_two_late = after(
        (grad_qk, grad_normed_two, middle, ffn_out_far, og_got, inv_two), normed_parts
    )
    og_rows = near_add(og_both, og_got)
    og_grad = to_row_owners(after(og_rows, down_grad))
    layer_out = whole_block((middle + down_sums[:chunk_rows] + ffn_out_far.astype(f32)).astype(bf16))
    gains = jnp.concatenate(
        [
            from_own_first(jnp.sum(normed_parts.astype(f32) * normed, axis=0) / gain_one, odd_near),
            from_own_first(jnp.sum(grad_normed_two * middle * gain_two_late, axis=0), odd_near),
            query_gain_part,
            key_gain_part,
        ]
    )
    gains = (gains + plane_swap(gains, 1)) + (plane_swap(gains, 2) + plane_swap(gains, 3))
    for axis in ("near", "y", "c"):
        gains = gains + pair_swap(gains, axis)
    grad_normed = sum_chunks(normed_parts, down_grad)
    qk_both = core_sum(*(contract_first(normed, g).astype(bf16) for g in grad_qk))
    qk_rows = near_add(qk_both, pair_swap(qk_both[qk_both.shape[0] // 2 :], "near"))
    qk_grad = to_row_owners(after(qk_rows, og_grad))
    input_chunk = (grad_middle + norm_back(grad_normed, hidden32, inv_one, gain_one)).astype(bf16)
    input_grad = whole_block(input_chunk)

    def own_columns(by_z):
        kept = jnp.where(odd_c, by_z[2:], by_z[:2])
        taken = pair_swap(jnp.where(odd_c, by_z[:2], by_z[2:]), "c")
        return jnp.where(odd_c, taken, kept), jnp.where(odd_c, kept, taken)

    def per_head(halves, start):
        columns = [half[i, :, start : start + low] for i in range(2) for half in halves]
        return jnp.concatenate(columns, axis=1).astype(f32)

    def per_group(half):
        return jnp.concatenate([half[0, :, low:], half[1, :, low:]], axis=1).astype(f32)

    og_halves, qk_halves = own_columns(og_grad), own_columns(qk_grad)
    gate_weight_grad, out_weight_grad = per_head(og_halves, 0), per_head(og_halves, low)
    query_weight_grad = per_head(qk_halves, 0)
    key_weight_grad, value_weight_grad = per_group(qk_halves[0]), per_group(qk_halves[1])

    def flat(grad):
        return jnp.concatenate([grad[p] for p in range(PLANES)], axis=1).astype(f32)

    return (
        layer_out,
        input_grad,
        query_weight_grad,
        key_weight_grad,
        value_weight_grad,
        gate_weight_grad,
        out_weight_grad,
        flat(gate_up_grad[:, :, :units]),
        flat(gate_up_grad[:, :, units:]),
        flat(down_grad),
        gains[:width],
        gains[width : 2 * width],
        gains[2 * width : 2 * width + HEAD_WIDTH],
        gains[2 * width + HEAD_WIDTH :],
    )


def solution(mesh):
    wide, head = mesh.shape["wide"], mesh.shape["head"]
    if wide == 2 * PLANES and head == 4:
        devices = mesh.devices.reshape(2, 2, 2, 2, 2)
        mesh = Mesh(devices, ("far", "near", "x", "y", "c"))
        program, rows, columns = on_slice_device, ("far", "near", "x"), ("y", "c")
    else:
        program, rows, columns = on_device, "wide", "head"
    tokens, weight = P(rows, None), P(rows, columns)
    return jax.shard_map(
        program,
        mesh=mesh,
        in_specs=(tokens, tokens, P()) + (weight,) * 8 + (P(),) * 4,
        out_specs=(tokens, tokens) + (weight,) * 8 + (P(),) * 4,
        check_vma=False,
    )
```

```python
import jax
import jax.numpy as jnp
from jax import lax
from jax.experimental import pallas as pl
from jax.experimental.pallas import tpu as pltpu
from jax.sharding import Mesh
from jax.sharding import PartitionSpec as P

HEAD_WIDTH = 128


epsilon = 1e-06
rope_base = 1000000.0
masked_score = -1e30


def segment_of(lengths, token_ids):
    doc_ends = jnp.cumsum(lengths)
    return jnp.sum((token_ids[:, None] >= doc_ends[None, :]).astype(jnp.int32), axis=1)


def doc_tables(lengths, token_ids):
    doc_ends = jnp.cumsum(lengths)
    starts = doc_ends - lengths
    segment = segment_of(lengths, token_ids)
    labels = jnp.arange(lengths.shape[0], dtype=jnp.int32)
    doc_begin = jnp.sum(jnp.where(segment[:, None] == labels[None, :], starts[None, :], 0), axis=1)
    return (segment, token_ids - doc_begin)


def rope_tables(positions, head_size):
    half_size = head_size // 2
    frequency = rope_base ** (-2.0 * jnp.arange(half_size, dtype=jnp.float32) / head_size)
    angles = positions.astype(jnp.float32)[:, None] * frequency[None, :]
    cosine = jnp.cos(angles)
    sine_table = jnp.sin(angles)
    return (
        jnp.concatenate([cosine, cosine], axis=1),
        jnp.concatenate([sine_table, sine_table], axis=1),
    )


def rotate_half(values):
    half_size = values.shape[-1] // 2
    return jnp.concatenate([-values[..., half_size:], values[..., :half_size]], axis=-1)


def rotate_back(values):
    half_size = values.shape[-1] // 2
    return jnp.concatenate([values[..., half_size:], -values[..., :half_size]], axis=-1)


def apply_rope(values, cos_table, sin_table):
    return values * cos_table[:, None, :] + rotate_half(values) * sin_table[:, None, :]


def rope_back(grads, cos_table, sin_table):
    return grads * cos_table[:, None, :] + rotate_back(grads * sin_table[:, None, :])


def contract_last(left, right):
    return lax.dot_general(
        left, right, (((1,), (1,)), ((), ())), preferred_element_type=jnp.float32
    )


def contract_first(left, right):
    return lax.dot_general(
        left, right, (((0,), (0,)), ((), ())), preferred_element_type=jnp.float32
    )


def norm_back(grad_out, inputs, inv_root, gain):
    scaled = grad_out * gain
    return inv_root * scaled - inputs * inv_root**3 * jnp.mean(
        scaled * inputs, axis=-1, keepdims=True
    )


def on_device(
    hidden_in,
    out_cotangent,
    doc_lengths,
    query_weight,
    key_matrix,
    value_matrix,
    gate_weight,
    out_weight,
    ffn_gate_weight,
    ffn_up_weight,
    ffn_down_weight,
    attn_gain,
    ffn_gain,
    query_gain,
    key_gain,
):
    tok_rows = hidden_in.shape[0]
    row_length = tok_rows * lax.axis_size("wide")
    first_row = lax.axis_index("wide") * tok_rows
    token_ids = first_row + jnp.arange(tok_rows, dtype=jnp.int32)
    segment, positions = doc_tables(doc_lengths, token_ids)
    shard_begin = first_row - positions[0]
    shard_last = first_row + tok_rows - 1
    cos_table, sin_table = rope_tables(positions, HEAD_WIDTH)
    local_heads = query_weight.shape[1] // HEAD_WIDTH
    kv_heads = key_matrix.shape[1] // HEAD_WIDTH
    group_width = local_heads // kv_heads
    query_rows = group_width * tok_rows
    score_scale = HEAD_WIDTH ** (-0.5)
    (
        full_query,
        full_key,
        full_value,
        full_gate,
        full_out,
        full_ffn_gate,
        full_ffn_up,
        full_ffn_down,
    ) = (
        lax.all_gather(query_weight, "wide", axis=0, tiled=True),
        lax.all_gather(key_matrix, "wide", axis=0, tiled=True),
        lax.all_gather(value_matrix, "wide", axis=0, tiled=True),
        lax.all_gather(gate_weight, "wide", axis=0, tiled=True),
        lax.all_gather(out_weight, "wide", axis=0, tiled=True),
        lax.all_gather(ffn_gate_weight, "wide", axis=0, tiled=True),
        lax.all_gather(ffn_up_weight, "wide", axis=0, tiled=True),
        lax.all_gather(ffn_down_weight, "wide", axis=0, tiled=True),
    )
    hidden32 = hidden_in.astype(jnp.float32)
    inv_one = lax.rsqrt(jnp.mean(hidden32 * hidden32, axis=1, keepdims=True) + epsilon)
    normed_input = (hidden32 * inv_one * attn_gain).astype(jnp.bfloat16)
    query_pre = jnp.dot(normed_input, full_query, preferred_element_type=jnp.float32).reshape(
        tok_rows, local_heads, HEAD_WIDTH
    )
    key_before_norm = jnp.dot(normed_input, full_key, preferred_element_type=jnp.float32).reshape(
        tok_rows, kv_heads, HEAD_WIDTH
    )
    value_rows = jnp.dot(normed_input, full_value, preferred_element_type=jnp.float32).astype(
        jnp.bfloat16
    )
    gate_pre = jnp.dot(normed_input, full_gate, preferred_element_type=jnp.float32)
    inv_query = lax.rsqrt(jnp.mean(query_pre * query_pre, axis=-1, keepdims=True) + epsilon)
    inv_key = lax.rsqrt(
        jnp.mean(key_before_norm * key_before_norm, axis=-1, keepdims=True) + epsilon
    )
    query_unit = query_pre * inv_query
    key_unit = key_before_norm * inv_key
    query_rot = apply_rope(query_unit * query_gain, cos_table, sin_table).astype(jnp.bfloat16)
    key_rows = (
        apply_rope(key_unit * key_gain, cos_table, sin_table)
        .astype(jnp.bfloat16)
        .reshape(tok_rows, kv_heads * HEAD_WIDTH)
    )
    query_heads = (
        query_rot.reshape(tok_rows, kv_heads, group_width, HEAD_WIDTH)
        .transpose(1, 2, 0, 3)
        .reshape(kv_heads, query_rows, HEAD_WIDTH)
    )
    query_seg = jnp.tile(segment, group_width)
    query_ids = jnp.tile(token_ids, group_width)
    start_state = (
        jnp.full((kv_heads, query_rows), masked_score, jnp.float32),
        jnp.zeros((kv_heads, query_rows), jnp.float32),
        jnp.zeros((kv_heads, query_rows, HEAD_WIDTH), jnp.float32),
    )
    key_piece = lax.all_gather(key_rows, "wide", axis=0, tiled=True)
    value_piece = lax.all_gather(value_rows, "wide", axis=0, tiled=True)
    count = key_piece.shape[0]
    step_rows = 512
    steps_count = count // step_rows
    key_ids = jnp.arange(count, dtype=jnp.int32)
    key_seg = segment_of(doc_lengths, key_ids)
    key_blocks = key_piece.reshape(steps_count, step_rows, kv_heads, HEAD_WIDTH).transpose(
        0, 2, 1, 3
    )
    value_blocks = value_piece.reshape(steps_count, step_rows, kv_heads, HEAD_WIDTH).transpose(
        0, 2, 1, 3
    )

    def inner(state, block):
        key_block, value_block, block_seg, block_ids = block

        def inner_work(state_in):
            scores = (
                jnp.einsum(
                    "hqd,hkd->hqk", query_heads, key_block, preferred_element_type=jnp.float32
                )
                * score_scale
            )
            allowed = (
                (query_seg[:, None] == block_seg[None, :])
                & (block_ids[None, :] <= query_ids[:, None])
            )[None]
            scores = jnp.where(allowed, scores, masked_score)
            running, total, accum = state_in
            newest = jnp.maximum(running, jnp.max(scores, axis=-1))
            factor = jnp.exp(running - newest)
            weights = jnp.where(allowed, jnp.exp(scores - newest[..., None]), 0.0)
            total = total * factor + jnp.sum(weights, axis=-1)
            accum = accum * factor[..., None] + jnp.einsum(
                "hqk,hkd->hqd",
                weights.astype(jnp.bfloat16),
                value_block,
                preferred_element_type=jnp.float32,
            )
            return (newest, total, accum)

        useful = (block_ids[0] <= shard_last) & (block_ids[step_rows - 1] >= shard_begin)
        return (lax.cond(useful, inner_work, lambda state_in: state_in, state), None)

    state, unused = lax.scan(
        inner,
        start_state,
        (
            key_blocks,
            value_blocks,
            key_seg.reshape(steps_count, step_rows),
            key_ids.reshape(steps_count, step_rows),
        ),
    )
    running, total, accum = state
    attended_heads = accum / total[..., None]
    log_total = running + jnp.log(total)
    attended = (
        attended_heads.reshape(kv_heads, group_width, tok_rows, HEAD_WIDTH)
        .transpose(2, 0, 1, 3)
        .reshape(tok_rows, local_heads * HEAD_WIDTH)
    )
    gate_sig = jax.nn.sigmoid(gate_pre)
    gated = (attended * gate_sig).astype(jnp.bfloat16)
    branch = lax.psum(contract_last(gated, full_out).astype(jnp.bfloat16), "head").astype(
        jnp.float32
    )
    middle = hidden32 + branch
    inv_two = lax.rsqrt(jnp.mean(middle * middle, axis=1, keepdims=True) + epsilon)
    normed_two = (middle * inv_two * ffn_gain).astype(jnp.bfloat16)
    ffn_gate_pre = jnp.dot(normed_two, full_ffn_gate, preferred_element_type=jnp.float32)
    ffn_up_pre = jnp.dot(normed_two, full_ffn_up, preferred_element_type=jnp.float32)
    gate_act = jax.nn.sigmoid(ffn_gate_pre)
    silu_gate = ffn_gate_pre * gate_act
    hidden_act = (silu_gate * ffn_up_pre).astype(jnp.bfloat16)
    ffn_out = lax.psum(
        contract_last(hidden_act, full_ffn_down).astype(jnp.bfloat16), "head"
    ).astype(jnp.float32)
    layer_out = (middle + ffn_out).astype(jnp.bfloat16)
    grad32 = out_cotangent.astype(jnp.float32)
    grad_hidden = jnp.dot(out_cotangent, full_ffn_down, preferred_element_type=jnp.float32)
    grad_ffn_gate = (
        grad_hidden * ffn_up_pre * gate_act * (1.0 + ffn_gate_pre * (1.0 - gate_act))
    ).astype(jnp.bfloat16)
    grad_ffn_up = (grad_hidden * silu_gate).astype(jnp.bfloat16)
    grad_normed_two = lax.psum(
        (
            contract_last(grad_ffn_gate, full_ffn_gate) + contract_last(grad_ffn_up, full_ffn_up)
        ).astype(jnp.bfloat16),
        "head",
    ).astype(jnp.float32)
    grad_middle = grad32 + norm_back(grad_normed_two, middle, inv_two, ffn_gain)
    grad_branch = grad_middle.astype(jnp.bfloat16)
    grad_gated = jnp.dot(grad_branch, full_out, preferred_element_type=jnp.float32)
    grad_attended = (grad_gated * gate_sig).astype(jnp.bfloat16)
    grad_gate_pre = (grad_gated * attended * gate_sig * (1.0 - gate_sig)).astype(jnp.bfloat16)
    grad_heads = (
        grad_attended.reshape(tok_rows, kv_heads, group_width, HEAD_WIDTH)
        .transpose(1, 2, 0, 3)
        .reshape(kv_heads, query_rows, HEAD_WIDTH)
    )
    delta = jnp.sum(grad_heads.astype(jnp.float32) * attended_heads, axis=-1)
    all_keys, all_values = key_piece, value_piece
    key_step = 512
    key_count = row_length // key_step
    all_ids = jnp.arange(row_length, dtype=jnp.int32)
    all_seg = segment_of(doc_lengths, all_ids)
    key_blocks = all_keys.reshape(key_count, key_step, kv_heads, HEAD_WIDTH).transpose(0, 2, 1, 3)
    value_blocks = all_values.reshape(key_count, key_step, kv_heads, HEAD_WIDTH).transpose(
        0, 2, 1, 3
    )
    key_scan_items = (
        key_blocks,
        value_blocks,
        all_seg.reshape(key_count, key_step),
        all_ids.reshape(key_count, key_step),
    )
    zero_query = jnp.zeros((kv_heads, query_rows, HEAD_WIDTH), jnp.float32)

    def block_terms(key_block, value_block, block_seg, block_ids):
        scores = (
            jnp.einsum("hqd,hkd->hqk", query_heads, key_block, preferred_element_type=jnp.float32)
            * score_scale
        )
        allowed = (
            (query_seg[:, None] == block_seg[None, :]) & (block_ids[None, :] <= query_ids[:, None])
        )[None]
        weights = jnp.where(
            allowed, jnp.exp(jnp.where(allowed, scores, masked_score) - log_total[..., None]), 0.0
        )
        grad_weights = jnp.einsum(
            "hqd,hkd->hqk", grad_heads, value_block, preferred_element_type=jnp.float32
        )
        grad_scores = (weights * (grad_weights - delta[..., None])).astype(jnp.bfloat16)
        return (weights, grad_scores)

    def block_useful(block_ids):
        return (block_ids[0] <= shard_last) & (block_ids[key_step - 1] >= shard_begin)

    def back_block(grad_query, block):
        key_block, value_block, block_seg, block_ids = block

        def back_work(grad_in):
            weights, grad_scores = block_terms(key_block, value_block, block_seg, block_ids)
            grad_out = (
                grad_in
                + jnp.einsum(
                    "hqk,hkd->hqd", grad_scores, key_block, preferred_element_type=jnp.float32
                )
                * score_scale
            )
            grad_key = (
                jnp.einsum(
                    "hqk,hqd->hkd", grad_scores, query_heads, preferred_element_type=jnp.float32
                )
                * score_scale
            )
            grad_value = jnp.einsum(
                "hqk,hqd->hkd",
                weights.astype(jnp.bfloat16),
                grad_heads,
                preferred_element_type=jnp.float32,
            )
            return (grad_out, (grad_key, grad_value))

        def skip(grad_in):
            nothing = jnp.zeros((kv_heads, key_step, HEAD_WIDTH), jnp.float32)
            return (grad_in, (nothing, nothing))

        return lax.cond(block_useful(block_ids), back_work, skip, grad_query)

    grad_query, (key_parts, value_parts) = lax.scan(back_block, zero_query, key_scan_items)
    key_grad_rows = key_parts.transpose(0, 2, 1, 3).reshape(row_length, kv_heads * HEAD_WIDTH)
    value_grad_rows = value_parts.transpose(0, 2, 1, 3).reshape(row_length, kv_heads * HEAD_WIDTH)
    key_total, value_total = (
        lax.psum_scatter(
            key_grad_rows.astype(jnp.bfloat16), "wide", scatter_dimension=0, tiled=True
        ).astype(jnp.float32),
        lax.psum_scatter(
            value_grad_rows.astype(jnp.bfloat16), "wide", scatter_dimension=0, tiled=True
        ).astype(jnp.float32),
    )
    grad_values = value_total.astype(jnp.bfloat16)
    grad_key_rot = (
        key_total.astype(jnp.bfloat16).astype(jnp.float32).reshape(tok_rows, kv_heads, HEAD_WIDTH)
    )
    grad_query_rot = (
        grad_query.astype(jnp.bfloat16)
        .astype(jnp.float32)
        .reshape(kv_heads, group_width, tok_rows, HEAD_WIDTH)
        .transpose(2, 0, 1, 3)
        .reshape(tok_rows, local_heads, HEAD_WIDTH)
    )
    grad_query_unit = rope_back(grad_query_rot, cos_table, sin_table)
    grad_key_unit = rope_back(grad_key_rot, cos_table, sin_table)
    query_gain_part = jnp.sum(grad_query_unit * query_unit, axis=(0, 1))
    key_gain_part = jnp.sum(grad_key_unit * key_unit, axis=(0, 1))
    grad_query_pre = (
        norm_back(grad_query_unit, query_pre, inv_query, query_gain)
        .reshape(tok_rows, local_heads * HEAD_WIDTH)
        .astype(jnp.bfloat16)
    )
    grad_key_pre = (
        norm_back(grad_key_unit, key_before_norm, inv_key, key_gain)
        .reshape(tok_rows, kv_heads * HEAD_WIDTH)
        .astype(jnp.bfloat16)
    )
    grad_normed_part = (
        contract_last(grad_query_pre, full_query)
        + contract_last(grad_key_pre, full_key)
        + contract_last(grad_values, full_value)
        + contract_last(grad_gate_pre, full_gate)
    )
    grad_normed = lax.psum(grad_normed_part.astype(jnp.bfloat16), "head").astype(jnp.float32)
    input_grad = (grad_middle + norm_back(grad_normed, hidden32, inv_one, attn_gain)).astype(
        jnp.bfloat16
    )
    attn_gain_part = jnp.sum(grad_normed * hidden32 * inv_one, axis=0)
    ffn_gain_part = jnp.sum(grad_normed_two * middle * inv_two, axis=0)
    weight_grads = lax.psum_scatter(
        jnp.concatenate(
            [
                contract_first(normed_input, grad_query_pre),
                contract_first(normed_input, grad_key_pre),
                contract_first(normed_input, grad_values),
                contract_first(normed_input, grad_gate_pre),
                contract_first(grad_branch, gated),
                contract_first(normed_two, grad_ffn_gate),
                contract_first(normed_two, grad_ffn_up),
                contract_first(out_cotangent, hidden_act),
            ],
            axis=1,
        ).astype(jnp.bfloat16),
        "wide",
        scatter_dimension=0,
        tiled=True,
    ).astype(jnp.float32)
    col_widths = [
        query_weight.shape[1],
        key_matrix.shape[1],
        value_matrix.shape[1],
        gate_weight.shape[1],
        out_weight.shape[1],
        ffn_gate_weight.shape[1],
        ffn_up_weight.shape[1],
        ffn_down_weight.shape[1],
    ]
    pieces = []
    offset = 0
    for width in col_widths:
        pieces.append(weight_grads[:, offset : offset + width])
        offset = offset + width
    head_first = (lax.axis_index("head") == 0).astype(jnp.float32)
    attn_gain_grad, ffn_gain_grad, query_gain_grad, key_gain_grad = lax.psum(
        (attn_gain_part * head_first, ffn_gain_part * head_first, query_gain_part, key_gain_part),
        ("wide", "head"),
    )
    return (
        layer_out,
        input_grad,
        pieces[0],
        pieces[1],
        pieces[2],
        pieces[3],
        pieces[4],
        pieces[5],
        pieces[6],
        pieces[7],
        attn_gain_grad,
        ffn_gain_grad,
        query_gain_grad,
        key_gain_grad,
    )


PLANES = 4
PLANE = ("far", "x")


def pair_swap(values, axis):
    return lax.ppermute(values, axis, [(0, 1), (1, 0)])


def plane_swap(values, step):
    return lax.ppermute(values, PLANE, [(i, i ^ step) for i in range(PLANES)])


def side_swap(values, step):
    return lax.ppermute(values, ("x", "y"), [(i, i ^ step) for i in range(4)])


def after(values, *done):
    return lax.optimization_barrier((values, done))[0]


def gather_chunks(chunk):
    far = pair_swap(chunk, "far")
    near = [side_swap(chunk, step) for step in range(1, 4)]
    away = [side_swap(far, step) for step in range(1, 4)]
    pieces = [chunk, far]
    for pair in zip(near, away):
        pieces.extend(pair)
    return pieces


def sum_sends(parts):
    return [
        [parts[far]] + [side_swap(parts[2 * step + far], step) for step in range(1, 4)]
        for far in (1, 0)
    ]


def sum_pieces(pieces):
    total = pieces[0].astype(jnp.float32)
    for piece in pieces[1:]:
        total = total + piece.astype(jnp.float32)
    return total


def flip_if(values, axis, flag):
    return jnp.where(flag, jnp.flip(values, axis), values)


def to_own_first(values, flag):
    lead = values.shape[:-1]
    width = values.shape[-1]
    split = values.reshape(lead + (2, 2, width // 4))
    zero = split[..., 0, :].reshape(lead + (width // 2,))
    one = split[..., 1, :].reshape(lead + (width // 2,))
    return jnp.concatenate([jnp.where(flag, one, zero), jnp.where(flag, zero, one)], axis=-1)


def from_own_first(values, flag):
    lead = values.shape[:-1]
    width = values.shape[-1]
    own = values[..., : width // 2].reshape(lead + (2, width // 4))
    other = values[..., width // 2 :].reshape(lead + (2, width // 4))
    pair = jnp.stack([jnp.where(flag, other, own), jnp.where(flag, own, other)], axis=-2)
    return pair.reshape(lead + (width,))


def to_plane_owners(local):
    planes, rows, width = local.shape
    return lax.all_to_all(
        local.reshape(planes * rows, width), PLANE, split_axis=0, concat_axis=0, tiled=True
    )


HEADS = ("far", "x", "c")


def head_pairs(a, b, back):
    pairs = []
    for f in range(2):
        for x in range(2):
            for c in range(2):
                pairs.append((4 * f + 2 * x + c, 4 * c + 2 * (x ^ a) + (f ^ b)))
    return [(j, i) for i, j in pairs] if back else pairs


def to_head_owners(columns, far, x, c):
    turned = flip_if(flip_if(columns, 0, x == 1), 1, far == 1)
    sent = [
        [lax.ppermute(turned[a, b], HEADS, head_pairs(a, b, False)) for a in range(2)]
        for b in range(2)
    ]
    pieces = jnp.stack([jnp.stack(row) for row in sent])
    rows = flip_if(flip_if(pieces, 0, c == 1), 1, x == 1)
    return rows.reshape(PLANES * columns.shape[2], columns.shape[3]), sent


def from_head_owners(rows, far, x, c):
    blocks = rows.reshape(2, 2, rows.shape[0] // PLANES, rows.shape[1])
    blocks = flip_if(flip_if(blocks, 0, c == 1), 1, x == 1)
    pieces = jnp.stack(
        [
            jnp.stack(
                [lax.ppermute(blocks[b, a], HEADS, head_pairs(a, b, True)) for b in range(2)]
            )
            for a in range(2)
        ]
    )
    return flip_if(flip_if(pieces, 0, x == 1), 1, far == 1)


def core_sum(mine, other):
    both = mine.astype(jnp.float32) + pair_swap(other, "c").astype(jnp.float32)
    return both.astype(jnp.bfloat16)


def near_add(both, got):
    half = both.shape[0] // 2
    return (both[:half].astype(jnp.float32) + got.astype(jnp.float32)).astype(jnp.bfloat16)


def to_row_owners(rows):
    back = lax.all_to_all(rows, PLANE, split_axis=0, concat_axis=0, tiled=True)
    return back.reshape(PLANES, rows.shape[0] // PLANES, rows.shape[1])


VMEM_BYTES = 56 * 1024 * 1024


def kernel_call(body, operands, outs, scratch=(), flags=None, flops=0):
    specs = [pl.BlockSpec(memory_space=pltpu.VMEM)] * len(operands)
    if flags is not None:
        operands = [flags] + list(operands)
        specs = [pl.BlockSpec(memory_space=pltpu.SMEM)] + specs
    moved = sum(v.size * v.dtype.itemsize for v in operands)
    moved += sum(v.size * v.dtype.itemsize for v in outs)
    return pl.pallas_call(
        body,
        out_shape=outs,
        in_specs=specs,
        out_specs=[pl.BlockSpec(memory_space=pltpu.VMEM)] * len(outs),
        scratch_shapes=list(scratch),
        compiler_params=pltpu.CompilerParams(vmem_limit_bytes=VMEM_BYTES),
        cost_estimate=pl.CostEstimate(flops=flops, bytes_accessed=moved, transcendentals=0),
    )(*operands)


def shaped(shape, dtype):
    return jax.ShapeDtypeStruct(shape, dtype)


def dot_nn(left, right):
    return jnp.dot(left, right, preferred_element_type=jnp.float32)


def turned(values, cosine, signed_sine):
    return values * cosine + pltpu.roll(values, HEAD_WIDTH // 2, 1) * signed_sine


def turned_back(grads, cosine, signed_sine):
    return grads * cosine - pltpu.roll(grads, HEAD_WIDTH // 2, 1) * signed_sine


def sigmoid(values):
    return 1.0 / (1.0 + jnp.exp(-values))


def project_kernel(flag, *refs):
    hidden = refs[:8]
    gain, mine_own, mine_near, other_own, other_near, cosine, sine, qgain, kgain = refs[8:17]
    normed, pair, query_rot, query_pre, key_pre, scratch = refs[17:]
    rows = hidden[0].shape[0]
    for i in range(8):
        h = hidden[i][...].astype(jnp.float32)
        inverse = lax.rsqrt(jnp.mean(h * h, axis=1, keepdims=True) + epsilon)
        normed[i * rows : (i + 1) * rows, :] = (h * inverse * gain[...]).astype(jnp.bfloat16)
    half = normed.shape[1] // 2
    left, right = normed[:, :half], normed[:, half:]
    for i, (own, near) in enumerate(((mine_own, mine_near), (other_own, other_near))):
        scratch[i] = dot_nn(left, own[...]) + dot_nn(right, near[...])
    cos, sin = cosine[...], sine[...]
    swapped = flag[0] == 1
    mine, other = scratch[0, :, HEAD_WIDTH:], scratch[1, :, HEAD_WIDTH:]
    pre = jnp.where(swapped, other, mine)
    key_pre[...] = pre
    pair[:, HEAD_WIDTH:] = jnp.where(swapped, mine, other).astype(jnp.bfloat16)
    unit = pre * lax.rsqrt(jnp.mean(pre * pre, axis=1, keepdims=True) + epsilon)
    pair[:, :HEAD_WIDTH] = turned(unit * kgain[...], cos, sin).astype(jnp.bfloat16)
    for i in range(2):
        pre = scratch[i, :, :HEAD_WIDTH]
        query_pre[i] = pre
        unit = pre * lax.rsqrt(jnp.mean(pre * pre, axis=1, keepdims=True) + epsilon)
        query_rot[i] = turned(unit * qgain[...], cos, sin).astype(jnp.bfloat16)


def attend_kernel(query_rot, first, second, third, fourth, bounds, key_ids, gate_pre, *refs):
    outs_w, gated, attended, log_total, parts, total = refs[:4], *refs[4:7], refs[7:15], refs[15]
    scale = HEAD_WIDTH ** (-0.5)
    pairs = (first, second, third, fourth)
    rows = first.shape[0]
    tile = rows // 2

    def step(i, carry):
        head, at = i // 2, pl.multiple_of(i % 2 * tile, tile)
        query = query_rot[head, pl.ds(at, tile), :]
        start, last = bounds[pl.ds(at, tile), 0:1], bounds[pl.ds(at, tile), 1:2]
        scores = []
        for j, pair in enumerate(pairs):
            ids = key_ids[:, j * rows : (j + 1) * rows]
            allowed = (ids >= start) & (ids <= last)
            score = contract_last(query, pair[:, :HEAD_WIDTH]) * scale
            scores.append(jnp.where(allowed, score, masked_score))
        top = jnp.max(scores[0], axis=1, keepdims=True)
        for score in scores[1:]:
            top = jnp.maximum(top, jnp.max(score, axis=1, keepdims=True))
        total = jnp.zeros_like(top)
        result = jnp.zeros((tile, HEAD_WIDTH), jnp.float32)
        for score, pair in zip(scores, pairs):
            raised = jnp.exp(score - top)
            total = total + jnp.sum(raised, axis=1, keepdims=True)
            result = result + dot_nn(raised.astype(jnp.bfloat16), pair[:, HEAD_WIDTH:])
        result = result / total
        attended[head, pl.ds(at, tile), :] = result
        log_total[head, pl.ds(at, tile), :] = jnp.broadcast_to(top + jnp.log(total), result.shape)
        gate = sigmoid(gate_pre[head, pl.ds(at, tile), :])
        gated[head, pl.ds(at, tile), :] = (result * gate).astype(jnp.bfloat16)
        return carry

    lax.fori_loop(0, 4, step, 0)
    half = total.shape[1] // 2
    for near in range(2):
        total[:, near * half : (near + 1) * half] = contract_last(
            gated[0], outs_w[near][:, HEAD_WIDTH:]
        ) + contract_last(gated[1], outs_w[2 + near][:, HEAD_WIDTH:])
    rows = parts[0].shape[0]
    for i in range(8):
        parts[i][...] = total[i * rows : (i + 1) * rows, :].astype(jnp.bfloat16)


def ffn_kernel(*refs):
    chunks, cotangent, gate_up, down = refs[:8], refs[8:12], refs[12:16], refs[16:20]
    acts, grads, two_parts, down_parts = refs[20:22], refs[22:24], refs[24:32], refs[32:36]
    normed_two, cot, total = refs[36:]
    rows = chunks[0].shape[0]
    for i in range(8):
        normed_two[i * rows : (i + 1) * rows, :] = chunks[i][...]
    rows = cotangent[0].shape[0]
    for i in range(4):
        cot[i * rows : (i + 1) * rows, :] = cotangent[i][...]
    half = cot.shape[1] // 2
    units = down[0].shape[1]
    tile = cot.shape[0] // 2

    def step(i, carry):
        at = pl.multiple_of(i * tile, tile)
        rows_at = pl.ds(at, tile)
        for side in range(2):
            wide = [gate_up[2 * side][...], gate_up[2 * side + 1][...]]
            pre = dot_nn(normed_two[rows_at, :half], wide[0]) + dot_nn(
                normed_two[rows_at, half:], wide[1]
            )
            grad = dot_nn(cot[rows_at, :half], down[2 * side][...]) + dot_nn(
                cot[rows_at, half:], down[2 * side + 1][...]
            )
            gate, up = pre[:, :units], pre[:, units:]
            act = sigmoid(gate)
            silu = gate * act
            acts[side][rows_at, :] = (silu * up).astype(jnp.bfloat16)
            grads[side][rows_at, :units] = (
                grad * up * act * (1.0 + gate * (1.0 - act))
            ).astype(jnp.bfloat16)
            grads[side][rows_at, units:] = (grad * silu).astype(jnp.bfloat16)
        for near in range(2):
            total[0, rows_at, near * half : (near + 1) * half] = contract_last(
                grads[0][rows_at, :], gate_up[near][...]
            ) + contract_last(grads[1][rows_at, :], gate_up[2 + near][...])
            total[1, rows_at, near * half : (near + 1) * half] = contract_last(
                acts[0][rows_at, :], down[near][...]
            ) + contract_last(acts[1][rows_at, :], down[2 + near][...])
        return carry

    lax.fori_loop(0, 2, step, 0)
    rows = two_parts[0].shape[0]
    for i in range(8):
        two_parts[i][...] = total[0, i * rows : (i + 1) * rows, :].astype(jnp.bfloat16)
    rows = down_parts[0].shape[0]
    for i in range(4):
        down_parts[i][...] = total[1, i * rows : (i + 1) * rows, :].astype(jnp.bfloat16)


def attend_back_kernel(*refs):
    chunks, outs_w, pairs = refs[:8], refs[8:12], refs[12:16]
    bounds, key_ids, query_rot, query_pre, gate_pre, attended, log_total = refs[16:23]
    cosine, sine, qgain = refs[23:26]
    branch, grad_gate, grad_query, grad_pairs, gain_part = refs[26:31]
    gated_grad, keys_acc, vals_acc = refs[31:]
    scale = HEAD_WIDTH ** (-0.5)
    rows = chunks[0].shape[0]
    for i in range(8):
        branch[i * rows : (i + 1) * rows, :] = chunks[i][...]
    half = branch.shape[1] // 2
    for side in range(2):
        gated_grad[side] = dot_nn(branch[:, :half], outs_w[2 * side][:, HEAD_WIDTH:]) + dot_nn(
            branch[:, half:], outs_w[2 * side + 1][:, HEAD_WIDTH:]
        )
    keys_acc[...] = jnp.zeros_like(keys_acc)
    vals_acc[...] = jnp.zeros_like(vals_acc)
    gain_part[...] = jnp.zeros_like(gain_part)
    rows = pairs[0].shape[0]
    tile = rows // 2

    def step(i, carry):
        head, at = i // 2, pl.multiple_of(i % 2 * tile, tile)
        rows_at = pl.ds(at, tile)
        grad = gated_grad[head, rows_at, :]
        gate = sigmoid(gate_pre[head, rows_at, :])
        out = attended[head, rows_at, :]
        grad_gate[head, rows_at, :] = (grad * out * gate * (1.0 - gate)).astype(jnp.bfloat16)
        grad_out = (grad * gate).astype(jnp.bfloat16)
        delta = jnp.sum(grad_out.astype(jnp.float32) * out, axis=1, keepdims=True)
        query = query_rot[head, rows_at, :]
        start, last = bounds[rows_at, 0:1], bounds[rows_at, 1:2]
        log = log_total[head, rows_at, 0:1]
        grad_rot = jnp.zeros((tile, HEAD_WIDTH), jnp.float32)
        for j, pair in enumerate(pairs):
            ids = key_ids[:, j * rows : (j + 1) * rows]
            allowed = (ids >= start) & (ids <= last)
            keys, vals = pair[:, :HEAD_WIDTH], pair[:, HEAD_WIDTH:]
            score = jnp.where(allowed, contract_last(query, keys) * scale, masked_score)
            weight = jnp.exp(score - log)
            grad_score = (weight * (contract_last(grad_out, vals) - delta)).astype(jnp.bfloat16)
            grad_rot = grad_rot + dot_nn(grad_score, keys)
            at_keys = slice(j * rows, (j + 1) * rows)
            keys_acc[at_keys, :] += contract_first(grad_score, query)
            vals_acc[at_keys, :] += contract_first(weight.astype(jnp.bfloat16), grad_out)
        grad_rot = (grad_rot * scale).astype(jnp.bfloat16).astype(jnp.float32)
        grad_unit = turned_back(grad_rot, cosine[rows_at, :], sine[rows_at, :])
        pre = query_pre[head, rows_at, :]
        inverse = lax.rsqrt(jnp.mean(pre * pre, axis=1, keepdims=True) + epsilon)
        gain_part[...] += jnp.sum(grad_unit * (pre * inverse), axis=0, keepdims=True)
        grad_query[head, rows_at, :] = norm_back(grad_unit, pre, inverse, qgain[...]).astype(
            jnp.bfloat16
        )
        return carry

    lax.fori_loop(0, 4, step, 0)
    grad_pairs[:, :HEAD_WIDTH] = (keys_acc[...] * scale).astype(jnp.bfloat16)
    grad_pairs[:, HEAD_WIDTH:] = vals_acc[...].astype(jnp.bfloat16)


def tables_kernel(lengths, coords, frequency, bounds, key_ids, angles):
    far, near, x, y, c = (coords[i] for i in range(5))
    rows = bounds.shape[0] // 8

    def ids_of(at, near_at, c_at):
        chunk, row = at // rows, at % rows
        x_at, y_at, far_at = x ^ (chunk // 4), y ^ (chunk // 2 % 2), far ^ (chunk % 2)
        return (((far_at * 2 + near_at) * 2 + x_at) * 4 + y_at * 2 + c_at) * rows + row

    at = lax.broadcasted_iota(jnp.int32, bounds.shape, 0)
    lane = lax.broadcasted_iota(jnp.int32, bounds.shape, 1)
    ids = ids_of(at, near, c)
    start = jnp.zeros_like(ids)
    end = jnp.int32(0)
    for i in range(lengths.shape[0]):
        end = end + lengths[i]
        start = jnp.where(ids >= end, end, start)
    bounds[...] = jnp.where(lane == 0, start, ids)
    angles[...] = (ids - start).astype(jnp.float32) * frequency[...]
    at = lax.broadcasted_iota(jnp.int32, key_ids.shape, 1)
    group = at // (8 * rows)
    key_ids[...] = ids_of(at % (8 * rows), near ^ (group % 2), c ^ (group // 2))


def gate_kernel(normed, mine_own, mine_near, other_own, other_near, gate_pre):
    half = normed.shape[1] // 2
    for i, (own, near) in enumerate(((mine_own, mine_near), (other_own, other_near))):
        gate_pre[i] = dot_nn(normed[:, :half], own[:, :HEAD_WIDTH]) + dot_nn(
            normed[:, half:], near[:, :HEAD_WIDTH]
        )


def input_kernel(flag, *refs):
    own_pair, got_pair, key_pre, cosine, sine, kgain, grad_query, grad_gate, normed = refs[:9]
    qk, og = refs[9:13], refs[13:17]
    grad_qk, parts, key_gain, input_gain, total = refs[17:19], refs[19:27], refs[27], refs[28], refs[29]
    pair = own_pair[...].astype(jnp.float32) + got_pair[...].astype(jnp.float32)
    grad_unit = turned_back(
        pair[:, :HEAD_WIDTH].astype(jnp.bfloat16).astype(jnp.float32), cosine[...], sine[...]
    )
    pre = key_pre[...]
    inverse = lax.rsqrt(jnp.mean(pre * pre, axis=1, keepdims=True) + epsilon)
    key_gain[...] = jnp.sum(grad_unit * (pre * inverse), axis=0, keepdims=True)
    grad_key = norm_back(grad_unit, pre, inverse, kgain[...]).astype(jnp.bfloat16)
    grad_value = pair[:, HEAD_WIDTH:].astype(jnp.bfloat16)
    swapped = flag[0] == 1
    for side in range(2):
        grad_qk[side][:, :HEAD_WIDTH] = grad_query[side]
        first, second = (grad_key, grad_value) if side == 0 else (grad_value, grad_key)
        grad_qk[side][:, HEAD_WIDTH:] = jnp.where(swapped, second, first)
    half = total.shape[1] // 2
    tile = total.shape[0] // 2

    def step(i, carry):
        rows_at = pl.ds(pl.multiple_of(i * tile, tile), tile)
        for near in range(2):
            acc = None
            for side in range(2):
                part = contract_last(grad_qk[side][rows_at, :], qk[2 * side + near][...])
                part = part + contract_last(
                    grad_gate[side, rows_at, :], og[2 * side + near][:, :HEAD_WIDTH]
                )
                acc = part if acc is None else acc + part
            total[rows_at, near * half : (near + 1) * half] = acc
        return carry

    lax.fori_loop(0, 2, step, 0)
    rows = parts[0].shape[0]
    gain = jnp.zeros(input_gain.shape, jnp.float32)
    for i in range(8):
        part = total[i * rows : (i + 1) * rows, :]
        parts[i][...] = part.astype(jnp.bfloat16)
        gain = gain + jnp.sum(
            part * normed[i * rows : (i + 1) * rows, :].astype(jnp.float32), axis=0, keepdims=True
        )
    input_gain[...] = gain


def on_slice_device(
    hidden_in,
    out_cotangent,
    doc_lengths,
    query_weight,
    key_matrix,
    value_matrix,
    gate_weight,
    out_weight,
    ffn_gate_weight,
    ffn_up_weight,
    ffn_down_weight,
    attn_gain,
    ffn_gain,
    query_gain,
    key_gain,
):
    bf16, f32 = jnp.bfloat16, jnp.float32
    block_rows, width = hidden_in.shape
    chunk_rows = block_rows // 4
    tokens = 8 * chunk_rows
    low = HEAD_WIDTH
    units = ffn_gate_weight.shape[1] // PLANES
    coords = [lax.axis_index(name) for name in ("far", "near", "x", "y", "c")]
    far, near, x, y, c = coords
    odd_near = near == 1
    core_flag = c.reshape(1)

    def columns(x_at, head):
        at = (2 * x_at + head) * low
        third = (key_matrix if head == 0 else value_matrix)[:, x_at * low : (x_at + 1) * low]
        parts = (query_weight[:, at : at + low], third)
        parts += (gate_weight[:, at : at + low], out_weight[:, at : at + low])
        return jnp.concatenate(parts, axis=1)

    own_hidden = to_own_first(
        lax.dynamic_slice_in_dim(hidden_in, (y * 2 + c) * chunk_rows, chunk_rows, 0), odd_near
    )
    hidden = gather_chunks(own_hidden)
    attn_half, attn_sent = to_head_owners(
        jnp.stack([jnp.stack([columns(i, j) for j in range(2)]) for i in range(2)]), far, x, c
    )
    qk_half, og_half = attn_half[:, : 2 * low], attn_half[:, 2 * low :]
    qk_near = pair_swap(qk_half, "near")
    og_near = pair_swap(after(og_half, qk_near), "near")
    qk = [qk_half, qk_near, pair_swap(qk_half, "c"), pair_swap(after(qk_near, hidden), "c")]
    gain_one = to_own_first(attn_gain, odd_near)
    out_cotangent, ffn_gain = after((out_cotangent, ffn_gain), hidden[1])
    cotangent = to_own_first(
        lax.dynamic_slice_in_dim(out_cotangent, (y * 2 + c) * chunk_rows, chunk_rows, 0), odd_near
    )
    gain_two = to_own_first(ffn_gain, odd_near)
    cotangent_far = pair_swap(cotangent, "far")
    hidden, cotangent_far = after((hidden, cotangent_far))
    ffn_gate_weight, ffn_up_weight, ffn_down_weight = after(
        (ffn_gate_weight, ffn_up_weight, ffn_down_weight), qk_near, hidden, cotangent_far
    )
    cotangent_pair = jnp.concatenate([cotangent, cotangent_far], axis=0)
    cotangents = [cotangent_pair] + [side_swap(cotangent_pair, i) for i in range(1, 4)]

    def by_plane(*weights):
        return jnp.stack(
            [
                jnp.concatenate([w[:, p * units : (p + 1) * units] for w in weights], axis=1)
                for p in range(PLANES)
            ]
        )

    gate_up_half = to_plane_owners(by_plane(ffn_gate_weight, ffn_up_weight))

    half_width = low // 2
    frequency = rope_base ** (-2.0 * jnp.arange(half_width, dtype=f32) / low)
    frequency = jnp.concatenate([frequency, frequency])[None, :]
    bounds, key_ids, angles = pl.pallas_call(
        tables_kernel,
        out_shape=[
            shaped((tokens, low), jnp.int32),
            shaped((1, 4 * tokens), jnp.int32),
            shaped((tokens, low), f32),
        ],
        in_specs=[pl.BlockSpec(memory_space=pltpu.SMEM)] * 2
        + [pl.BlockSpec(memory_space=pltpu.VMEM)],
        out_specs=[pl.BlockSpec(memory_space=pltpu.VMEM)] * 3,
    )(after(doc_lengths, qk_near), jnp.stack(coords), frequency)
    sign = jnp.where(jnp.arange(low) < half_width, -1.0, 1.0).astype(f32)
    cosine, sine = jnp.cos(angles), jnp.sin(angles) * sign[None, :]
    query_gain, key_gain = query_gain[None, :], key_gain[None, :]

    normed, pair, query_rot, query_pre, key_pre = kernel_call(
        project_kernel,
        hidden + [gain_one[None, :]] + qk + [cosine, sine, query_gain, key_gain],
        [
            shaped((tokens, width), bf16),
            shaped((tokens, 2 * low), bf16),
            shaped((2, tokens, low), bf16),
            shaped((2, tokens, low), f32),
            shaped((tokens, low), f32),
        ],
        [pltpu.VMEM((2, tokens, 2 * low), f32)],
        core_flag,
        4 * tokens * width * 2 * low,
    )
    pair_near = pair_swap(pair, "near")
    pairs = [pair, pair_near, pair_swap(pair, "c"), pair_swap(pair_near, "c")]

    og = [og_half, og_near] + [pair_swap(after(part, pair), "c") for part in (og_half, og_near)]
    gate_up_near = pair_swap(after(gate_up_half, pair_near), "near")
    down_half = to_plane_owners(after(by_plane(ffn_down_weight), gate_up_half))
    query_rot, cotangents, gate_up_half = after((query_rot, cotangents, gate_up_half))

    (gate_pre,) = kernel_call(
        gate_kernel,
        [normed] + og,
        [shaped((2, tokens, low), f32)],
        flops=4 * tokens * width * low,
    )
    outs = kernel_call(
        attend_kernel,
        [query_rot] + pairs + [bounds, key_ids, gate_pre] + og,
        [shaped((2, tokens, low), bf16)]
        + [shaped((2, tokens, low), f32)] * 2
        + [shaped((chunk_rows, width), bf16)] * 8,
        [pltpu.VMEM((tokens, width), f32)],
        None,
        8 * tokens * 4 * tokens * low,
    )
    gated, attended, log_total, branch_parts = outs[0], outs[1], outs[2], outs[3:]
    away, own = sum_sends(branch_parts)
    away, gate_up_near, down_half = after((sum_pieces(away).astype(bf16), gate_up_near, down_half))
    hidden32 = own_hidden.astype(f32)
    middle = hidden32 + sum_pieces(own + [pair_swap(away, "far")])
    inv_two = lax.rsqrt(jnp.mean(middle * middle, axis=1, keepdims=True) + epsilon)
    normed_two_chunk = (middle * inv_two * gain_two).astype(bf16)
    normed_two_pieces = gather_chunks(normed_two_chunk)
    gate_up = [
        gate_up_half,
        gate_up_near,
        pair_swap(gate_up_half, "c"),
        pair_swap(gate_up_near, "c"),
    ]
    down_near = pair_swap(after(down_half, gate_up_near), "near")
    down = [down_half, down_near, pair_swap(down_half, "c"), pair_swap(down_near, "c")]

    outs = kernel_call(
        ffn_kernel,
        normed_two_pieces + cotangents + gate_up + down,
        [shaped((tokens, units), bf16)] * 2
        + [shaped((tokens, 2 * units), bf16)] * 2
        + [shaped((chunk_rows, width), bf16)] * 8
        + [shaped((2 * chunk_rows, width), bf16)] * 4
        + [shaped((tokens, width), bf16)] * 2,
        [pltpu.VMEM((2, tokens, width), f32)],
        None,
        24 * tokens * width * units,
    )
    hidden_acts, grad_ffn, two_parts, down_parts = outs[:2], outs[2:4], outs[4:12], outs[12:16]
    normed_two, all_cotangent = outs[16:]
    away, own = sum_sends(two_parts)
    two_far = pair_swap(sum_pieces(away).astype(bf16), "far")
    two_away = own, two_far
    gate_up_both = core_sum(*(contract_first(normed_two, g).astype(bf16) for g in grad_ffn))
    down_both = core_sum(*(contract_first(all_cotangent, act).astype(bf16) for act in hidden_acts))

    (own, two_far), down_both, gate_up_both = after((two_away, down_both, gate_up_both))
    grad_normed_two = sum_pieces(own + [two_far])

    def whole_block(chunk):
        chunk = from_own_first(chunk, odd_near)
        by_y = jnp.stack([chunk, pair_swap(chunk, "y")])
        by_core = jnp.stack([by_y, pair_swap(by_y, "c")], axis=1)
        return flip_if(flip_if(by_core, 1, c == 1), 0, y == 1).reshape(block_rows, width)

    grad_middle = cotangent.astype(f32) + norm_back(grad_normed_two, middle, inv_two, gain_two)
    grad_branch = grad_middle.astype(bf16)
    branch_pieces = gather_chunks(grad_branch)
    down_parts = after(down_parts, branch_pieces)
    down_pieces = [down_parts[0]] + [side_swap(down_parts[i], i) for i in range(1, 4)]
    half = width // 2
    gate_up_got = pair_swap(gate_up_both[half:], "near")
    down_got = pair_swap(down_both[half:], "near")

    all_branch, grad_gate, grad_query, grad_pairs, query_gain_part = kernel_call(
        attend_back_kernel,
        branch_pieces
        + og
        + pairs
        + [bounds, key_ids, query_rot, query_pre, gate_pre, attended, log_total]
        + [cosine, sine, query_gain],
        [
            shaped((tokens, width), bf16),
            shaped((2, tokens, low), bf16),
            shaped((2, tokens, low), bf16),
            shaped((4 * tokens, 2 * low), bf16),
            shaped((1, low), f32),
        ],
        [
            pltpu.VMEM((2, tokens, low), f32),
            pltpu.VMEM((4 * tokens, low), f32),
            pltpu.VMEM((4 * tokens, low), f32),
        ],
        None,
        20 * tokens * 4 * tokens * low,
    )
    pair_other = pair_swap(grad_pairs[2 * tokens :], "c")
    gate_up_got, down_got, down_pieces, normed_later = after(
        (gate_up_got, down_got, down_pieces, normed), grad_pairs
    )
    near_pairs = grad_pairs[: 2 * tokens].astype(f32) + pair_other.astype(f32)
    near_pairs = near_pairs.astype(bf16)
    pair_got = pair_swap(near_pairs[tokens:], "near")
    gate_up_rows = near_add(gate_up_both, gate_up_got)
    down_got, gate_up_rows = after((down_got, gate_up_rows))
    down_rows = near_add(down_both, down_got)
    gate_up_grad = to_row_owners(gate_up_rows)
    down_grad = to_row_owners(after(down_rows, gate_up_grad))
    down_sums = sum_pieces(down_pieces)
    down_far = pair_swap(down_sums[chunk_rows:].astype(bf16), "far")
    og_both = core_sum(
        *(
            jnp.concatenate(
                [
                    contract_first(normed_later, grad_gate[i]).astype(bf16),
                    contract_first(all_branch, gated[i]).astype(bf16),
                ],
                axis=1,
            )
            for i in range(2)
        )
    )
    key_pre, gate_up_rows, down_rows, down_sums = after(
        (key_pre, gate_up_rows, down_rows, down_sums)
    )
    og_got = pair_swap(after(og_both, pair_got)[half:], "near")
    outs = kernel_call(
        input_kernel,
        [near_pairs[:tokens], pair_got, key_pre, cosine, sine, key_gain]
        + [grad_query, grad_gate, normed]
        + qk
        + og,
        [shaped((tokens, 2 * low), bf16)] * 2
        + [shaped((chunk_rows, width), bf16)] * 8
        + [shaped((1, low), f32), shaped((1, width), f32)],
        [pltpu.VMEM((tokens, width), f32)],
        core_flag,
        12 * tokens * width * low,
    )
    grad_qk, normed_parts, key_gain_part, input_gain_part = outs[:2], outs[2:10], outs[10], outs[11]
    away, own = sum_sends(normed_parts)
    away = sum_pieces(away).astype(bf16)
    qk_sides = [contract_first(normed, g).astype(bf16) for g in after(grad_qk, normed_parts[1])]
    qk_other = pair_swap(qk_sides[1], "c")
    away, qk_other, gate_up_grad = after((away, qk_other, gate_up_grad))
    qk_both = (qk_sides[0].astype(f32) + qk_other.astype(f32)).astype(bf16)
    qk_got = pair_swap(qk_both[half:], "near")
    grad_far = pair_swap(away, "far")
    grad_normed = sum_pieces(own + [grad_far])
    inv_one = lax.rsqrt(jnp.mean(hidden32 * hidden32, axis=1, keepdims=True) + epsilon)
    input_chunk = (grad_middle + norm_back(grad_normed, hidden32, inv_one, gain_one)).astype(bf16)
    input_grad = whole_block(input_chunk)
    og_got, down_far, down_grad, gain_parts = after(
        (og_got, down_far, down_grad, (input_gain_part, query_gain_part, key_gain_part)), grad_far
    )
    attn_rows = jnp.concatenate([near_add(qk_both, qk_got), near_add(og_both, og_got)], axis=1)
    attn_grad = from_head_owners(attn_rows, far, x, c)
    qk_grad, og_grad = attn_grad[..., : 2 * low], attn_grad[..., 2 * low :]
    layer_out = whole_block((middle + down_sums[:chunk_rows] + down_far.astype(f32)).astype(bf16))
    gains = jnp.concatenate(
        [
            from_own_first(gain_parts[0][0] / gain_one, odd_near),
            from_own_first(jnp.sum(grad_normed_two * middle * inv_two, axis=0), odd_near),
            gain_parts[1][0],
            gain_parts[2][0],
        ]
    )
    gains = (gains + plane_swap(gains, 1)) + (plane_swap(gains, 2) + plane_swap(gains, 3))
    for axis in ("near", "y", "c"):
        gains = gains + pair_swap(gains, axis)

    def per_head(grad, start):
        columns = [grad[i, j, :, start : start + low] for i in range(2) for j in range(2)]
        return jnp.concatenate(columns, axis=1).astype(f32)

    def per_group(grad, j):
        return jnp.concatenate([grad[0, j, :, low:], grad[1, j, :, low:]], axis=1).astype(f32)

    def flat(grad):
        return jnp.concatenate([grad[p] for p in range(PLANES)], axis=1).astype(f32)

    return (
        layer_out,
        input_grad,
        per_head(qk_grad, 0),
        per_group(qk_grad, 0),
        per_group(qk_grad, 1),
        per_head(og_grad, 0),
        per_head(og_grad, low),
        flat(gate_up_grad[:, :, :units]),
        flat(gate_up_grad[:, :, units:]),
        flat(down_grad),
        gains[:width],
        gains[width : 2 * width],
        gains[2 * width : 2 * width + low],
        gains[2 * width + low :],
    )


def solution(mesh):
    wide, head = mesh.shape["wide"], mesh.shape["head"]
    if wide == 2 * PLANES and head == 4:
        devices = mesh.devices.reshape(2, 2, 2, 2, 2)
        mesh = Mesh(devices, ("far", "near", "x", "y", "c"))
        program, rows, columns = on_slice_device, ("far", "near", "x"), ("y", "c")
    else:
        program, rows, columns = on_device, "wide", "head"
    tokens, weight = P(rows, None), P(rows, columns)
    return jax.shard_map(
        program,
        mesh=mesh,
        in_specs=(tokens, tokens, P()) + (weight,) * 8 + (P(),) * 4,
        out_specs=(tokens, tokens) + (weight,) * 8 + (P(),) * 4,
        check_vma=False,
    )
```

```python
import jax
import jax.numpy as jnp
from jax import lax
from jax.experimental import pallas as pl
from jax.experimental.pallas import tpu as pltpu
from jax.sharding import Mesh
from jax.sharding import PartitionSpec as P

HEAD_WIDTH = 128


epsilon = 1e-06
rope_base = 1000000.0
masked_score = -1e30


def segment_of(lengths, token_ids):
    doc_ends = jnp.cumsum(lengths)
    return jnp.sum((token_ids[:, None] >= doc_ends[None, :]).astype(jnp.int32), axis=1)


def doc_tables(lengths, token_ids):
    doc_ends = jnp.cumsum(lengths)
    starts = doc_ends - lengths
    segment = segment_of(lengths, token_ids)
    labels = jnp.arange(lengths.shape[0], dtype=jnp.int32)
    doc_begin = jnp.sum(jnp.where(segment[:, None] == labels[None, :], starts[None, :], 0), axis=1)
    return (segment, token_ids - doc_begin)


def rope_tables(positions, head_size):
    half_size = head_size // 2
    frequency = rope_base ** (-2.0 * jnp.arange(half_size, dtype=jnp.float32) / head_size)
    angles = positions.astype(jnp.float32)[:, None] * frequency[None, :]
    cosine = jnp.cos(angles)
    sine_table = jnp.sin(angles)
    return (
        jnp.concatenate([cosine, cosine], axis=1),
        jnp.concatenate([sine_table, sine_table], axis=1),
    )


def rotate_half(values):
    half_size = values.shape[-1] // 2
    return jnp.concatenate([-values[..., half_size:], values[..., :half_size]], axis=-1)


def rotate_back(values):
    half_size = values.shape[-1] // 2
    return jnp.concatenate([values[..., half_size:], -values[..., :half_size]], axis=-1)


def apply_rope(values, cos_table, sin_table):
    return values * cos_table[:, None, :] + rotate_half(values) * sin_table[:, None, :]


def rope_back(grads, cos_table, sin_table):
    return grads * cos_table[:, None, :] + rotate_back(grads * sin_table[:, None, :])


def contract_last(left, right):
    return lax.dot_general(
        left, right, (((1,), (1,)), ((), ())), preferred_element_type=jnp.float32
    )


def contract_first(left, right):
    return lax.dot_general(
        left, right, (((0,), (0,)), ((), ())), preferred_element_type=jnp.float32
    )


def norm_back(grad_out, inputs, inv_root, gain):
    scaled = grad_out * gain
    return inv_root * scaled - inputs * inv_root**3 * jnp.mean(
        scaled * inputs, axis=-1, keepdims=True
    )


def on_device(
    hidden_in,
    out_cotangent,
    doc_lengths,
    query_weight,
    key_matrix,
    value_matrix,
    gate_weight,
    out_weight,
    ffn_gate_weight,
    ffn_up_weight,
    ffn_down_weight,
    attn_gain,
    ffn_gain,
    query_gain,
    key_gain,
):
    tok_rows = hidden_in.shape[0]
    row_length = tok_rows * lax.axis_size("wide")
    first_row = lax.axis_index("wide") * tok_rows
    token_ids = first_row + jnp.arange(tok_rows, dtype=jnp.int32)
    segment, positions = doc_tables(doc_lengths, token_ids)
    shard_begin = first_row - positions[0]
    shard_last = first_row + tok_rows - 1
    cos_table, sin_table = rope_tables(positions, HEAD_WIDTH)
    local_heads = query_weight.shape[1] // HEAD_WIDTH
    kv_heads = key_matrix.shape[1] // HEAD_WIDTH
    group_width = local_heads // kv_heads
    query_rows = group_width * tok_rows
    score_scale = HEAD_WIDTH ** (-0.5)
    (
        full_query,
        full_key,
        full_value,
        full_gate,
        full_out,
        full_ffn_gate,
        full_ffn_up,
        full_ffn_down,
    ) = (
        lax.all_gather(query_weight, "wide", axis=0, tiled=True),
        lax.all_gather(key_matrix, "wide", axis=0, tiled=True),
        lax.all_gather(value_matrix, "wide", axis=0, tiled=True),
        lax.all_gather(gate_weight, "wide", axis=0, tiled=True),
        lax.all_gather(out_weight, "wide", axis=0, tiled=True),
        lax.all_gather(ffn_gate_weight, "wide", axis=0, tiled=True),
        lax.all_gather(ffn_up_weight, "wide", axis=0, tiled=True),
        lax.all_gather(ffn_down_weight, "wide", axis=0, tiled=True),
    )
    hidden32 = hidden_in.astype(jnp.float32)
    inv_one = lax.rsqrt(jnp.mean(hidden32 * hidden32, axis=1, keepdims=True) + epsilon)
    normed_input = (hidden32 * inv_one * attn_gain).astype(jnp.bfloat16)
    query_pre = jnp.dot(normed_input, full_query, preferred_element_type=jnp.float32).reshape(
        tok_rows, local_heads, HEAD_WIDTH
    )
    key_before_norm = jnp.dot(normed_input, full_key, preferred_element_type=jnp.float32).reshape(
        tok_rows, kv_heads, HEAD_WIDTH
    )
    value_rows = jnp.dot(normed_input, full_value, preferred_element_type=jnp.float32).astype(
        jnp.bfloat16
    )
    gate_pre = jnp.dot(normed_input, full_gate, preferred_element_type=jnp.float32)
    inv_query = lax.rsqrt(jnp.mean(query_pre * query_pre, axis=-1, keepdims=True) + epsilon)
    inv_key = lax.rsqrt(
        jnp.mean(key_before_norm * key_before_norm, axis=-1, keepdims=True) + epsilon
    )
    query_unit = query_pre * inv_query
    key_unit = key_before_norm * inv_key
    query_rot = apply_rope(query_unit * query_gain, cos_table, sin_table).astype(jnp.bfloat16)
    key_rows = (
        apply_rope(key_unit * key_gain, cos_table, sin_table)
        .astype(jnp.bfloat16)
        .reshape(tok_rows, kv_heads * HEAD_WIDTH)
    )
    query_heads = (
        query_rot.reshape(tok_rows, kv_heads, group_width, HEAD_WIDTH)
        .transpose(1, 2, 0, 3)
        .reshape(kv_heads, query_rows, HEAD_WIDTH)
    )
    query_seg = jnp.tile(segment, group_width)
    query_ids = jnp.tile(token_ids, group_width)
    start_state = (
        jnp.full((kv_heads, query_rows), masked_score, jnp.float32),
        jnp.zeros((kv_heads, query_rows), jnp.float32),
        jnp.zeros((kv_heads, query_rows, HEAD_WIDTH), jnp.float32),
    )
    key_piece = lax.all_gather(key_rows, "wide", axis=0, tiled=True)
    value_piece = lax.all_gather(value_rows, "wide", axis=0, tiled=True)
    count = key_piece.shape[0]
    step_rows = 512
    steps_count = count // step_rows
    key_ids = jnp.arange(count, dtype=jnp.int32)
    key_seg = segment_of(doc_lengths, key_ids)
    key_blocks = key_piece.reshape(steps_count, step_rows, kv_heads, HEAD_WIDTH).transpose(
        0, 2, 1, 3
    )
    value_blocks = value_piece.reshape(steps_count, step_rows, kv_heads, HEAD_WIDTH).transpose(
        0, 2, 1, 3
    )

    def inner(state, block):
        key_block, value_block, block_seg, block_ids = block

        def inner_work(state_in):
            scores = (
                jnp.einsum(
                    "hqd,hkd->hqk", query_heads, key_block, preferred_element_type=jnp.float32
                )
                * score_scale
            )
            allowed = (
                (query_seg[:, None] == block_seg[None, :])
                & (block_ids[None, :] <= query_ids[:, None])
            )[None]
            scores = jnp.where(allowed, scores, masked_score)
            running, total, accum = state_in
            newest = jnp.maximum(running, jnp.max(scores, axis=-1))
            factor = jnp.exp(running - newest)
            weights = jnp.where(allowed, jnp.exp(scores - newest[..., None]), 0.0)
            total = total * factor + jnp.sum(weights, axis=-1)
            accum = accum * factor[..., None] + jnp.einsum(
                "hqk,hkd->hqd",
                weights.astype(jnp.bfloat16),
                value_block,
                preferred_element_type=jnp.float32,
            )
            return (newest, total, accum)

        useful = (block_ids[0] <= shard_last) & (block_ids[step_rows - 1] >= shard_begin)
        return (lax.cond(useful, inner_work, lambda state_in: state_in, state), None)

    state, unused = lax.scan(
        inner,
        start_state,
        (
            key_blocks,
            value_blocks,
            key_seg.reshape(steps_count, step_rows),
            key_ids.reshape(steps_count, step_rows),
        ),
    )
    running, total, accum = state
    attended_heads = accum / total[..., None]
    log_total = running + jnp.log(total)
    attended = (
        attended_heads.reshape(kv_heads, group_width, tok_rows, HEAD_WIDTH)
        .transpose(2, 0, 1, 3)
        .reshape(tok_rows, local_heads * HEAD_WIDTH)
    )
    gate_sig = jax.nn.sigmoid(gate_pre)
    gated = (attended * gate_sig).astype(jnp.bfloat16)
    branch = lax.psum(contract_last(gated, full_out).astype(jnp.bfloat16), "head").astype(
        jnp.float32
    )
    middle = hidden32 + branch
    inv_two = lax.rsqrt(jnp.mean(middle * middle, axis=1, keepdims=True) + epsilon)
    normed_two = (middle * inv_two * ffn_gain).astype(jnp.bfloat16)
    ffn_gate_pre = jnp.dot(normed_two, full_ffn_gate, preferred_element_type=jnp.float32)
    ffn_up_pre = jnp.dot(normed_two, full_ffn_up, preferred_element_type=jnp.float32)
    gate_act = jax.nn.sigmoid(ffn_gate_pre)
    silu_gate = ffn_gate_pre * gate_act
    hidden_act = (silu_gate * ffn_up_pre).astype(jnp.bfloat16)
    ffn_out = lax.psum(
        contract_last(hidden_act, full_ffn_down).astype(jnp.bfloat16), "head"
    ).astype(jnp.float32)
    layer_out = (middle + ffn_out).astype(jnp.bfloat16)
    grad32 = out_cotangent.astype(jnp.float32)
    grad_hidden = jnp.dot(out_cotangent, full_ffn_down, preferred_element_type=jnp.float32)
    grad_ffn_gate = (
        grad_hidden * ffn_up_pre * gate_act * (1.0 + ffn_gate_pre * (1.0 - gate_act))
    ).astype(jnp.bfloat16)
    grad_ffn_up = (grad_hidden * silu_gate).astype(jnp.bfloat16)
    grad_normed_two = lax.psum(
        (
            contract_last(grad_ffn_gate, full_ffn_gate) + contract_last(grad_ffn_up, full_ffn_up)
        ).astype(jnp.bfloat16),
        "head",
    ).astype(jnp.float32)
    grad_middle = grad32 + norm_back(grad_normed_two, middle, inv_two, ffn_gain)
    grad_branch = grad_middle.astype(jnp.bfloat16)
    grad_gated = jnp.dot(grad_branch, full_out, preferred_element_type=jnp.float32)
    grad_attended = (grad_gated * gate_sig).astype(jnp.bfloat16)
    grad_gate_pre = (grad_gated * attended * gate_sig * (1.0 - gate_sig)).astype(jnp.bfloat16)
    grad_heads = (
        grad_attended.reshape(tok_rows, kv_heads, group_width, HEAD_WIDTH)
        .transpose(1, 2, 0, 3)
        .reshape(kv_heads, query_rows, HEAD_WIDTH)
    )
    delta = jnp.sum(grad_heads.astype(jnp.float32) * attended_heads, axis=-1)
    all_keys, all_values = key_piece, value_piece
    key_step = 512
    key_count = row_length // key_step
    all_ids = jnp.arange(row_length, dtype=jnp.int32)
    all_seg = segment_of(doc_lengths, all_ids)
    key_blocks = all_keys.reshape(key_count, key_step, kv_heads, HEAD_WIDTH).transpose(0, 2, 1, 3)
    value_blocks = all_values.reshape(key_count, key_step, kv_heads, HEAD_WIDTH).transpose(
        0, 2, 1, 3
    )
    key_scan_items = (
        key_blocks,
        value_blocks,
        all_seg.reshape(key_count, key_step),
        all_ids.reshape(key_count, key_step),
    )
    zero_query = jnp.zeros((kv_heads, query_rows, HEAD_WIDTH), jnp.float32)

    def block_terms(key_block, value_block, block_seg, block_ids):
        scores = (
            jnp.einsum("hqd,hkd->hqk", query_heads, key_block, preferred_element_type=jnp.float32)
            * score_scale
        )
        allowed = (
            (query_seg[:, None] == block_seg[None, :]) & (block_ids[None, :] <= query_ids[:, None])
        )[None]
        weights = jnp.where(
            allowed, jnp.exp(jnp.where(allowed, scores, masked_score) - log_total[..., None]), 0.0
        )
        grad_weights = jnp.einsum(
            "hqd,hkd->hqk", grad_heads, value_block, preferred_element_type=jnp.float32
        )
        grad_scores = (weights * (grad_weights - delta[..., None])).astype(jnp.bfloat16)
        return (weights, grad_scores)

    def block_useful(block_ids):
        return (block_ids[0] <= shard_last) & (block_ids[key_step - 1] >= shard_begin)

    def back_block(grad_query, block):
        key_block, value_block, block_seg, block_ids = block

        def back_work(grad_in):
            weights, grad_scores = block_terms(key_block, value_block, block_seg, block_ids)
            grad_out = (
                grad_in
                + jnp.einsum(
                    "hqk,hkd->hqd", grad_scores, key_block, preferred_element_type=jnp.float32
                )
                * score_scale
            )
            grad_key = (
                jnp.einsum(
                    "hqk,hqd->hkd", grad_scores, query_heads, preferred_element_type=jnp.float32
                )
                * score_scale
            )
            grad_value = jnp.einsum(
                "hqk,hqd->hkd",
                weights.astype(jnp.bfloat16),
                grad_heads,
                preferred_element_type=jnp.float32,
            )
            return (grad_out, (grad_key, grad_value))

        def skip(grad_in):
            nothing = jnp.zeros((kv_heads, key_step, HEAD_WIDTH), jnp.float32)
            return (grad_in, (nothing, nothing))

        return lax.cond(block_useful(block_ids), back_work, skip, grad_query)

    grad_query, (key_parts, value_parts) = lax.scan(back_block, zero_query, key_scan_items)
    key_grad_rows = key_parts.transpose(0, 2, 1, 3).reshape(row_length, kv_heads * HEAD_WIDTH)
    value_grad_rows = value_parts.transpose(0, 2, 1, 3).reshape(row_length, kv_heads * HEAD_WIDTH)
    key_total, value_total = (
        lax.psum_scatter(
            key_grad_rows.astype(jnp.bfloat16), "wide", scatter_dimension=0, tiled=True
        ).astype(jnp.float32),
        lax.psum_scatter(
            value_grad_rows.astype(jnp.bfloat16), "wide", scatter_dimension=0, tiled=True
        ).astype(jnp.float32),
    )
    grad_values = value_total.astype(jnp.bfloat16)
    grad_key_rot = (
        key_total.astype(jnp.bfloat16).astype(jnp.float32).reshape(tok_rows, kv_heads, HEAD_WIDTH)
    )
    grad_query_rot = (
        grad_query.astype(jnp.bfloat16)
        .astype(jnp.float32)
        .reshape(kv_heads, group_width, tok_rows, HEAD_WIDTH)
        .transpose(2, 0, 1, 3)
        .reshape(tok_rows, local_heads, HEAD_WIDTH)
    )
    grad_query_unit = rope_back(grad_query_rot, cos_table, sin_table)
    grad_key_unit = rope_back(grad_key_rot, cos_table, sin_table)
    query_gain_part = jnp.sum(grad_query_unit * query_unit, axis=(0, 1))
    key_gain_part = jnp.sum(grad_key_unit * key_unit, axis=(0, 1))
    grad_query_pre = (
        norm_back(grad_query_unit, query_pre, inv_query, query_gain)
        .reshape(tok_rows, local_heads * HEAD_WIDTH)
        .astype(jnp.bfloat16)
    )
    grad_key_pre = (
        norm_back(grad_key_unit, key_before_norm, inv_key, key_gain)
        .reshape(tok_rows, kv_heads * HEAD_WIDTH)
        .astype(jnp.bfloat16)
    )
    grad_normed_part = (
        contract_last(grad_query_pre, full_query)
        + contract_last(grad_key_pre, full_key)
        + contract_last(grad_values, full_value)
        + contract_last(grad_gate_pre, full_gate)
    )
    grad_normed = lax.psum(grad_normed_part.astype(jnp.bfloat16), "head").astype(jnp.float32)
    input_grad = (grad_middle + norm_back(grad_normed, hidden32, inv_one, attn_gain)).astype(
        jnp.bfloat16
    )
    attn_gain_part = jnp.sum(grad_normed * hidden32 * inv_one, axis=0)
    ffn_gain_part = jnp.sum(grad_normed_two * middle * inv_two, axis=0)
    weight_grads = lax.psum_scatter(
        jnp.concatenate(
            [
                contract_first(normed_input, grad_query_pre),
                contract_first(normed_input, grad_key_pre),
                contract_first(normed_input, grad_values),
                contract_first(normed_input, grad_gate_pre),
                contract_first(grad_branch, gated),
                contract_first(normed_two, grad_ffn_gate),
                contract_first(normed_two, grad_ffn_up),
                contract_first(out_cotangent, hidden_act),
            ],
            axis=1,
        ).astype(jnp.bfloat16),
        "wide",
        scatter_dimension=0,
        tiled=True,
    ).astype(jnp.float32)
    col_widths = [
        query_weight.shape[1],
        key_matrix.shape[1],
        value_matrix.shape[1],
        gate_weight.shape[1],
        out_weight.shape[1],
        ffn_gate_weight.shape[1],
        ffn_up_weight.shape[1],
        ffn_down_weight.shape[1],
    ]
    pieces = []
    offset = 0
    for width in col_widths:
        pieces.append(weight_grads[:, offset : offset + width])
        offset = offset + width
    head_first = (lax.axis_index("head") == 0).astype(jnp.float32)
    attn_gain_grad, ffn_gain_grad, query_gain_grad, key_gain_grad = lax.psum(
        (attn_gain_part * head_first, ffn_gain_part * head_first, query_gain_part, key_gain_part),
        ("wide", "head"),
    )
    return (
        layer_out,
        input_grad,
        pieces[0],
        pieces[1],
        pieces[2],
        pieces[3],
        pieces[4],
        pieces[5],
        pieces[6],
        pieces[7],
        attn_gain_grad,
        ffn_gain_grad,
        query_gain_grad,
        key_gain_grad,
    )


PLANES = 4
PLANE = ("far", "x")


def pair_swap(values, axis):
    return lax.ppermute(values, axis, [(0, 1), (1, 0)])


def plane_swap(values, step):
    return lax.ppermute(values, PLANE, [(i, i ^ step) for i in range(PLANES)])


def side_swap(values, step):
    return lax.ppermute(values, ("x", "y"), [(i, i ^ step) for i in range(4)])


def after(values, *done):
    return lax.optimization_barrier((values, done))[0]


def gather_chunks(chunk):
    far = pair_swap(chunk, "far")
    near = [side_swap(chunk, step) for step in range(1, 4)]
    away = [side_swap(far, step) for step in range(1, 4)]
    pieces = [chunk, far]
    for pair in zip(near, away):
        pieces.extend(pair)
    return pieces


def sum_sends(parts):
    return [
        [parts[far]] + [side_swap(parts[2 * step + far], step) for step in range(1, 4)]
        for far in (1, 0)
    ]


def sum_pieces(pieces):
    total = pieces[0].astype(jnp.float32)
    for piece in pieces[1:]:
        total = total + piece.astype(jnp.float32)
    return total


def flip_if(values, axis, flag):
    return jnp.where(flag, jnp.flip(values, axis), values)


def to_own_first(values, flag):
    lead = values.shape[:-1]
    width = values.shape[-1]
    split = values.reshape(lead + (2, 2, width // 4))
    zero = split[..., 0, :].reshape(lead + (width // 2,))
    one = split[..., 1, :].reshape(lead + (width // 2,))
    return jnp.concatenate([jnp.where(flag, one, zero), jnp.where(flag, zero, one)], axis=-1)


def from_own_first(values, flag):
    lead = values.shape[:-1]
    width = values.shape[-1]
    own = values[..., : width // 2].reshape(lead + (2, width // 4))
    other = values[..., width // 2 :].reshape(lead + (2, width // 4))
    pair = jnp.stack([jnp.where(flag, other, own), jnp.where(flag, own, other)], axis=-2)
    return pair.reshape(lead + (width,))


def to_plane_owners(local):
    planes, rows, width = local.shape
    return lax.all_to_all(
        local.reshape(planes * rows, width), PLANE, split_axis=0, concat_axis=0, tiled=True
    )


HEADS = ("far", "x", "c")


def head_pairs(a, b, back):
    pairs = []
    for f in range(2):
        for x in range(2):
            for c in range(2):
                pairs.append((4 * f + 2 * x + c, 4 * c + 2 * (x ^ a) + (f ^ b)))
    return [(j, i) for i, j in pairs] if back else pairs


def to_head_owners(columns, far, x, c):
    turned = flip_if(flip_if(columns, 0, x == 1), 1, far == 1)
    sent = [
        [lax.ppermute(turned[a, b], HEADS, head_pairs(a, b, False)) for a in range(2)]
        for b in range(2)
    ]
    pieces = jnp.stack([jnp.stack(row) for row in sent])
    rows = flip_if(flip_if(pieces, 0, c == 1), 1, x == 1)
    return rows.reshape(PLANES * columns.shape[2], columns.shape[3]), sent


def from_head_owners(rows, far, x, c):
    blocks = rows.reshape(2, 2, rows.shape[0] // PLANES, rows.shape[1])
    blocks = flip_if(flip_if(blocks, 0, c == 1), 1, x == 1)
    pieces = jnp.stack(
        [
            jnp.stack(
                [lax.ppermute(blocks[b, a], HEADS, head_pairs(a, b, True)) for b in range(2)]
            )
            for a in range(2)
        ]
    )
    return flip_if(flip_if(pieces, 0, x == 1), 1, far == 1)


def core_sum(mine, other):
    both = mine.astype(jnp.float32) + pair_swap(other, "c").astype(jnp.float32)
    return both.astype(jnp.bfloat16)


def near_add(both, got):
    half = both.shape[0] // 2
    return (both[:half].astype(jnp.float32) + got.astype(jnp.float32)).astype(jnp.bfloat16)


def to_row_owners(rows):
    back = lax.all_to_all(rows, PLANE, split_axis=0, concat_axis=0, tiled=True)
    return back.reshape(PLANES, rows.shape[0] // PLANES, rows.shape[1])


VMEM_BYTES = 56 * 1024 * 1024


def kernel_call(body, operands, outs, scratch=(), flags=None, flops=0):
    specs = [pl.BlockSpec(memory_space=pltpu.VMEM)] * len(operands)
    if flags is not None:
        operands = [flags] + list(operands)
        specs = [pl.BlockSpec(memory_space=pltpu.SMEM)] + specs
    moved = sum(v.size * v.dtype.itemsize for v in operands)
    moved += sum(v.size * v.dtype.itemsize for v in outs)
    return pl.pallas_call(
        body,
        out_shape=outs,
        in_specs=specs,
        out_specs=[pl.BlockSpec(memory_space=pltpu.VMEM)] * len(outs),
        scratch_shapes=list(scratch),
        compiler_params=pltpu.CompilerParams(vmem_limit_bytes=VMEM_BYTES),
        cost_estimate=pl.CostEstimate(flops=flops, bytes_accessed=moved, transcendentals=0),
    )(*operands)


def shaped(shape, dtype):
    return jax.ShapeDtypeStruct(shape, dtype)


def dot_nn(left, right):
    return jnp.dot(left, right, preferred_element_type=jnp.float32)


def turned(values, cosine, signed_sine):
    return values * cosine + pltpu.roll(values, HEAD_WIDTH // 2, 1) * signed_sine


def turned_back(grads, cosine, signed_sine):
    return grads * cosine - pltpu.roll(grads, HEAD_WIDTH // 2, 1) * signed_sine


def sigmoid(values):
    return 1.0 / (1.0 + jnp.exp(-values))


def project_kernel(flag, *refs):
    hidden = refs[:8]
    gain, mine_own, mine_near, other_own, other_near, cosine, sine, qgain, kgain = refs[8:17]
    normed, pair, query_rot, query_pre, key_pre, scratch = refs[17:]
    rows = hidden[0].shape[0]
    for i in range(8):
        h = hidden[i][...].astype(jnp.float32)
        inverse = lax.rsqrt(jnp.mean(h * h, axis=1, keepdims=True) + epsilon)
        normed[i * rows : (i + 1) * rows, :] = (h * inverse * gain[...]).astype(jnp.bfloat16)
    half = normed.shape[1] // 2
    left, right = normed[:, :half], normed[:, half:]
    for i, (own, near) in enumerate(((mine_own, mine_near), (other_own, other_near))):
        scratch[i] = dot_nn(left, own[...]) + dot_nn(right, near[...])
    cos, sin = cosine[...], sine[...]
    swapped = flag[0] == 1
    mine, other = scratch[0, :, HEAD_WIDTH:], scratch[1, :, HEAD_WIDTH:]
    pre = jnp.where(swapped, other, mine)
    key_pre[...] = pre
    pair[:, HEAD_WIDTH:] = jnp.where(swapped, mine, other).astype(jnp.bfloat16)
    unit = pre * lax.rsqrt(jnp.mean(pre * pre, axis=1, keepdims=True) + epsilon)
    pair[:, :HEAD_WIDTH] = turned(unit * kgain[...], cos, sin).astype(jnp.bfloat16)
    for i in range(2):
        pre = scratch[i, :, :HEAD_WIDTH]
        query_pre[i] = pre
        unit = pre * lax.rsqrt(jnp.mean(pre * pre, axis=1, keepdims=True) + epsilon)
        query_rot[i] = turned(unit * qgain[...], cos, sin).astype(jnp.bfloat16)


def attend_kernel(query_rot, first, second, third, fourth, bounds, key_ids, gate_pre, *refs):
    outs_w, gated, attended, log_total, parts, total = refs[:4], *refs[4:7], refs[7:15], refs[15]
    scale = HEAD_WIDTH ** (-0.5)
    pairs = (first, second, third, fourth)
    rows = first.shape[0]
    tile = rows // 2

    def step(i, carry):
        head, at = i // 2, pl.multiple_of(i % 2 * tile, tile)
        query = query_rot[head, pl.ds(at, tile), :]
        start, last = bounds[pl.ds(at, tile), 0:1], bounds[pl.ds(at, tile), 1:2]
        scores = []
        for j, pair in enumerate(pairs):
            ids = key_ids[:, j * rows : (j + 1) * rows]
            allowed = (ids >= start) & (ids <= last)
            score = contract_last(query, pair[:, :HEAD_WIDTH]) * scale
            scores.append(jnp.where(allowed, score, masked_score))
        top = jnp.max(scores[0], axis=1, keepdims=True)
        for score in scores[1:]:
            top = jnp.maximum(top, jnp.max(score, axis=1, keepdims=True))
        total = jnp.zeros_like(top)
        result = jnp.zeros((tile, HEAD_WIDTH), jnp.float32)
        for score, pair in zip(scores, pairs):
            raised = jnp.exp(score - top)
            total = total + jnp.sum(raised, axis=1, keepdims=True)
            result = result + dot_nn(raised.astype(jnp.bfloat16), pair[:, HEAD_WIDTH:])
        result = result / total
        attended[head, pl.ds(at, tile), :] = result
        log_total[head, pl.ds(at, tile), :] = jnp.broadcast_to(top + jnp.log(total), result.shape)
        gate = sigmoid(gate_pre[head, pl.ds(at, tile), :])
        gated[head, pl.ds(at, tile), :] = (result * gate).astype(jnp.bfloat16)
        return carry

    lax.fori_loop(0, 4, step, 0)
    half = total.shape[1] // 2
    for near in range(2):
        total[:, near * half : (near + 1) * half] = contract_last(
            gated[0], outs_w[near][:, HEAD_WIDTH:]
        ) + contract_last(gated[1], outs_w[2 + near][:, HEAD_WIDTH:])
    rows = parts[0].shape[0]
    for i in range(8):
        parts[i][...] = total[i * rows : (i + 1) * rows, :].astype(jnp.bfloat16)


def ffn_kernel(*refs):
    chunks, cotangent, gate_up, down = refs[:8], refs[8:12], refs[12:16], refs[16:20]
    acts, grads, two_parts, down_parts = refs[20:22], refs[22:24], refs[24:32], refs[32:36]
    normed_two, cot, total = refs[36:]
    rows = chunks[0].shape[0]
    for i in range(8):
        normed_two[i * rows : (i + 1) * rows, :] = chunks[i][...]
    rows = cotangent[0].shape[0]
    for i in range(4):
        cot[i * rows : (i + 1) * rows, :] = cotangent[i][...]
    half = cot.shape[1] // 2
    units = down[0].shape[1]
    tile = cot.shape[0] // 2

    def step(i, carry):
        at = pl.multiple_of(i * tile, tile)
        rows_at = pl.ds(at, tile)
        for side in range(2):
            wide = [gate_up[2 * side][...], gate_up[2 * side + 1][...]]
            pre = dot_nn(normed_two[rows_at, :half], wide[0]) + dot_nn(
                normed_two[rows_at, half:], wide[1]
            )
            grad = dot_nn(cot[rows_at, :half], down[2 * side][...]) + dot_nn(
                cot[rows_at, half:], down[2 * side + 1][...]
            )
            gate, up = pre[:, :units], pre[:, units:]
            act = sigmoid(gate)
            silu = gate * act
            acts[side][rows_at, :] = (silu * up).astype(jnp.bfloat16)
            grads[side][rows_at, :units] = (
                grad * up * act * (1.0 + gate * (1.0 - act))
            ).astype(jnp.bfloat16)
            grads[side][rows_at, units:] = (grad * silu).astype(jnp.bfloat16)
        for near in range(2):
            total[0, rows_at, near * half : (near + 1) * half] = contract_last(
                grads[0][rows_at, :], gate_up[near][...]
            ) + contract_last(grads[1][rows_at, :], gate_up[2 + near][...])
            total[1, rows_at, near * half : (near + 1) * half] = contract_last(
                acts[0][rows_at, :], down[near][...]
            ) + contract_last(acts[1][rows_at, :], down[2 + near][...])
        return carry

    lax.fori_loop(0, 2, step, 0)
    rows = two_parts[0].shape[0]
    for i in range(8):
        two_parts[i][...] = total[0, i * rows : (i + 1) * rows, :].astype(jnp.bfloat16)
    rows = down_parts[0].shape[0]
    for i in range(4):
        down_parts[i][...] = total[1, i * rows : (i + 1) * rows, :].astype(jnp.bfloat16)


def attend_back_kernel(*refs):
    chunks, outs_w, pairs = refs[:8], refs[8:12], refs[12:16]
    bounds, key_ids, query_rot, query_pre, gate_pre, attended, log_total = refs[16:23]
    cosine, sine, qgain = refs[23:26]
    branch, grad_gate, grad_query, grad_pairs, gain_part = refs[26:31]
    gated_grad, keys_acc, vals_acc = refs[31:]
    scale = HEAD_WIDTH ** (-0.5)
    rows = chunks[0].shape[0]
    for i in range(8):
        branch[i * rows : (i + 1) * rows, :] = chunks[i][...]
    half = branch.shape[1] // 2
    for side in range(2):
        gated_grad[side] = dot_nn(branch[:, :half], outs_w[2 * side][:, HEAD_WIDTH:]) + dot_nn(
            branch[:, half:], outs_w[2 * side + 1][:, HEAD_WIDTH:]
        )
    keys_acc[...] = jnp.zeros_like(keys_acc)
    vals_acc[...] = jnp.zeros_like(vals_acc)
    gain_part[...] = jnp.zeros_like(gain_part)
    rows = pairs[0].shape[0]
    tile = rows // 2

    def step(i, carry):
        head, at = i // 2, pl.multiple_of(i % 2 * tile, tile)
        rows_at = pl.ds(at, tile)
        grad = gated_grad[head, rows_at, :]
        gate = sigmoid(gate_pre[head, rows_at, :])
        out = attended[head, rows_at, :]
        grad_gate[head, rows_at, :] = (grad * out * gate * (1.0 - gate)).astype(jnp.bfloat16)
        grad_out = (grad * gate).astype(jnp.bfloat16)
        delta = jnp.sum(grad_out.astype(jnp.float32) * out, axis=1, keepdims=True)
        query = query_rot[head, rows_at, :]
        start, last = bounds[rows_at, 0:1], bounds[rows_at, 1:2]
        log = log_total[head, rows_at, 0:1]
        grad_rot = jnp.zeros((tile, HEAD_WIDTH), jnp.float32)
        for j, pair in enumerate(pairs):
            ids = key_ids[:, j * rows : (j + 1) * rows]
            allowed = (ids >= start) & (ids <= last)
            keys, vals = pair[:, :HEAD_WIDTH], pair[:, HEAD_WIDTH:]
            score = jnp.where(allowed, contract_last(query, keys) * scale, masked_score)
            weight = jnp.exp(score - log)
            grad_score = (weight * (contract_last(grad_out, vals) - delta)).astype(jnp.bfloat16)
            grad_rot = grad_rot + dot_nn(grad_score, keys)
            at_keys = slice(j * rows, (j + 1) * rows)
            keys_acc[at_keys, :] += contract_first(grad_score, query)
            vals_acc[at_keys, :] += contract_first(weight.astype(jnp.bfloat16), grad_out)
        grad_rot = (grad_rot * scale).astype(jnp.bfloat16).astype(jnp.float32)
        grad_unit = turned_back(grad_rot, cosine[rows_at, :], sine[rows_at, :])
        pre = query_pre[head, rows_at, :]
        inverse = lax.rsqrt(jnp.mean(pre * pre, axis=1, keepdims=True) + epsilon)
        gain_part[...] += jnp.sum(grad_unit * (pre * inverse), axis=0, keepdims=True)
        grad_query[head, rows_at, :] = norm_back(grad_unit, pre, inverse, qgain[...]).astype(
            jnp.bfloat16
        )
        return carry

    lax.fori_loop(0, 4, step, 0)
    grad_pairs[:, :HEAD_WIDTH] = (keys_acc[...] * scale).astype(jnp.bfloat16)
    grad_pairs[:, HEAD_WIDTH:] = vals_acc[...].astype(jnp.bfloat16)


def tables_kernel(lengths, coords, frequency, bounds, key_ids, angles):
    far, near, x, y, c = (coords[i] for i in range(5))
    rows = bounds.shape[0] // 8

    def ids_of(at, near_at, c_at):
        chunk, row = at // rows, at % rows
        x_at, y_at, far_at = x ^ (chunk // 4), y ^ (chunk // 2 % 2), far ^ (chunk % 2)
        return (((far_at * 2 + near_at) * 2 + x_at) * 4 + y_at * 2 + c_at) * rows + row

    at = lax.broadcasted_iota(jnp.int32, bounds.shape, 0)
    lane = lax.broadcasted_iota(jnp.int32, bounds.shape, 1)
    ids = ids_of(at, near, c)
    start = jnp.zeros_like(ids)
    end = jnp.int32(0)
    for i in range(lengths.shape[0]):
        end = end + lengths[i]
        start = jnp.where(ids >= end, end, start)
    bounds[...] = jnp.where(lane == 0, start, ids)
    angles[...] = (ids - start).astype(jnp.float32) * frequency[...]
    at = lax.broadcasted_iota(jnp.int32, key_ids.shape, 1)
    group = at // (8 * rows)
    key_ids[...] = ids_of(at % (8 * rows), near ^ (group % 2), c ^ (group // 2))


def gate_kernel(normed, mine_own, mine_near, other_own, other_near, gate_pre):
    half = normed.shape[1] // 2
    for i, (own, near) in enumerate(((mine_own, mine_near), (other_own, other_near))):
        gate_pre[i] = dot_nn(normed[:, :half], own[:, :HEAD_WIDTH]) + dot_nn(
            normed[:, half:], near[:, :HEAD_WIDTH]
        )


def input_kernel(flag, *refs):
    own_pair, got_pair, key_pre, cosine, sine, kgain, grad_query, grad_gate, normed = refs[:9]
    qk, og = refs[9:13], refs[13:17]
    grad_qk, parts, key_gain, input_gain, total = refs[17:19], refs[19:27], refs[27], refs[28], refs[29]
    pair = own_pair[...].astype(jnp.float32) + got_pair[...].astype(jnp.float32)
    grad_unit = turned_back(
        pair[:, :HEAD_WIDTH].astype(jnp.bfloat16).astype(jnp.float32), cosine[...], sine[...]
    )
    pre = key_pre[...]
    inverse = lax.rsqrt(jnp.mean(pre * pre, axis=1, keepdims=True) + epsilon)
    key_gain[...] = jnp.sum(grad_unit * (pre * inverse), axis=0, keepdims=True)
    grad_key = norm_back(grad_unit, pre, inverse, kgain[...]).astype(jnp.bfloat16)
    grad_value = pair[:, HEAD_WIDTH:].astype(jnp.bfloat16)
    swapped = flag[0] == 1
    for side in range(2):
        grad_qk[side][:, :HEAD_WIDTH] = grad_query[side]
        first, second = (grad_key, grad_value) if side == 0 else (grad_value, grad_key)
        grad_qk[side][:, HEAD_WIDTH:] = jnp.where(swapped, second, first)
    half = total.shape[1] // 2
    tile = total.shape[0] // 2

    def step(i, carry):
        rows_at = pl.ds(pl.multiple_of(i * tile, tile), tile)
        for near in range(2):
            acc = None
            for side in range(2):
                part = contract_last(grad_qk[side][rows_at, :], qk[2 * side + near][...])
                part = part + contract_last(
                    grad_gate[side, rows_at, :], og[2 * side + near][:, :HEAD_WIDTH]
                )
                acc = part if acc is None else acc + part
            total[rows_at, near * half : (near + 1) * half] = acc
        return carry

    lax.fori_loop(0, 2, step, 0)
    rows = parts[0].shape[0]
    gain = jnp.zeros(input_gain.shape, jnp.float32)
    for i in range(8):
        part = total[i * rows : (i + 1) * rows, :]
        parts[i][...] = part.astype(jnp.bfloat16)
        gain = gain + jnp.sum(
            part * normed[i * rows : (i + 1) * rows, :].astype(jnp.float32), axis=0, keepdims=True
        )
    input_gain[...] = gain


def on_slice_device(
    hidden_in,
    out_cotangent,
    doc_lengths,
    query_weight,
    key_matrix,
    value_matrix,
    gate_weight,
    out_weight,
    ffn_gate_weight,
    ffn_up_weight,
    ffn_down_weight,
    attn_gain,
    ffn_gain,
    query_gain,
    key_gain,
):
    bf16, f32 = jnp.bfloat16, jnp.float32
    block_rows, width = hidden_in.shape
    chunk_rows = block_rows // 4
    tokens = 8 * chunk_rows
    low = HEAD_WIDTH
    units = ffn_gate_weight.shape[1] // PLANES
    coords = [lax.axis_index(name) for name in ("far", "near", "x", "y", "c")]
    far, near, x, y, c = coords
    odd_near = near == 1
    core_flag = c.reshape(1)

    def columns(x_at, head):
        at = (2 * x_at + head) * low
        third = (key_matrix if head == 0 else value_matrix)[:, x_at * low : (x_at + 1) * low]
        parts = (query_weight[:, at : at + low], third)
        parts += (gate_weight[:, at : at + low], out_weight[:, at : at + low])
        return jnp.concatenate(parts, axis=1)

    own_hidden = to_own_first(
        lax.dynamic_slice_in_dim(hidden_in, (y * 2 + c) * chunk_rows, chunk_rows, 0), odd_near
    )
    hidden = gather_chunks(own_hidden)
    attn_half, attn_sent = to_head_owners(
        jnp.stack([jnp.stack([columns(i, j) for j in range(2)]) for i in range(2)]), far, x, c
    )
    qk_half, og_half = attn_half[:, : 2 * low], attn_half[:, 2 * low :]
    qk_near = pair_swap(qk_half, "near")
    og_near = pair_swap(after(og_half, qk_near), "near")
    qk = [qk_half, qk_near, pair_swap(qk_half, "c"), pair_swap(after(qk_near, hidden), "c")]
    gain_one = to_own_first(attn_gain, odd_near)
    out_cotangent, ffn_gain = after((out_cotangent, ffn_gain), hidden[1])
    cotangent = to_own_first(
        lax.dynamic_slice_in_dim(out_cotangent, (y * 2 + c) * chunk_rows, chunk_rows, 0), odd_near
    )
    gain_two = to_own_first(ffn_gain, odd_near)
    cotangent_far = pair_swap(cotangent, "far")
    hidden, cotangent_far = after((hidden, cotangent_far))
    ffn_gate_weight, ffn_up_weight, ffn_down_weight = after(
        (ffn_gate_weight, ffn_up_weight, ffn_down_weight), qk_near, hidden, cotangent_far
    )
    cotangent_pair = jnp.concatenate([cotangent, cotangent_far], axis=0)
    cotangents = [cotangent_pair] + [side_swap(cotangent_pair, i) for i in range(1, 4)]

    def by_plane(*weights):
        return jnp.stack(
            [
                jnp.concatenate([w[:, p * units : (p + 1) * units] for w in weights], axis=1)
                for p in range(PLANES)
            ]
        )

    gate_up_half = to_plane_owners(by_plane(ffn_gate_weight, ffn_up_weight))

    half_width = low // 2
    frequency = rope_base ** (-2.0 * jnp.arange(half_width, dtype=f32) / low)
    frequency = jnp.concatenate([frequency, frequency])[None, :]
    bounds, key_ids, angles = pl.pallas_call(
        tables_kernel,
        out_shape=[
            shaped((tokens, low), jnp.int32),
            shaped((1, 4 * tokens), jnp.int32),
            shaped((tokens, low), f32),
        ],
        in_specs=[pl.BlockSpec(memory_space=pltpu.SMEM)] * 2
        + [pl.BlockSpec(memory_space=pltpu.VMEM)],
        out_specs=[pl.BlockSpec(memory_space=pltpu.VMEM)] * 3,
    )(after(doc_lengths, qk_near), jnp.stack(coords), frequency)
    sign = jnp.where(jnp.arange(low) < half_width, -1.0, 1.0).astype(f32)
    cosine, sine = jnp.cos(angles), jnp.sin(angles) * sign[None, :]
    query_gain, key_gain = query_gain[None, :], key_gain[None, :]

    normed, pair, query_rot, query_pre, key_pre = kernel_call(
        project_kernel,
        hidden + [gain_one[None, :]] + qk + [cosine, sine, query_gain, key_gain],
        [
            shaped((tokens, width), bf16),
            shaped((tokens, 2 * low), bf16),
            shaped((2, tokens, low), bf16),
            shaped((2, tokens, low), f32),
            shaped((tokens, low), f32),
        ],
        [pltpu.VMEM((2, tokens, 2 * low), f32)],
        core_flag,
        4 * tokens * width * 2 * low,
    )
    pair_near = pair_swap(pair, "near")
    pairs = [pair, pair_near, pair_swap(pair, "c"), pair_swap(pair_near, "c")]

    og = [og_half, og_near] + [pair_swap(after(part, pair), "c") for part in (og_half, og_near)]
    gate_up_near = pair_swap(after(gate_up_half, pair_near), "near")
    down_half = to_plane_owners(after(by_plane(ffn_down_weight), gate_up_half))
    query_rot, cotangents, gate_up_half = after((query_rot, cotangents, gate_up_half))

    (gate_pre,) = kernel_call(
        gate_kernel,
        [normed] + og,
        [shaped((2, tokens, low), f32)],
        flops=4 * tokens * width * low,
    )
    outs = kernel_call(
        attend_kernel,
        [query_rot] + pairs + [bounds, key_ids, gate_pre] + og,
        [shaped((2, tokens, low), bf16)]
        + [shaped((2, tokens, low), f32)] * 2
        + [shaped((chunk_rows, width), bf16)] * 8,
        [pltpu.VMEM((tokens, width), f32)],
        None,
        8 * tokens * 4 * tokens * low,
    )
    gated, attended, log_total, branch_parts = outs[0], outs[1], outs[2], outs[3:]
    away, own = sum_sends(branch_parts)
    away, gate_up_near, down_half = after((sum_pieces(away).astype(bf16), gate_up_near, down_half))
    hidden32 = own_hidden.astype(f32)
    middle = hidden32 + sum_pieces(own + [pair_swap(away, "far")])
    inv_two = lax.rsqrt(jnp.mean(middle * middle, axis=1, keepdims=True) + epsilon)
    normed_two_chunk = (middle * inv_two * gain_two).astype(bf16)
    normed_two_pieces = gather_chunks(normed_two_chunk)
    gate_up = [
        gate_up_half,
        gate_up_near,
        pair_swap(gate_up_half, "c"),
        pair_swap(gate_up_near, "c"),
    ]
    down_near = pair_swap(after(down_half, gate_up_near), "near")
    down = [down_half, down_near, pair_swap(down_half, "c"), pair_swap(down_near, "c")]

    outs = kernel_call(
        ffn_kernel,
        normed_two_pieces + cotangents + gate_up + down,
        [shaped((tokens, units), bf16)] * 2
        + [shaped((tokens, 2 * units), bf16)] * 2
        + [shaped((chunk_rows, width), bf16)] * 8
        + [shaped((2 * chunk_rows, width), bf16)] * 4
        + [shaped((tokens, width), bf16)] * 2,
        [pltpu.VMEM((2, tokens, width), f32)],
        None,
        24 * tokens * width * units,
    )
    hidden_acts, grad_ffn, two_parts, down_parts = outs[:2], outs[2:4], outs[4:12], outs[12:16]
    normed_two, all_cotangent = outs[16:]
    away, own = sum_sends(two_parts)
    two_far = pair_swap(sum_pieces(away).astype(bf16), "far")
    two_away = own, two_far
    gate_up_both = core_sum(*(contract_first(normed_two, g).astype(bf16) for g in grad_ffn))
    down_both = core_sum(*(contract_first(all_cotangent, act).astype(bf16) for act in hidden_acts))

    (own, two_far), down_both, gate_up_both = after((two_away, down_both, gate_up_both))
    grad_normed_two = sum_pieces(own + [two_far])

    def whole_block(chunk):
        chunk = from_own_first(chunk, odd_near)
        by_y = jnp.stack([chunk, pair_swap(chunk, "y")])
        by_core = jnp.stack([by_y, pair_swap(by_y, "c")], axis=1)
        return flip_if(flip_if(by_core, 1, c == 1), 0, y == 1).reshape(block_rows, width)

    grad_middle = cotangent.astype(f32) + norm_back(grad_normed_two, middle, inv_two, gain_two)
    grad_branch = grad_middle.astype(bf16)
    branch_pieces = gather_chunks(grad_branch)
    down_parts = after(down_parts, branch_pieces)
    down_pieces = [down_parts[0]] + [side_swap(down_parts[i], i) for i in range(1, 4)]
    half = width // 2
    gate_up_got = pair_swap(gate_up_both[half:], "near")

    all_branch, grad_gate, grad_query, grad_pairs, query_gain_part = kernel_call(
        attend_back_kernel,
        branch_pieces
        + og
        + pairs
        + [bounds, key_ids, query_rot, query_pre, gate_pre, attended, log_total]
        + [cosine, sine, query_gain],
        [
            shaped((tokens, width), bf16),
            shaped((2, tokens, low), bf16),
            shaped((2, tokens, low), bf16),
            shaped((4 * tokens, 2 * low), bf16),
            shaped((1, low), f32),
        ],
        [
            pltpu.VMEM((2, tokens, low), f32),
            pltpu.VMEM((4 * tokens, low), f32),
            pltpu.VMEM((4 * tokens, low), f32),
        ],
        None,
        20 * tokens * 4 * tokens * low,
    )
    pair_other = pair_swap(grad_pairs[2 * tokens :], "c")
    gate_up_got, normed_later = after((gate_up_got, normed), grad_pairs)
    near_pairs = grad_pairs[: 2 * tokens].astype(f32) + pair_other.astype(f32)
    near_pairs = near_pairs.astype(bf16)
    pair_got = pair_swap(near_pairs[tokens:], "near")
    gate_up_rows = near_add(gate_up_both, gate_up_got)
    down_got = pair_swap(after(down_both, pair_got)[half:], "near")
    gate_up_grad = to_row_owners(gate_up_rows)
    og_both = core_sum(
        *(
            jnp.concatenate(
                [
                    contract_first(normed_later, grad_gate[i]).astype(bf16),
                    contract_first(all_branch, gated[i]).astype(bf16),
                ],
                axis=1,
            )
            for i in range(2)
        )
    )
    key_pre, gate_up_rows = after((key_pre, gate_up_rows))
    og_got = pair_swap(after(og_both, pair_got)[half:], "near")
    outs = kernel_call(
        input_kernel,
        [near_pairs[:tokens], pair_got, key_pre, cosine, sine, key_gain]
        + [grad_query, grad_gate, normed]
        + qk
        + og,
        [shaped((tokens, 2 * low), bf16)] * 2
        + [shaped((chunk_rows, width), bf16)] * 8
        + [shaped((1, low), f32), shaped((1, width), f32)],
        [pltpu.VMEM((tokens, width), f32)],
        core_flag,
        12 * tokens * width * low,
    )
    grad_qk, normed_parts, key_gain_part, input_gain_part = outs[:2], outs[2:10], outs[10], outs[11]
    away, own = sum_sends(normed_parts)
    away = sum_pieces(away).astype(bf16)
    qk_sides = [contract_first(normed, g).astype(bf16) for g in after(grad_qk, normed_parts[1])]
    qk_other = pair_swap(qk_sides[1], "c")
    away, qk_other, gate_up_grad = after((away, qk_other, gate_up_grad))
    qk_both = (qk_sides[0].astype(f32) + qk_other.astype(f32)).astype(bf16)
    qk_got = pair_swap(qk_both[half:], "near")
    grad_far = pair_swap(away, "far")
    grad_far, down_got = after((grad_far, down_got))
    down_pieces = after(down_pieces, grad_far)
    down_sums = sum_pieces(down_pieces)
    down_far = pair_swap(down_sums[chunk_rows:].astype(bf16), "far")
    down_rows = near_add(down_both, down_got)
    grad_far, qk_got = after((grad_far, qk_got))
    grad_normed = sum_pieces(own + [grad_far])
    inv_one = lax.rsqrt(jnp.mean(hidden32 * hidden32, axis=1, keepdims=True) + epsilon)
    input_chunk = (grad_middle + norm_back(grad_normed, hidden32, inv_one, gain_one)).astype(bf16)
    input_grad = whole_block(input_chunk)
    og_got = after(og_got, grad_far)
    down_far, gain_parts = after(
        (down_far, (input_gain_part, query_gain_part, key_gain_part)), grad_far
    )
    attn_rows = jnp.concatenate([near_add(qk_both, qk_got), near_add(og_both, og_got)], axis=1)
    attn_grad = from_head_owners(attn_rows, far, x, c)
    down_grad = to_row_owners(after(down_rows, grad_far, gate_up_grad))
    qk_grad, og_grad = attn_grad[..., : 2 * low], attn_grad[..., 2 * low :]
    layer_out = whole_block((middle + down_sums[:chunk_rows] + down_far.astype(f32)).astype(bf16))
    gains = jnp.concatenate(
        [
            from_own_first(gain_parts[0][0] / gain_one, odd_near),
            from_own_first(jnp.sum(grad_normed_two * middle * inv_two, axis=0), odd_near),
            gain_parts[1][0],
            gain_parts[2][0],
        ]
    )
    gains = (gains + plane_swap(gains, 1)) + (plane_swap(gains, 2) + plane_swap(gains, 3))
    for axis in ("y", "c", "near"):
        gains = gains + pair_swap(gains, axis)

    def per_head(grad, start):
        columns = [grad[i, j, :, start : start + low] for i in range(2) for j in range(2)]
        return jnp.concatenate(columns, axis=1).astype(f32)

    def per_group(grad, j):
        return jnp.concatenate([grad[0, j, :, low:], grad[1, j, :, low:]], axis=1).astype(f32)

    def flat(grad):
        return jnp.concatenate([grad[p] for p in range(PLANES)], axis=1).astype(f32)

    return (
        layer_out,
        input_grad,
        per_head(qk_grad, 0),
        per_group(qk_grad, 0),
        per_group(qk_grad, 1),
        per_head(og_grad, 0),
        per_head(og_grad, low),
        flat(gate_up_grad[:, :, :units]),
        flat(gate_up_grad[:, :, units:]),
        flat(down_grad),
        gains[:width],
        gains[width : 2 * width],
        gains[2 * width : 2 * width + low],
        gains[2 * width + low :],
    )


def solution(mesh):
    wide, head = mesh.shape["wide"], mesh.shape["head"]
    if wide == 2 * PLANES and head == 4:
        devices = mesh.devices.reshape(2, 2, 2, 2, 2)
        mesh = Mesh(devices, ("far", "near", "x", "y", "c"))
        program, rows, columns = on_slice_device, ("far", "near", "x"), ("y", "c")
    else:
        program, rows, columns = on_device, "wide", "head"
    tokens, weight = P(rows, None), P(rows, columns)
    return jax.shard_map(
        program,
        mesh=mesh,
        in_specs=(tokens, tokens, P()) + (weight,) * 8 + (P(),) * 4,
        out_specs=(tokens, tokens) + (weight,) * 8 + (P(),) * 4,
        check_vma=False,
    )
```

```python
import jax
import jax.numpy as jnp
from jax import lax
from jax.experimental import pallas as pl
from jax.experimental.pallas import tpu as pltpu
from jax.sharding import Mesh
from jax.sharding import PartitionSpec as P

HEAD_WIDTH = 128


epsilon = 1e-06
rope_base = 1000000.0
masked_score = -1e30


def segment_of(lengths, token_ids):
    doc_ends = jnp.cumsum(lengths)
    return jnp.sum((token_ids[:, None] >= doc_ends[None, :]).astype(jnp.int32), axis=1)


def doc_tables(lengths, token_ids):
    doc_ends = jnp.cumsum(lengths)
    starts = doc_ends - lengths
    segment = segment_of(lengths, token_ids)
    labels = jnp.arange(lengths.shape[0], dtype=jnp.int32)
    doc_begin = jnp.sum(jnp.where(segment[:, None] == labels[None, :], starts[None, :], 0), axis=1)
    return (segment, token_ids - doc_begin)


def rope_tables(positions, head_size):
    half_size = head_size // 2
    frequency = rope_base ** (-2.0 * jnp.arange(half_size, dtype=jnp.float32) / head_size)
    angles = positions.astype(jnp.float32)[:, None] * frequency[None, :]
    cosine = jnp.cos(angles)
    sine_table = jnp.sin(angles)
    return (
        jnp.concatenate([cosine, cosine], axis=1),
        jnp.concatenate([sine_table, sine_table], axis=1),
    )


def rotate_half(values):
    half_size = values.shape[-1] // 2
    return jnp.concatenate([-values[..., half_size:], values[..., :half_size]], axis=-1)


def rotate_back(values):
    half_size = values.shape[-1] // 2
    return jnp.concatenate([values[..., half_size:], -values[..., :half_size]], axis=-1)


def apply_rope(values, cos_table, sin_table):
    return values * cos_table[:, None, :] + rotate_half(values) * sin_table[:, None, :]


def rope_back(grads, cos_table, sin_table):
    return grads * cos_table[:, None, :] + rotate_back(grads * sin_table[:, None, :])


def contract_last(left, right):
    return lax.dot_general(
        left, right, (((1,), (1,)), ((), ())), preferred_element_type=jnp.float32
    )


def contract_first(left, right):
    return lax.dot_general(
        left, right, (((0,), (0,)), ((), ())), preferred_element_type=jnp.float32
    )


def norm_back(grad_out, inputs, inv_root, gain):
    scaled = grad_out * gain
    return inv_root * scaled - inputs * inv_root**3 * jnp.mean(
        scaled * inputs, axis=-1, keepdims=True
    )


def on_device(
    hidden_in,
    out_cotangent,
    doc_lengths,
    query_weight,
    key_matrix,
    value_matrix,
    gate_weight,
    out_weight,
    ffn_gate_weight,
    ffn_up_weight,
    ffn_down_weight,
    attn_gain,
    ffn_gain,
    query_gain,
    key_gain,
):
    tok_rows = hidden_in.shape[0]
    row_length = tok_rows * lax.axis_size("wide")
    first_row = lax.axis_index("wide") * tok_rows
    token_ids = first_row + jnp.arange(tok_rows, dtype=jnp.int32)
    segment, positions = doc_tables(doc_lengths, token_ids)
    shard_begin = first_row - positions[0]
    shard_last = first_row + tok_rows - 1
    cos_table, sin_table = rope_tables(positions, HEAD_WIDTH)
    local_heads = query_weight.shape[1] // HEAD_WIDTH
    kv_heads = key_matrix.shape[1] // HEAD_WIDTH
    group_width = local_heads // kv_heads
    query_rows = group_width * tok_rows
    score_scale = HEAD_WIDTH ** (-0.5)
    (
        full_query,
        full_key,
        full_value,
        full_gate,
        full_out,
        full_ffn_gate,
        full_ffn_up,
        full_ffn_down,
    ) = (
        lax.all_gather(query_weight, "wide", axis=0, tiled=True),
        lax.all_gather(key_matrix, "wide", axis=0, tiled=True),
        lax.all_gather(value_matrix, "wide", axis=0, tiled=True),
        lax.all_gather(gate_weight, "wide", axis=0, tiled=True),
        lax.all_gather(out_weight, "wide", axis=0, tiled=True),
        lax.all_gather(ffn_gate_weight, "wide", axis=0, tiled=True),
        lax.all_gather(ffn_up_weight, "wide", axis=0, tiled=True),
        lax.all_gather(ffn_down_weight, "wide", axis=0, tiled=True),
    )
    hidden32 = hidden_in.astype(jnp.float32)
    inv_one = lax.rsqrt(jnp.mean(hidden32 * hidden32, axis=1, keepdims=True) + epsilon)
    normed_input = (hidden32 * inv_one * attn_gain).astype(jnp.bfloat16)
    query_pre = jnp.dot(normed_input, full_query, preferred_element_type=jnp.float32).reshape(
        tok_rows, local_heads, HEAD_WIDTH
    )
    key_before_norm = jnp.dot(normed_input, full_key, preferred_element_type=jnp.float32).reshape(
        tok_rows, kv_heads, HEAD_WIDTH
    )
    value_rows = jnp.dot(normed_input, full_value, preferred_element_type=jnp.float32).astype(
        jnp.bfloat16
    )
    gate_pre = jnp.dot(normed_input, full_gate, preferred_element_type=jnp.float32)
    inv_query = lax.rsqrt(jnp.mean(query_pre * query_pre, axis=-1, keepdims=True) + epsilon)
    inv_key = lax.rsqrt(
        jnp.mean(key_before_norm * key_before_norm, axis=-1, keepdims=True) + epsilon
    )
    query_unit = query_pre * inv_query
    key_unit = key_before_norm * inv_key
    query_rot = apply_rope(query_unit * query_gain, cos_table, sin_table).astype(jnp.bfloat16)
    key_rows = (
        apply_rope(key_unit * key_gain, cos_table, sin_table)
        .astype(jnp.bfloat16)
        .reshape(tok_rows, kv_heads * HEAD_WIDTH)
    )
    query_heads = (
        query_rot.reshape(tok_rows, kv_heads, group_width, HEAD_WIDTH)
        .transpose(1, 2, 0, 3)
        .reshape(kv_heads, query_rows, HEAD_WIDTH)
    )
    query_seg = jnp.tile(segment, group_width)
    query_ids = jnp.tile(token_ids, group_width)
    start_state = (
        jnp.full((kv_heads, query_rows), masked_score, jnp.float32),
        jnp.zeros((kv_heads, query_rows), jnp.float32),
        jnp.zeros((kv_heads, query_rows, HEAD_WIDTH), jnp.float32),
    )
    key_piece = lax.all_gather(key_rows, "wide", axis=0, tiled=True)
    value_piece = lax.all_gather(value_rows, "wide", axis=0, tiled=True)
    count = key_piece.shape[0]
    step_rows = 512
    steps_count = count // step_rows
    key_ids = jnp.arange(count, dtype=jnp.int32)
    key_seg = segment_of(doc_lengths, key_ids)
    key_blocks = key_piece.reshape(steps_count, step_rows, kv_heads, HEAD_WIDTH).transpose(
        0, 2, 1, 3
    )
    value_blocks = value_piece.reshape(steps_count, step_rows, kv_heads, HEAD_WIDTH).transpose(
        0, 2, 1, 3
    )

    def inner(state, block):
        key_block, value_block, block_seg, block_ids = block

        def inner_work(state_in):
            scores = (
                jnp.einsum(
                    "hqd,hkd->hqk", query_heads, key_block, preferred_element_type=jnp.float32
                )
                * score_scale
            )
            allowed = (
                (query_seg[:, None] == block_seg[None, :])
                & (block_ids[None, :] <= query_ids[:, None])
            )[None]
            scores = jnp.where(allowed, scores, masked_score)
            running, total, accum = state_in
            newest = jnp.maximum(running, jnp.max(scores, axis=-1))
            factor = jnp.exp(running - newest)
            weights = jnp.where(allowed, jnp.exp(scores - newest[..., None]), 0.0)
            total = total * factor + jnp.sum(weights, axis=-1)
            accum = accum * factor[..., None] + jnp.einsum(
                "hqk,hkd->hqd",
                weights.astype(jnp.bfloat16),
                value_block,
                preferred_element_type=jnp.float32,
            )
            return (newest, total, accum)

        useful = (block_ids[0] <= shard_last) & (block_ids[step_rows - 1] >= shard_begin)
        return (lax.cond(useful, inner_work, lambda state_in: state_in, state), None)

    state, unused = lax.scan(
        inner,
        start_state,
        (
            key_blocks,
            value_blocks,
            key_seg.reshape(steps_count, step_rows),
            key_ids.reshape(steps_count, step_rows),
        ),
    )
    running, total, accum = state
    attended_heads = accum / total[..., None]
    log_total = running + jnp.log(total)
    attended = (
        attended_heads.reshape(kv_heads, group_width, tok_rows, HEAD_WIDTH)
        .transpose(2, 0, 1, 3)
        .reshape(tok_rows, local_heads * HEAD_WIDTH)
    )
    gate_sig = jax.nn.sigmoid(gate_pre)
    gated = (attended * gate_sig).astype(jnp.bfloat16)
    branch = lax.psum(contract_last(gated, full_out).astype(jnp.bfloat16), "head").astype(
        jnp.float32
    )
    middle = hidden32 + branch
    inv_two = lax.rsqrt(jnp.mean(middle * middle, axis=1, keepdims=True) + epsilon)
    normed_two = (middle * inv_two * ffn_gain).astype(jnp.bfloat16)
    ffn_gate_pre = jnp.dot(normed_two, full_ffn_gate, preferred_element_type=jnp.float32)
    ffn_up_pre = jnp.dot(normed_two, full_ffn_up, preferred_element_type=jnp.float32)
    gate_act = jax.nn.sigmoid(ffn_gate_pre)
    silu_gate = ffn_gate_pre * gate_act
    hidden_act = (silu_gate * ffn_up_pre).astype(jnp.bfloat16)
    ffn_out = lax.psum(
        contract_last(hidden_act, full_ffn_down).astype(jnp.bfloat16), "head"
    ).astype(jnp.float32)
    layer_out = (middle + ffn_out).astype(jnp.bfloat16)
    grad32 = out_cotangent.astype(jnp.float32)
    grad_hidden = jnp.dot(out_cotangent, full_ffn_down, preferred_element_type=jnp.float32)
    grad_ffn_gate = (
        grad_hidden * ffn_up_pre * gate_act * (1.0 + ffn_gate_pre * (1.0 - gate_act))
    ).astype(jnp.bfloat16)
    grad_ffn_up = (grad_hidden * silu_gate).astype(jnp.bfloat16)
    grad_normed_two = lax.psum(
        (
            contract_last(grad_ffn_gate, full_ffn_gate) + contract_last(grad_ffn_up, full_ffn_up)
        ).astype(jnp.bfloat16),
        "head",
    ).astype(jnp.float32)
    grad_middle = grad32 + norm_back(grad_normed_two, middle, inv_two, ffn_gain)
    grad_branch = grad_middle.astype(jnp.bfloat16)
    grad_gated = jnp.dot(grad_branch, full_out, preferred_element_type=jnp.float32)
    grad_attended = (grad_gated * gate_sig).astype(jnp.bfloat16)
    grad_gate_pre = (grad_gated * attended * gate_sig * (1.0 - gate_sig)).astype(jnp.bfloat16)
    grad_heads = (
        grad_attended.reshape(tok_rows, kv_heads, group_width, HEAD_WIDTH)
        .transpose(1, 2, 0, 3)
        .reshape(kv_heads, query_rows, HEAD_WIDTH)
    )
    delta = jnp.sum(grad_heads.astype(jnp.float32) * attended_heads, axis=-1)
    all_keys, all_values = key_piece, value_piece
    key_step = 512
    key_count = row_length // key_step
    all_ids = jnp.arange(row_length, dtype=jnp.int32)
    all_seg = segment_of(doc_lengths, all_ids)
    key_blocks = all_keys.reshape(key_count, key_step, kv_heads, HEAD_WIDTH).transpose(0, 2, 1, 3)
    value_blocks = all_values.reshape(key_count, key_step, kv_heads, HEAD_WIDTH).transpose(
        0, 2, 1, 3
    )
    key_scan_items = (
        key_blocks,
        value_blocks,
        all_seg.reshape(key_count, key_step),
        all_ids.reshape(key_count, key_step),
    )
    zero_query = jnp.zeros((kv_heads, query_rows, HEAD_WIDTH), jnp.float32)

    def block_terms(key_block, value_block, block_seg, block_ids):
        scores = (
            jnp.einsum("hqd,hkd->hqk", query_heads, key_block, preferred_element_type=jnp.float32)
            * score_scale
        )
        allowed = (
            (query_seg[:, None] == block_seg[None, :]) & (block_ids[None, :] <= query_ids[:, None])
        )[None]
        weights = jnp.where(
            allowed, jnp.exp(jnp.where(allowed, scores, masked_score) - log_total[..., None]), 0.0
        )
        grad_weights = jnp.einsum(
            "hqd,hkd->hqk", grad_heads, value_block, preferred_element_type=jnp.float32
        )
        grad_scores = (weights * (grad_weights - delta[..., None])).astype(jnp.bfloat16)
        return (weights, grad_scores)

    def block_useful(block_ids):
        return (block_ids[0] <= shard_last) & (block_ids[key_step - 1] >= shard_begin)

    def back_block(grad_query, block):
        key_block, value_block, block_seg, block_ids = block

        def back_work(grad_in):
            weights, grad_scores = block_terms(key_block, value_block, block_seg, block_ids)
            grad_out = (
                grad_in
                + jnp.einsum(
                    "hqk,hkd->hqd", grad_scores, key_block, preferred_element_type=jnp.float32
                )
                * score_scale
            )
            grad_key = (
                jnp.einsum(
                    "hqk,hqd->hkd", grad_scores, query_heads, preferred_element_type=jnp.float32
                )
                * score_scale
            )
            grad_value = jnp.einsum(
                "hqk,hqd->hkd",
                weights.astype(jnp.bfloat16),
                grad_heads,
                preferred_element_type=jnp.float32,
            )
            return (grad_out, (grad_key, grad_value))

        def skip(grad_in):
            nothing = jnp.zeros((kv_heads, key_step, HEAD_WIDTH), jnp.float32)
            return (grad_in, (nothing, nothing))

        return lax.cond(block_useful(block_ids), back_work, skip, grad_query)

    grad_query, (key_parts, value_parts) = lax.scan(back_block, zero_query, key_scan_items)
    key_grad_rows = key_parts.transpose(0, 2, 1, 3).reshape(row_length, kv_heads * HEAD_WIDTH)
    value_grad_rows = value_parts.transpose(0, 2, 1, 3).reshape(row_length, kv_heads * HEAD_WIDTH)
    key_total, value_total = (
        lax.psum_scatter(
            key_grad_rows.astype(jnp.bfloat16), "wide", scatter_dimension=0, tiled=True
        ).astype(jnp.float32),
        lax.psum_scatter(
            value_grad_rows.astype(jnp.bfloat16), "wide", scatter_dimension=0, tiled=True
        ).astype(jnp.float32),
    )
    grad_values = value_total.astype(jnp.bfloat16)
    grad_key_rot = (
        key_total.astype(jnp.bfloat16).astype(jnp.float32).reshape(tok_rows, kv_heads, HEAD_WIDTH)
    )
    grad_query_rot = (
        grad_query.astype(jnp.bfloat16)
        .astype(jnp.float32)
        .reshape(kv_heads, group_width, tok_rows, HEAD_WIDTH)
        .transpose(2, 0, 1, 3)
        .reshape(tok_rows, local_heads, HEAD_WIDTH)
    )
    grad_query_unit = rope_back(grad_query_rot, cos_table, sin_table)
    grad_key_unit = rope_back(grad_key_rot, cos_table, sin_table)
    query_gain_part = jnp.sum(grad_query_unit * query_unit, axis=(0, 1))
    key_gain_part = jnp.sum(grad_key_unit * key_unit, axis=(0, 1))
    grad_query_pre = (
        norm_back(grad_query_unit, query_pre, inv_query, query_gain)
        .reshape(tok_rows, local_heads * HEAD_WIDTH)
        .astype(jnp.bfloat16)
    )
    grad_key_pre = (
        norm_back(grad_key_unit, key_before_norm, inv_key, key_gain)
        .reshape(tok_rows, kv_heads * HEAD_WIDTH)
        .astype(jnp.bfloat16)
    )
    grad_normed_part = (
        contract_last(grad_query_pre, full_query)
        + contract_last(grad_key_pre, full_key)
        + contract_last(grad_values, full_value)
        + contract_last(grad_gate_pre, full_gate)
    )
    grad_normed = lax.psum(grad_normed_part.astype(jnp.bfloat16), "head").astype(jnp.float32)
    input_grad = (grad_middle + norm_back(grad_normed, hidden32, inv_one, attn_gain)).astype(
        jnp.bfloat16
    )
    attn_gain_part = jnp.sum(grad_normed * hidden32 * inv_one, axis=0)
    ffn_gain_part = jnp.sum(grad_normed_two * middle * inv_two, axis=0)
    weight_grads = lax.psum_scatter(
        jnp.concatenate(
            [
                contract_first(normed_input, grad_query_pre),
                contract_first(normed_input, grad_key_pre),
                contract_first(normed_input, grad_values),
                contract_first(normed_input, grad_gate_pre),
                contract_first(grad_branch, gated),
                contract_first(normed_two, grad_ffn_gate),
                contract_first(normed_two, grad_ffn_up),
                contract_first(out_cotangent, hidden_act),
            ],
            axis=1,
        ).astype(jnp.bfloat16),
        "wide",
        scatter_dimension=0,
        tiled=True,
    ).astype(jnp.float32)
    col_widths = [
        query_weight.shape[1],
        key_matrix.shape[1],
        value_matrix.shape[1],
        gate_weight.shape[1],
        out_weight.shape[1],
        ffn_gate_weight.shape[1],
        ffn_up_weight.shape[1],
        ffn_down_weight.shape[1],
    ]
    pieces = []
    offset = 0
    for width in col_widths:
        pieces.append(weight_grads[:, offset : offset + width])
        offset = offset + width
    head_first = (lax.axis_index("head") == 0).astype(jnp.float32)
    attn_gain_grad, ffn_gain_grad, query_gain_grad, key_gain_grad = lax.psum(
        (attn_gain_part * head_first, ffn_gain_part * head_first, query_gain_part, key_gain_part),
        ("wide", "head"),
    )
    return (
        layer_out,
        input_grad,
        pieces[0],
        pieces[1],
        pieces[2],
        pieces[3],
        pieces[4],
        pieces[5],
        pieces[6],
        pieces[7],
        attn_gain_grad,
        ffn_gain_grad,
        query_gain_grad,
        key_gain_grad,
    )


PLANES = 4
PLANE = ("far", "x")


def pair_swap(values, axis):
    return lax.ppermute(values, axis, [(0, 1), (1, 0)])


def plane_swap(values, step):
    return lax.ppermute(values, PLANE, [(i, i ^ step) for i in range(PLANES)])


def side_swap(values, step):
    return lax.ppermute(values, ("x", "y"), [(i, i ^ step) for i in range(4)])


def after(values, *done):
    return lax.optimization_barrier((values, done))[0]


def gather_chunks(chunk):
    far = pair_swap(chunk, "far")
    near = [side_swap(chunk, step) for step in range(1, 4)]
    away = [side_swap(far, step) for step in range(1, 4)]
    pieces = [chunk, far]
    for pair in zip(near, away):
        pieces.extend(pair)
    return pieces


def sum_sends(parts):
    return [
        [parts[far]] + [side_swap(parts[2 * step + far], step) for step in range(1, 4)]
        for far in (1, 0)
    ]


def sum_pieces(pieces):
    total = pieces[0].astype(jnp.float32)
    for piece in pieces[1:]:
        total = total + piece.astype(jnp.float32)
    return total


def flip_if(values, axis, flag):
    return jnp.where(flag, jnp.flip(values, axis), values)


def to_own_first(values, flag):
    lead = values.shape[:-1]
    width = values.shape[-1]
    split = values.reshape(lead + (2, 2, width // 4))
    zero = split[..., 0, :].reshape(lead + (width // 2,))
    one = split[..., 1, :].reshape(lead + (width // 2,))
    return jnp.concatenate([jnp.where(flag, one, zero), jnp.where(flag, zero, one)], axis=-1)


def from_own_first(values, flag):
    lead = values.shape[:-1]
    width = values.shape[-1]
    own = values[..., : width // 2].reshape(lead + (2, width // 4))
    other = values[..., width // 2 :].reshape(lead + (2, width // 4))
    pair = jnp.stack([jnp.where(flag, other, own), jnp.where(flag, own, other)], axis=-2)
    return pair.reshape(lead + (width,))


def to_plane_owners(local):
    planes, rows, width = local.shape
    return lax.all_to_all(
        local.reshape(planes * rows, width), PLANE, split_axis=0, concat_axis=0, tiled=True
    )


HEADS = ("far", "x", "c")


def head_pairs(a, b, back):
    pairs = []
    for f in range(2):
        for x in range(2):
            for c in range(2):
                pairs.append((4 * f + 2 * x + c, 4 * c + 2 * (x ^ a) + (f ^ b)))
    return [(j, i) for i, j in pairs] if back else pairs


def to_head_owners(columns, far, x, c):
    turned = flip_if(flip_if(columns, 0, x == 1), 1, far == 1)
    sent = [
        [lax.ppermute(turned[a, b], HEADS, head_pairs(a, b, False)) for a in range(2)]
        for b in range(2)
    ]
    pieces = jnp.stack([jnp.stack(row) for row in sent])
    rows = flip_if(flip_if(pieces, 0, c == 1), 1, x == 1)
    return rows.reshape(PLANES * columns.shape[2], columns.shape[3]), sent


def from_head_owners(rows, far, x, c):
    blocks = rows.reshape(2, 2, rows.shape[0] // PLANES, rows.shape[1])
    blocks = flip_if(flip_if(blocks, 0, c == 1), 1, x == 1)
    pieces = jnp.stack(
        [
            jnp.stack(
                [lax.ppermute(blocks[b, a], HEADS, head_pairs(a, b, True)) for b in range(2)]
            )
            for a in range(2)
        ]
    )
    return flip_if(flip_if(pieces, 0, x == 1), 1, far == 1)


def core_sum(mine, other):
    both = mine.astype(jnp.float32) + pair_swap(other, "c").astype(jnp.float32)
    return both.astype(jnp.bfloat16)


def near_add(both, got):
    half = both.shape[0] // 2
    return (both[:half].astype(jnp.float32) + got.astype(jnp.float32)).astype(jnp.bfloat16)


def to_row_owners(rows):
    back = lax.all_to_all(rows, PLANE, split_axis=0, concat_axis=0, tiled=True)
    return back.reshape(PLANES, rows.shape[0] // PLANES, rows.shape[1])


VMEM_BYTES = 56 * 1024 * 1024


def kernel_call(body, operands, outs, scratch=(), flags=None, flops=0, far_operands=0):
    specs = [pl.BlockSpec(memory_space=pltpu.VMEM)] * (len(operands) - far_operands)
    specs += [pl.BlockSpec(memory_space=pl.ANY)] * far_operands
    if flags is not None:
        operands = [flags] + list(operands)
        specs = [pl.BlockSpec(memory_space=pltpu.SMEM)] + specs
    moved = sum(v.size * v.dtype.itemsize for v in operands)
    moved += sum(v.size * v.dtype.itemsize for v in outs)
    return pl.pallas_call(
        body,
        out_shape=outs,
        in_specs=specs,
        out_specs=[pl.BlockSpec(memory_space=pltpu.VMEM)] * len(outs),
        scratch_shapes=list(scratch),
        compiler_params=pltpu.CompilerParams(vmem_limit_bytes=VMEM_BYTES),
        cost_estimate=pl.CostEstimate(flops=flops, bytes_accessed=moved, transcendentals=0),
    )(*operands)


def shaped(shape, dtype):
    return jax.ShapeDtypeStruct(shape, dtype)


def dot_nn(left, right):
    return jnp.dot(left, right, preferred_element_type=jnp.float32)


def turned(values, cosine, signed_sine):
    return values * cosine + pltpu.roll(values, HEAD_WIDTH // 2, 1) * signed_sine


def turned_back(grads, cosine, signed_sine):
    return grads * cosine - pltpu.roll(grads, HEAD_WIDTH // 2, 1) * signed_sine


def sigmoid(values):
    return 1.0 / (1.0 + jnp.exp(-values))


def project_kernel(flag, *refs):
    hidden = refs[:8]
    gain, mine_own, mine_near, other_own, other_near, cosine, sine, qgain, kgain = refs[8:17]
    normed, pair, query_rot, query_pre, key_pre, scratch = refs[17:]
    rows = hidden[0].shape[0]
    for i in range(8):
        h = hidden[i][...].astype(jnp.float32)
        inverse = lax.rsqrt(jnp.mean(h * h, axis=1, keepdims=True) + epsilon)
        normed[i * rows : (i + 1) * rows, :] = (h * inverse * gain[...]).astype(jnp.bfloat16)
    half = normed.shape[1] // 2
    left, right = normed[:, :half], normed[:, half:]
    for i, (own, near) in enumerate(((mine_own, mine_near), (other_own, other_near))):
        scratch[i] = dot_nn(left, own[...]) + dot_nn(right, near[...])
    cos, sin = cosine[...], sine[...]
    swapped = flag[0] == 1
    mine, other = scratch[0, :, HEAD_WIDTH:], scratch[1, :, HEAD_WIDTH:]
    pre = jnp.where(swapped, other, mine)
    key_pre[...] = pre
    pair[:, HEAD_WIDTH:] = jnp.where(swapped, mine, other).astype(jnp.bfloat16)
    unit = pre * lax.rsqrt(jnp.mean(pre * pre, axis=1, keepdims=True) + epsilon)
    pair[:, :HEAD_WIDTH] = turned(unit * kgain[...], cos, sin).astype(jnp.bfloat16)
    for i in range(2):
        pre = scratch[i, :, :HEAD_WIDTH]
        query_pre[i] = pre
        unit = pre * lax.rsqrt(jnp.mean(pre * pre, axis=1, keepdims=True) + epsilon)
        query_rot[i] = turned(unit * qgain[...], cos, sin).astype(jnp.bfloat16)


def attend_kernel(query_rot, first, second, third, fourth, bounds, key_ids, gate_pre, *refs):
    outs_w, gated, attended, log_total, parts, total = refs[:4], *refs[4:7], refs[7:15], refs[15]
    scale = HEAD_WIDTH ** (-0.5)
    pairs = (first, second, third, fourth)
    rows = first.shape[0]
    tile = rows // 2

    def step(i, carry):
        head, at = i // 2, pl.multiple_of(i % 2 * tile, tile)
        query = query_rot[head, pl.ds(at, tile), :]
        start, last = bounds[pl.ds(at, tile), 0:1], bounds[pl.ds(at, tile), 1:2]
        scores = []
        for j, pair in enumerate(pairs):
            ids = key_ids[:, j * rows : (j + 1) * rows]
            allowed = (ids >= start) & (ids <= last)
            score = contract_last(query, pair[:, :HEAD_WIDTH]) * scale
            scores.append(jnp.where(allowed, score, masked_score))
        top = jnp.max(scores[0], axis=1, keepdims=True)
        for score in scores[1:]:
            top = jnp.maximum(top, jnp.max(score, axis=1, keepdims=True))
        total = jnp.zeros_like(top)
        result = jnp.zeros((tile, HEAD_WIDTH), jnp.float32)
        for score, pair in zip(scores, pairs):
            raised = jnp.exp(score - top)
            total = total + jnp.sum(raised, axis=1, keepdims=True)
            result = result + dot_nn(raised.astype(jnp.bfloat16), pair[:, HEAD_WIDTH:])
        result = result / total
        attended[head, pl.ds(at, tile), :] = result
        log_total[head, pl.ds(at, tile), :] = jnp.broadcast_to(top + jnp.log(total), result.shape)
        gate = sigmoid(gate_pre[head, pl.ds(at, tile), :])
        gated[head, pl.ds(at, tile), :] = (result * gate).astype(jnp.bfloat16)
        return carry

    lax.fori_loop(0, 4, step, 0)
    half = total.shape[1] // 2
    for near in range(2):
        total[:, near * half : (near + 1) * half] = contract_last(
            gated[0], outs_w[near][:, HEAD_WIDTH:]
        ) + contract_last(gated[1], outs_w[2 + near][:, HEAD_WIDTH:])
    rows = parts[0].shape[0]
    for i in range(8):
        parts[i][...] = total[i * rows : (i + 1) * rows, :].astype(jnp.bfloat16)


def ffn_kernel(*refs):
    chunks, cotangent, gate_up, down = refs[:8], refs[8:12], refs[12:16], refs[16:20]
    acts, grads, two_parts = refs[20:22], refs[22:24], refs[24:32]
    normed_two, cot, total = refs[32:35]
    gate_up_here, down_here, sems = refs[35:39], refs[39:43], refs[43]
    copies = []
    for side in range(2):
        for i in (2 * side, 2 * side + 1):
            copies.append(pltpu.make_async_copy(gate_up[i], gate_up_here[i], sems.at[len(copies)]))
        for i in (2 * side, 2 * side + 1):
            copies.append(pltpu.make_async_copy(down[i], down_here[i], sems.at[len(copies)]))
    for copy in copies:
        copy.start()
    rows = chunks[0].shape[0]
    for i in range(8):
        normed_two[i * rows : (i + 1) * rows, :] = chunks[i][...]
    rows = cotangent[0].shape[0]
    for i in range(4):
        cot[i * rows : (i + 1) * rows, :] = cotangent[i][...]
    half = cot.shape[1] // 2
    units = down_here[0].shape[1]
    tile = cot.shape[0] // 2
    for side in range(2):
        for copy in copies[4 * side : 4 * side + 4]:
            copy.wait()

        def step(i, carry, side=side):
            rows_at = pl.ds(pl.multiple_of(i * tile, tile), tile)
            own, near = 2 * side, 2 * side + 1
            pre = dot_nn(normed_two[rows_at, :half], gate_up_here[own][...]) + dot_nn(
                normed_two[rows_at, half:], gate_up_here[near][...]
            )
            grad = dot_nn(cot[rows_at, :half], down_here[own][...]) + dot_nn(
                cot[rows_at, half:], down_here[near][...]
            )
            gate, up = pre[:, :units], pre[:, units:]
            act = sigmoid(gate)
            silu = gate * act
            acts[side][rows_at, :] = (silu * up).astype(jnp.bfloat16)
            grads[side][rows_at, :units] = (
                grad * up * act * (1.0 + gate * (1.0 - act))
            ).astype(jnp.bfloat16)
            grads[side][rows_at, units:] = (grad * silu).astype(jnp.bfloat16)
            for i_near in range(2):
                part = contract_last(
                    grads[side][rows_at, :], gate_up_here[2 * side + i_near][...]
                )
                columns = slice(i_near * half, (i_near + 1) * half)
                total[rows_at, columns] = part if side == 0 else total[rows_at, columns] + part
            return carry

        lax.fori_loop(0, 2, step, 0)
    rows = two_parts[0].shape[0]
    for i in range(8):
        two_parts[i][...] = total[i * rows : (i + 1) * rows, :].astype(jnp.bfloat16)


def down_kernel(*refs):
    acts, down, parts, total = refs[:2], refs[2:6], refs[6:10], refs[10]
    half = total.shape[1] // 2
    for near in range(2):
        total[:, near * half : (near + 1) * half] = contract_last(
            acts[0][...], down[near][...]
        ) + contract_last(acts[1][...], down[2 + near][...])
    rows = parts[0].shape[0]
    for i in range(4):
        parts[i][...] = total[i * rows : (i + 1) * rows, :].astype(jnp.bfloat16)


def attend_back_kernel(*refs):
    chunks, outs_w, pairs = refs[:8], refs[8:12], refs[12:16]
    bounds, key_ids, query_rot, query_pre, gate_pre, attended, log_total = refs[16:23]
    cosine, sine, qgain = refs[23:26]
    branch, grad_gate, grad_query, grad_pairs, gain_part = refs[26:31]
    gated_grad, keys_acc, vals_acc = refs[31:]
    scale = HEAD_WIDTH ** (-0.5)
    rows = chunks[0].shape[0]
    for i in range(8):
        branch[i * rows : (i + 1) * rows, :] = chunks[i][...]
    half = branch.shape[1] // 2
    for side in range(2):
        gated_grad[side] = dot_nn(branch[:, :half], outs_w[2 * side][:, HEAD_WIDTH:]) + dot_nn(
            branch[:, half:], outs_w[2 * side + 1][:, HEAD_WIDTH:]
        )
    keys_acc[...] = jnp.zeros_like(keys_acc)
    vals_acc[...] = jnp.zeros_like(vals_acc)
    gain_part[...] = jnp.zeros_like(gain_part)
    rows = pairs[0].shape[0]
    tile = rows // 2

    def step(i, carry):
        head, at = i // 2, pl.multiple_of(i % 2 * tile, tile)
        rows_at = pl.ds(at, tile)
        grad = gated_grad[head, rows_at, :]
        gate = sigmoid(gate_pre[head, rows_at, :])
        out = attended[head, rows_at, :]
        grad_gate[head, rows_at, :] = (grad * out * gate * (1.0 - gate)).astype(jnp.bfloat16)
        grad_out = (grad * gate).astype(jnp.bfloat16)
        delta = jnp.sum(grad_out.astype(jnp.float32) * out, axis=1, keepdims=True)
        query = query_rot[head, rows_at, :]
        start, last = bounds[rows_at, 0:1], bounds[rows_at, 1:2]
        log = log_total[head, rows_at, 0:1]
        grad_rot = jnp.zeros((tile, HEAD_WIDTH), jnp.float32)
        for j, pair in enumerate(pairs):
            ids = key_ids[:, j * rows : (j + 1) * rows]
            allowed = (ids >= start) & (ids <= last)
            keys, vals = pair[:, :HEAD_WIDTH], pair[:, HEAD_WIDTH:]
            score = jnp.where(allowed, contract_last(query, keys) * scale, masked_score)
            weight = jnp.exp(score - log)
            grad_score = (weight * (contract_last(grad_out, vals) - delta)).astype(jnp.bfloat16)
            grad_rot = grad_rot + dot_nn(grad_score, keys)
            at_keys = slice(j * rows, (j + 1) * rows)
            keys_acc[at_keys, :] += contract_first(grad_score, query)
            vals_acc[at_keys, :] += contract_first(weight.astype(jnp.bfloat16), grad_out)
        grad_rot = (grad_rot * scale).astype(jnp.bfloat16).astype(jnp.float32)
        grad_unit = turned_back(grad_rot, cosine[rows_at, :], sine[rows_at, :])
        pre = query_pre[head, rows_at, :]
        inverse = lax.rsqrt(jnp.mean(pre * pre, axis=1, keepdims=True) + epsilon)
        gain_part[...] += jnp.sum(grad_unit * (pre * inverse), axis=0, keepdims=True)
        grad_query[head, rows_at, :] = norm_back(grad_unit, pre, inverse, qgain[...]).astype(
            jnp.bfloat16
        )
        return carry

    lax.fori_loop(0, 4, step, 0)
    grad_pairs[:, :HEAD_WIDTH] = (keys_acc[...] * scale).astype(jnp.bfloat16)
    grad_pairs[:, HEAD_WIDTH:] = vals_acc[...].astype(jnp.bfloat16)


def tables_kernel(lengths, coords, frequency, bounds, key_ids, angles):
    far, near, x, y, c = (coords[i] for i in range(5))
    rows = bounds.shape[0] // 8

    def ids_of(at, near_at, c_at):
        chunk, row = at // rows, at % rows
        x_at, y_at, far_at = x ^ (chunk // 4), y ^ (chunk // 2 % 2), far ^ (chunk % 2)
        return (((far_at * 2 + near_at) * 2 + x_at) * 4 + y_at * 2 + c_at) * rows + row

    at = lax.broadcasted_iota(jnp.int32, bounds.shape, 0)
    lane = lax.broadcasted_iota(jnp.int32, bounds.shape, 1)
    ids = ids_of(at, near, c)
    start = jnp.zeros_like(ids)
    end = jnp.int32(0)
    for i in range(lengths.shape[0]):
        end = end + lengths[i]
        start = jnp.where(ids >= end, end, start)
    bounds[...] = jnp.where(lane == 0, start, ids)
    angles[...] = (ids - start).astype(jnp.float32) * frequency[...]
    at = lax.broadcasted_iota(jnp.int32, key_ids.shape, 1)
    group = at // (8 * rows)
    key_ids[...] = ids_of(at % (8 * rows), near ^ (group % 2), c ^ (group // 2))


def gate_kernel(normed, mine_own, mine_near, other_own, other_near, gate_pre):
    half = normed.shape[1] // 2
    for i, (own, near) in enumerate(((mine_own, mine_near), (other_own, other_near))):
        gate_pre[i] = dot_nn(normed[:, :half], own[:, :HEAD_WIDTH]) + dot_nn(
            normed[:, half:], near[:, :HEAD_WIDTH]
        )


def input_kernel(flag, *refs):
    own_pair, got_pair, key_pre, cosine, sine, kgain, grad_query, grad_gate, normed = refs[:9]
    qk, og = refs[9:13], refs[13:17]
    grad_qk, parts, key_gain, input_gain, total = refs[17:19], refs[19:27], refs[27], refs[28], refs[29]
    pair = own_pair[...].astype(jnp.float32) + got_pair[...].astype(jnp.float32)
    grad_unit = turned_back(
        pair[:, :HEAD_WIDTH].astype(jnp.bfloat16).astype(jnp.float32), cosine[...], sine[...]
    )
    pre = key_pre[...]
    inverse = lax.rsqrt(jnp.mean(pre * pre, axis=1, keepdims=True) + epsilon)
    key_gain[...] = jnp.sum(grad_unit * (pre * inverse), axis=0, keepdims=True)
    grad_key = norm_back(grad_unit, pre, inverse, kgain[...]).astype(jnp.bfloat16)
    grad_value = pair[:, HEAD_WIDTH:].astype(jnp.bfloat16)
    swapped = flag[0] == 1
    for side in range(2):
        grad_qk[side][:, :HEAD_WIDTH] = grad_query[side]
        first, second = (grad_key, grad_value) if side == 0 else (grad_value, grad_key)
        grad_qk[side][:, HEAD_WIDTH:] = jnp.where(swapped, second, first)
    half = total.shape[1] // 2
    tile = total.shape[0] // 2

    def step(i, carry):
        rows_at = pl.ds(pl.multiple_of(i * tile, tile), tile)
        for near in range(2):
            acc = None
            for side in range(2):
                part = contract_last(grad_qk[side][rows_at, :], qk[2 * side + near][...])
                part = part + contract_last(
                    grad_gate[side, rows_at, :], og[2 * side + near][:, :HEAD_WIDTH]
                )
                acc = part if acc is None else acc + part
            total[rows_at, near * half : (near + 1) * half] = acc
        return carry

    lax.fori_loop(0, 2, step, 0)
    rows = parts[0].shape[0]
    gain = jnp.zeros(input_gain.shape, jnp.float32)
    for i in range(8):
        part = total[i * rows : (i + 1) * rows, :]
        parts[i][...] = part.astype(jnp.bfloat16)
        gain = gain + jnp.sum(
            part * normed[i * rows : (i + 1) * rows, :].astype(jnp.float32), axis=0, keepdims=True
        )
    input_gain[...] = gain


def on_slice_device(
    hidden_in,
    out_cotangent,
    doc_lengths,
    query_weight,
    key_matrix,
    value_matrix,
    gate_weight,
    out_weight,
    ffn_gate_weight,
    ffn_up_weight,
    ffn_down_weight,
    attn_gain,
    ffn_gain,
    query_gain,
    key_gain,
):
    bf16, f32 = jnp.bfloat16, jnp.float32
    block_rows, width = hidden_in.shape
    chunk_rows = block_rows // 4
    tokens = 8 * chunk_rows
    low = HEAD_WIDTH
    units = ffn_gate_weight.shape[1] // PLANES
    coords = [lax.axis_index(name) for name in ("far", "near", "x", "y", "c")]
    far, near, x, y, c = coords
    odd_near = near == 1
    core_flag = c.reshape(1)

    def columns(x_at, head):
        at = (2 * x_at + head) * low
        third = (key_matrix if head == 0 else value_matrix)[:, x_at * low : (x_at + 1) * low]
        parts = (query_weight[:, at : at + low], third)
        parts += (gate_weight[:, at : at + low], out_weight[:, at : at + low])
        return jnp.concatenate(parts, axis=1)

    own_hidden = to_own_first(
        lax.dynamic_slice_in_dim(hidden_in, (y * 2 + c) * chunk_rows, chunk_rows, 0), odd_near
    )
    hidden = gather_chunks(own_hidden)
    attn_half, attn_sent = to_head_owners(
        jnp.stack([jnp.stack([columns(i, j) for j in range(2)]) for i in range(2)]), far, x, c
    )
    qk_half, og_half = attn_half[:, : 2 * low], attn_half[:, 2 * low :]
    qk_near = pair_swap(qk_half, "near")
    og_near = pair_swap(after(og_half, qk_near), "near")
    qk = [qk_half, qk_near, pair_swap(qk_half, "c"), pair_swap(after(qk_near, hidden), "c")]
    gain_one = to_own_first(attn_gain, odd_near)
    out_cotangent, ffn_gain = after((out_cotangent, ffn_gain), hidden[1])
    cotangent = to_own_first(
        lax.dynamic_slice_in_dim(out_cotangent, (y * 2 + c) * chunk_rows, chunk_rows, 0), odd_near
    )
    gain_two = to_own_first(ffn_gain, odd_near)
    cotangent_far = pair_swap(cotangent, "far")
    hidden, cotangent_far = after((hidden, cotangent_far))
    ffn_gate_weight, ffn_up_weight, ffn_down_weight = after(
        (ffn_gate_weight, ffn_up_weight, ffn_down_weight), qk_near, hidden, cotangent_far
    )
    cotangent_pair = jnp.concatenate([cotangent, cotangent_far], axis=0)
    cotangents = [cotangent_pair] + [side_swap(cotangent_pair, i) for i in range(1, 4)]

    def by_plane(*weights):
        return jnp.stack(
            [
                jnp.concatenate([w[:, p * units : (p + 1) * units] for w in weights], axis=1)
                for p in range(PLANES)
            ]
        )

    gate_up_half = to_plane_owners(by_plane(ffn_gate_weight, ffn_up_weight))

    half_width = low // 2
    frequency = rope_base ** (-2.0 * jnp.arange(half_width, dtype=f32) / low)
    frequency = jnp.concatenate([frequency, frequency])[None, :]
    bounds, key_ids, angles = pl.pallas_call(
        tables_kernel,
        out_shape=[
            shaped((tokens, low), jnp.int32),
            shaped((1, 4 * tokens), jnp.int32),
            shaped((tokens, low), f32),
        ],
        in_specs=[pl.BlockSpec(memory_space=pltpu.SMEM)] * 2
        + [pl.BlockSpec(memory_space=pltpu.VMEM)],
        out_specs=[pl.BlockSpec(memory_space=pltpu.VMEM)] * 3,
    )(after(doc_lengths, qk_near), jnp.stack(coords), frequency)
    sign = jnp.where(jnp.arange(low) < half_width, -1.0, 1.0).astype(f32)
    cosine, sine = jnp.cos(angles), jnp.sin(angles) * sign[None, :]
    query_gain, key_gain = query_gain[None, :], key_gain[None, :]

    normed, pair, query_rot, query_pre, key_pre = kernel_call(
        project_kernel,
        hidden + [gain_one[None, :]] + qk + [cosine, sine, query_gain, key_gain],
        [
            shaped((tokens, width), bf16),
            shaped((tokens, 2 * low), bf16),
            shaped((2, tokens, low), bf16),
            shaped((2, tokens, low), f32),
            shaped((tokens, low), f32),
        ],
        [pltpu.VMEM((2, tokens, 2 * low), f32)],
        core_flag,
        4 * tokens * width * 2 * low,
    )
    pair_near = pair_swap(pair, "near")
    pairs = [pair, pair_near, pair_swap(pair, "c"), pair_swap(pair_near, "c")]

    og = [og_half, og_near] + [pair_swap(after(part, pair), "c") for part in (og_half, og_near)]
    gate_up_near = pair_swap(after(gate_up_half, pair_near), "near")
    down_half = to_plane_owners(after(by_plane(ffn_down_weight), gate_up_half))
    query_rot, cotangents, gate_up_half = after((query_rot, cotangents, gate_up_half))

    (gate_pre,) = kernel_call(
        gate_kernel,
        [normed] + og,
        [shaped((2, tokens, low), f32)],
        flops=4 * tokens * width * low,
    )
    outs = kernel_call(
        attend_kernel,
        [query_rot] + pairs + [bounds, key_ids, gate_pre] + og,
        [shaped((2, tokens, low), bf16)]
        + [shaped((2, tokens, low), f32)] * 2
        + [shaped((chunk_rows, width), bf16)] * 8,
        [pltpu.VMEM((tokens, width), f32)],
        None,
        8 * tokens * 4 * tokens * low,
    )
    gated, attended, log_total, branch_parts = outs[0], outs[1], outs[2], outs[3:]
    away, own = sum_sends(branch_parts)
    away, gate_up_near, down_half = after((sum_pieces(away).astype(bf16), gate_up_near, down_half))
    hidden32 = own_hidden.astype(f32)
    middle = hidden32 + sum_pieces(own + [pair_swap(away, "far")])
    inv_two = lax.rsqrt(jnp.mean(middle * middle, axis=1, keepdims=True) + epsilon)
    normed_two_chunk = (middle * inv_two * gain_two).astype(bf16)
    normed_two_pieces = gather_chunks(normed_two_chunk)
    gate_up = [
        gate_up_half,
        gate_up_near,
        pair_swap(gate_up_half, "c"),
        pair_swap(gate_up_near, "c"),
    ]
    down_near = pair_swap(after(down_half, gate_up_near), "near")
    down = [down_half, down_near, pair_swap(down_half, "c"), pair_swap(down_near, "c")]

    outs = kernel_call(
        ffn_kernel,
        normed_two_pieces + cotangents + gate_up + down,
        [shaped((tokens, units), bf16)] * 2
        + [shaped((tokens, 2 * units), bf16)] * 2
        + [shaped((chunk_rows, width), bf16)] * 8,
        [pltpu.VMEM((tokens, width), bf16)] * 2
        + [pltpu.VMEM((tokens, width), f32)]
        + [pltpu.VMEM((width // 2, 2 * units), bf16)] * 4
        + [pltpu.VMEM((width // 2, units), bf16)] * 4
        + [pltpu.SemaphoreType.DMA((8,))],
        None,
        20 * tokens * width * units,
        8,
    )
    hidden_acts, grad_ffn, two_parts = outs[:2], outs[2:4], outs[4:12]
    away, own = sum_sends(two_parts)
    two_far = pair_swap(sum_pieces(away).astype(bf16), "far")
    pieces_late, hidden_acts, grad_ffn, cotangents = after(
        (normed_two_pieces, hidden_acts, grad_ffn, cotangents), two_parts[1]
    )
    normed_two = jnp.concatenate(pieces_late, axis=0)
    all_cotangent = jnp.concatenate(cotangents, axis=0)
    down_parts = kernel_call(
        down_kernel,
        list(hidden_acts) + list(down),
        [shaped((2 * chunk_rows, width), bf16)] * 4,
        [pltpu.VMEM((tokens, width), f32)],
        None,
        4 * tokens * width * units,
    )
    two_away = own, two_far
    gate_up_both = core_sum(*(contract_first(normed_two, g).astype(bf16) for g in grad_ffn))
    down_both = core_sum(*(contract_first(all_cotangent, act).astype(bf16) for act in hidden_acts))

    (own, two_far), down_both, gate_up_both = after((two_away, down_both, gate_up_both))
    grad_normed_two = sum_pieces(own + [two_far])

    def whole_block(chunk):
        chunk = from_own_first(chunk, odd_near)
        other = pair_swap(chunk, "y")
        by_y = jnp.stack([chunk, other])
        by_core = jnp.stack([by_y, pair_swap(by_y, "c")], axis=1)
        whole = flip_if(flip_if(by_core, 1, c == 1), 0, y == 1).reshape(block_rows, width)
        return other, whole

    grad_middle = cotangent.astype(f32) + norm_back(grad_normed_two, middle, inv_two, gain_two)
    grad_branch = grad_middle.astype(bf16)
    branch_pieces = gather_chunks(grad_branch)
    down_parts = after(down_parts, branch_pieces)
    down_pieces = [down_parts[0]] + [side_swap(down_parts[i], i) for i in range(1, 4)]
    half = width // 2
    gate_up_got = pair_swap(gate_up_both[half:], "near")

    all_branch, grad_gate, grad_query, grad_pairs, query_gain_part = kernel_call(
        attend_back_kernel,
        branch_pieces
        + og
        + pairs
        + [bounds, key_ids, query_rot, query_pre, gate_pre, attended, log_total]
        + [cosine, sine, query_gain],
        [
            shaped((tokens, width), bf16),
            shaped((2, tokens, low), bf16),
            shaped((2, tokens, low), bf16),
            shaped((4 * tokens, 2 * low), bf16),
            shaped((1, low), f32),
        ],
        [
            pltpu.VMEM((2, tokens, low), f32),
            pltpu.VMEM((4 * tokens, low), f32),
            pltpu.VMEM((4 * tokens, low), f32),
        ],
        None,
        20 * tokens * 4 * tokens * low,
    )
    pair_other = pair_swap(grad_pairs[2 * tokens :], "c")
    gate_up_got, normed_later = after((gate_up_got, normed), grad_pairs)
    near_pairs = grad_pairs[: 2 * tokens].astype(f32) + pair_other.astype(f32)
    near_pairs = near_pairs.astype(bf16)
    pair_got = pair_swap(near_pairs[tokens:], "near")
    gate_up_rows = near_add(gate_up_both, gate_up_got)
    down_got = pair_swap(after(down_both, pair_got)[half:], "near")
    gate_up_grad = to_row_owners(gate_up_rows)
    og_both = core_sum(
        *(
            jnp.concatenate(
                [
                    contract_first(normed_later, grad_gate[i]).astype(bf16),
                    contract_first(all_branch, gated[i]).astype(bf16),
                ],
                axis=1,
            )
            for i in range(2)
        )
    )
    key_pre, gate_up_rows, down_pieces = after((key_pre, gate_up_rows, down_pieces))
    og_got = pair_swap(after(og_both, pair_got)[half:], "near")
    outs = kernel_call(
        input_kernel,
        [near_pairs[:tokens], pair_got, key_pre, cosine, sine, key_gain]
        + [grad_query, grad_gate, normed]
        + qk
        + og,
        [shaped((tokens, 2 * low), bf16)] * 2
        + [shaped((chunk_rows, width), bf16)] * 8
        + [shaped((1, low), f32), shaped((1, width), f32)],
        [pltpu.VMEM((tokens, width), f32)],
        core_flag,
        12 * tokens * width * low,
    )
    grad_qk, normed_parts, key_gain_part, input_gain_part = outs[:2], outs[2:10], outs[10], outs[11]
    away, own = sum_sends(normed_parts)
    away = sum_pieces(away).astype(bf16)
    qk_sides = [contract_first(normed, g).astype(bf16) for g in after(grad_qk, normed_parts[1])]
    qk_other = pair_swap(qk_sides[1], "c")
    away, qk_other, gate_up_grad = after((away, qk_other, gate_up_grad))
    qk_both = (qk_sides[0].astype(f32) + qk_other.astype(f32)).astype(bf16)
    qk_got = pair_swap(qk_both[half:], "near")
    grad_far = pair_swap(away, "far")
    grad_far, down_got = after((grad_far, down_got))
    down_pieces = after(down_pieces, grad_far)
    down_sums = sum_pieces(down_pieces)
    down_far = pair_swap(down_sums[chunk_rows:].astype(bf16), "far")
    down_rows = near_add(down_both, down_got)
    grad_far, qk_got = after((grad_far, qk_got))
    grad_normed = sum_pieces(own + [grad_far])
    inv_one = lax.rsqrt(jnp.mean(hidden32 * hidden32, axis=1, keepdims=True) + epsilon)
    input_chunk = (grad_middle + norm_back(grad_normed, hidden32, inv_one, gain_one)).astype(bf16)
    input_y, input_grad = whole_block(input_chunk)
    og_got = after(og_got, grad_far)
    gain_parts = after((input_gain_part, query_gain_part, key_gain_part), input_y)
    down_far = after(down_far, grad_far)
    attn_rows = jnp.concatenate([near_add(qk_both, qk_got), near_add(og_both, og_got)], axis=1)
    attn_grad = from_head_owners(attn_rows, far, x, c)
    down_grad = to_row_owners(after(down_rows, grad_far, gate_up_grad))
    qk_grad, og_grad = attn_grad[..., : 2 * low], attn_grad[..., 2 * low :]
    layer_y, layer_out = whole_block(
        (middle + down_sums[:chunk_rows] + down_far.astype(f32)).astype(bf16)
    )
    gains = jnp.concatenate(
        [
            from_own_first(gain_parts[0][0] / gain_one, odd_near),
            from_own_first(jnp.sum(grad_normed_two * middle * inv_two, axis=0), odd_near),
            gain_parts[1][0],
            gain_parts[2][0],
        ]
    )
    gains = (gains + plane_swap(gains, 1)) + (plane_swap(gains, 2) + plane_swap(gains, 3))
    for axis in ("y", "c", "near"):
        gains = gains + pair_swap(gains, axis)

    def per_head(grad, start):
        columns = [grad[i, j, :, start : start + low] for i in range(2) for j in range(2)]
        return jnp.concatenate(columns, axis=1).astype(f32)

    def per_group(grad, j):
        return jnp.concatenate([grad[0, j, :, low:], grad[1, j, :, low:]], axis=1).astype(f32)

    def flat(grad):
        return jnp.concatenate([grad[p] for p in range(PLANES)], axis=1).astype(f32)

    return (
        layer_out,
        input_grad,
        per_head(qk_grad, 0),
        per_group(qk_grad, 0),
        per_group(qk_grad, 1),
        per_head(og_grad, 0),
        per_head(og_grad, low),
        flat(gate_up_grad[:, :, :units]),
        flat(gate_up_grad[:, :, units:]),
        flat(down_grad),
        gains[:width],
        gains[width : 2 * width],
        gains[2 * width : 2 * width + low],
        gains[2 * width + low :],
    )


def solution(mesh):
    wide, head = mesh.shape["wide"], mesh.shape["head"]
    if wide == 2 * PLANES and head == 4:
        devices = mesh.devices.reshape(2, 2, 2, 2, 2)
        mesh = Mesh(devices, ("far", "near", "x", "y", "c"))
        program, rows, columns = on_slice_device, ("far", "near", "x"), ("y", "c")
    else:
        program, rows, columns = on_device, "wide", "head"
    tokens, weight = P(rows, None), P(rows, columns)
    return jax.shard_map(
        program,
        mesh=mesh,
        in_specs=(tokens, tokens, P()) + (weight,) * 8 + (P(),) * 4,
        out_specs=(tokens, tokens) + (weight,) * 8 + (P(),) * 4,
        check_vma=False,
    )
```

```python
import jax
import jax.numpy as jnp
from jax import lax
from jax.experimental import pallas as pl
from jax.experimental.pallas import tpu as pltpu
from jax.sharding import Mesh
from jax.sharding import PartitionSpec as P

HEAD_WIDTH = 128


epsilon = 1e-06
rope_base = 1000000.0
masked_score = -1e30


def segment_of(lengths, token_ids):
    doc_ends = jnp.cumsum(lengths)
    return jnp.sum((token_ids[:, None] >= doc_ends[None, :]).astype(jnp.int32), axis=1)


def doc_tables(lengths, token_ids):
    doc_ends = jnp.cumsum(lengths)
    starts = doc_ends - lengths
    segment = segment_of(lengths, token_ids)
    labels = jnp.arange(lengths.shape[0], dtype=jnp.int32)
    doc_begin = jnp.sum(jnp.where(segment[:, None] == labels[None, :], starts[None, :], 0), axis=1)
    return (segment, token_ids - doc_begin)


def rope_tables(positions, head_size):
    half_size = head_size // 2
    frequency = rope_base ** (-2.0 * jnp.arange(half_size, dtype=jnp.float32) / head_size)
    angles = positions.astype(jnp.float32)[:, None] * frequency[None, :]
    cosine = jnp.cos(angles)
    sine_table = jnp.sin(angles)
    return (
        jnp.concatenate([cosine, cosine], axis=1),
        jnp.concatenate([sine_table, sine_table], axis=1),
    )


def rotate_half(values):
    half_size = values.shape[-1] // 2
    return jnp.concatenate([-values[..., half_size:], values[..., :half_size]], axis=-1)


def rotate_back(values):
    half_size = values.shape[-1] // 2
    return jnp.concatenate([values[..., half_size:], -values[..., :half_size]], axis=-1)


def apply_rope(values, cos_table, sin_table):
    return values * cos_table[:, None, :] + rotate_half(values) * sin_table[:, None, :]


def rope_back(grads, cos_table, sin_table):
    return grads * cos_table[:, None, :] + rotate_back(grads * sin_table[:, None, :])


def contract_last(left, right):
    return lax.dot_general(
        left, right, (((1,), (1,)), ((), ())), preferred_element_type=jnp.float32
    )


def contract_first(left, right):
    return lax.dot_general(
        left, right, (((0,), (0,)), ((), ())), preferred_element_type=jnp.float32
    )


def norm_back(grad_out, inputs, inv_root, gain):
    scaled = grad_out * gain
    return inv_root * scaled - inputs * inv_root**3 * jnp.mean(
        scaled * inputs, axis=-1, keepdims=True
    )


def on_device(
    hidden_in,
    out_cotangent,
    doc_lengths,
    query_weight,
    key_matrix,
    value_matrix,
    gate_weight,
    out_weight,
    ffn_gate_weight,
    ffn_up_weight,
    ffn_down_weight,
    attn_gain,
    ffn_gain,
    query_gain,
    key_gain,
):
    tok_rows = hidden_in.shape[0]
    row_length = tok_rows * lax.axis_size("wide")
    first_row = lax.axis_index("wide") * tok_rows
    token_ids = first_row + jnp.arange(tok_rows, dtype=jnp.int32)
    segment, positions = doc_tables(doc_lengths, token_ids)
    shard_begin = first_row - positions[0]
    shard_last = first_row + tok_rows - 1
    cos_table, sin_table = rope_tables(positions, HEAD_WIDTH)
    local_heads = query_weight.shape[1] // HEAD_WIDTH
    kv_heads = key_matrix.shape[1] // HEAD_WIDTH
    group_width = local_heads // kv_heads
    query_rows = group_width * tok_rows
    score_scale = HEAD_WIDTH ** (-0.5)
    (
        full_query,
        full_key,
        full_value,
        full_gate,
        full_out,
        full_ffn_gate,
        full_ffn_up,
        full_ffn_down,
    ) = (
        lax.all_gather(query_weight, "wide", axis=0, tiled=True),
        lax.all_gather(key_matrix, "wide", axis=0, tiled=True),
        lax.all_gather(value_matrix, "wide", axis=0, tiled=True),
        lax.all_gather(gate_weight, "wide", axis=0, tiled=True),
        lax.all_gather(out_weight, "wide", axis=0, tiled=True),
        lax.all_gather(ffn_gate_weight, "wide", axis=0, tiled=True),
        lax.all_gather(ffn_up_weight, "wide", axis=0, tiled=True),
        lax.all_gather(ffn_down_weight, "wide", axis=0, tiled=True),
    )
    hidden32 = hidden_in.astype(jnp.float32)
    inv_one = lax.rsqrt(jnp.mean(hidden32 * hidden32, axis=1, keepdims=True) + epsilon)
    normed_input = (hidden32 * inv_one * attn_gain).astype(jnp.bfloat16)
    query_pre = jnp.dot(normed_input, full_query, preferred_element_type=jnp.float32).reshape(
        tok_rows, local_heads, HEAD_WIDTH
    )
    key_before_norm = jnp.dot(normed_input, full_key, preferred_element_type=jnp.float32).reshape(
        tok_rows, kv_heads, HEAD_WIDTH
    )
    value_rows = jnp.dot(normed_input, full_value, preferred_element_type=jnp.float32).astype(
        jnp.bfloat16
    )
    gate_pre = jnp.dot(normed_input, full_gate, preferred_element_type=jnp.float32)
    inv_query = lax.rsqrt(jnp.mean(query_pre * query_pre, axis=-1, keepdims=True) + epsilon)
    inv_key = lax.rsqrt(
        jnp.mean(key_before_norm * key_before_norm, axis=-1, keepdims=True) + epsilon
    )
    query_unit = query_pre * inv_query
    key_unit = key_before_norm * inv_key
    query_rot = apply_rope(query_unit * query_gain, cos_table, sin_table).astype(jnp.bfloat16)
    key_rows = (
        apply_rope(key_unit * key_gain, cos_table, sin_table)
        .astype(jnp.bfloat16)
        .reshape(tok_rows, kv_heads * HEAD_WIDTH)
    )
    query_heads = (
        query_rot.reshape(tok_rows, kv_heads, group_width, HEAD_WIDTH)
        .transpose(1, 2, 0, 3)
        .reshape(kv_heads, query_rows, HEAD_WIDTH)
    )
    query_seg = jnp.tile(segment, group_width)
    query_ids = jnp.tile(token_ids, group_width)
    start_state = (
        jnp.full((kv_heads, query_rows), masked_score, jnp.float32),
        jnp.zeros((kv_heads, query_rows), jnp.float32),
        jnp.zeros((kv_heads, query_rows, HEAD_WIDTH), jnp.float32),
    )
    key_piece = lax.all_gather(key_rows, "wide", axis=0, tiled=True)
    value_piece = lax.all_gather(value_rows, "wide", axis=0, tiled=True)
    count = key_piece.shape[0]
    step_rows = 512
    steps_count = count // step_rows
    key_ids = jnp.arange(count, dtype=jnp.int32)
    key_seg = segment_of(doc_lengths, key_ids)
    key_blocks = key_piece.reshape(steps_count, step_rows, kv_heads, HEAD_WIDTH).transpose(
        0, 2, 1, 3
    )
    value_blocks = value_piece.reshape(steps_count, step_rows, kv_heads, HEAD_WIDTH).transpose(
        0, 2, 1, 3
    )

    def inner(state, block):
        key_block, value_block, block_seg, block_ids = block

        def inner_work(state_in):
            scores = (
                jnp.einsum(
                    "hqd,hkd->hqk", query_heads, key_block, preferred_element_type=jnp.float32
                )
                * score_scale
            )
            allowed = (
                (query_seg[:, None] == block_seg[None, :])
                & (block_ids[None, :] <= query_ids[:, None])
            )[None]
            scores = jnp.where(allowed, scores, masked_score)
            running, total, accum = state_in
            newest = jnp.maximum(running, jnp.max(scores, axis=-1))
            factor = jnp.exp(running - newest)
            weights = jnp.where(allowed, jnp.exp(scores - newest[..., None]), 0.0)
            total = total * factor + jnp.sum(weights, axis=-1)
            accum = accum * factor[..., None] + jnp.einsum(
                "hqk,hkd->hqd",
                weights.astype(jnp.bfloat16),
                value_block,
                preferred_element_type=jnp.float32,
            )
            return (newest, total, accum)

        useful = (block_ids[0] <= shard_last) & (block_ids[step_rows - 1] >= shard_begin)
        return (lax.cond(useful, inner_work, lambda state_in: state_in, state), None)

    state, unused = lax.scan(
        inner,
        start_state,
        (
            key_blocks,
            value_blocks,
            key_seg.reshape(steps_count, step_rows),
            key_ids.reshape(steps_count, step_rows),
        ),
    )
    running, total, accum = state
    attended_heads = accum / total[..., None]
    log_total = running + jnp.log(total)
    attended = (
        attended_heads.reshape(kv_heads, group_width, tok_rows, HEAD_WIDTH)
        .transpose(2, 0, 1, 3)
        .reshape(tok_rows, local_heads * HEAD_WIDTH)
    )
    gate_sig = jax.nn.sigmoid(gate_pre)
    gated = (attended * gate_sig).astype(jnp.bfloat16)
    branch = lax.psum(contract_last(gated, full_out).astype(jnp.bfloat16), "head").astype(
        jnp.float32
    )
    middle = hidden32 + branch
    inv_two = lax.rsqrt(jnp.mean(middle * middle, axis=1, keepdims=True) + epsilon)
    normed_two = (middle * inv_two * ffn_gain).astype(jnp.bfloat16)
    ffn_gate_pre = jnp.dot(normed_two, full_ffn_gate, preferred_element_type=jnp.float32)
    ffn_up_pre = jnp.dot(normed_two, full_ffn_up, preferred_element_type=jnp.float32)
    gate_act = jax.nn.sigmoid(ffn_gate_pre)
    silu_gate = ffn_gate_pre * gate_act
    hidden_act = (silu_gate * ffn_up_pre).astype(jnp.bfloat16)
    ffn_out = lax.psum(
        contract_last(hidden_act, full_ffn_down).astype(jnp.bfloat16), "head"
    ).astype(jnp.float32)
    layer_out = (middle + ffn_out).astype(jnp.bfloat16)
    grad32 = out_cotangent.astype(jnp.float32)
    grad_hidden = jnp.dot(out_cotangent, full_ffn_down, preferred_element_type=jnp.float32)
    grad_ffn_gate = (
        grad_hidden * ffn_up_pre * gate_act * (1.0 + ffn_gate_pre * (1.0 - gate_act))
    ).astype(jnp.bfloat16)
    grad_ffn_up = (grad_hidden * silu_gate).astype(jnp.bfloat16)
    grad_normed_two = lax.psum(
        (
            contract_last(grad_ffn_gate, full_ffn_gate) + contract_last(grad_ffn_up, full_ffn_up)
        ).astype(jnp.bfloat16),
        "head",
    ).astype(jnp.float32)
    grad_middle = grad32 + norm_back(grad_normed_two, middle, inv_two, ffn_gain)
    grad_branch = grad_middle.astype(jnp.bfloat16)
    grad_gated = jnp.dot(grad_branch, full_out, preferred_element_type=jnp.float32)
    grad_attended = (grad_gated * gate_sig).astype(jnp.bfloat16)
    grad_gate_pre = (grad_gated * attended * gate_sig * (1.0 - gate_sig)).astype(jnp.bfloat16)
    grad_heads = (
        grad_attended.reshape(tok_rows, kv_heads, group_width, HEAD_WIDTH)
        .transpose(1, 2, 0, 3)
        .reshape(kv_heads, query_rows, HEAD_WIDTH)
    )
    delta = jnp.sum(grad_heads.astype(jnp.float32) * attended_heads, axis=-1)
    all_keys, all_values = key_piece, value_piece
    key_step = 512
    key_count = row_length // key_step
    all_ids = jnp.arange(row_length, dtype=jnp.int32)
    all_seg = segment_of(doc_lengths, all_ids)
    key_blocks = all_keys.reshape(key_count, key_step, kv_heads, HEAD_WIDTH).transpose(0, 2, 1, 3)
    value_blocks = all_values.reshape(key_count, key_step, kv_heads, HEAD_WIDTH).transpose(
        0, 2, 1, 3
    )
    key_scan_items = (
        key_blocks,
        value_blocks,
        all_seg.reshape(key_count, key_step),
        all_ids.reshape(key_count, key_step),
    )
    zero_query = jnp.zeros((kv_heads, query_rows, HEAD_WIDTH), jnp.float32)

    def block_terms(key_block, value_block, block_seg, block_ids):
        scores = (
            jnp.einsum("hqd,hkd->hqk", query_heads, key_block, preferred_element_type=jnp.float32)
            * score_scale
        )
        allowed = (
            (query_seg[:, None] == block_seg[None, :]) & (block_ids[None, :] <= query_ids[:, None])
        )[None]
        weights = jnp.where(
            allowed, jnp.exp(jnp.where(allowed, scores, masked_score) - log_total[..., None]), 0.0
        )
        grad_weights = jnp.einsum(
            "hqd,hkd->hqk", grad_heads, value_block, preferred_element_type=jnp.float32
        )
        grad_scores = (weights * (grad_weights - delta[..., None])).astype(jnp.bfloat16)
        return (weights, grad_scores)

    def block_useful(block_ids):
        return (block_ids[0] <= shard_last) & (block_ids[key_step - 1] >= shard_begin)

    def back_block(grad_query, block):
        key_block, value_block, block_seg, block_ids = block

        def back_work(grad_in):
            weights, grad_scores = block_terms(key_block, value_block, block_seg, block_ids)
            grad_out = (
                grad_in
                + jnp.einsum(
                    "hqk,hkd->hqd", grad_scores, key_block, preferred_element_type=jnp.float32
                )
                * score_scale
            )
            grad_key = (
                jnp.einsum(
                    "hqk,hqd->hkd", grad_scores, query_heads, preferred_element_type=jnp.float32
                )
                * score_scale
            )
            grad_value = jnp.einsum(
                "hqk,hqd->hkd",
                weights.astype(jnp.bfloat16),
                grad_heads,
                preferred_element_type=jnp.float32,
            )
            return (grad_out, (grad_key, grad_value))

        def skip(grad_in):
            nothing = jnp.zeros((kv_heads, key_step, HEAD_WIDTH), jnp.float32)
            return (grad_in, (nothing, nothing))

        return lax.cond(block_useful(block_ids), back_work, skip, grad_query)

    grad_query, (key_parts, value_parts) = lax.scan(back_block, zero_query, key_scan_items)
    key_grad_rows = key_parts.transpose(0, 2, 1, 3).reshape(row_length, kv_heads * HEAD_WIDTH)
    value_grad_rows = value_parts.transpose(0, 2, 1, 3).reshape(row_length, kv_heads * HEAD_WIDTH)
    key_total, value_total = (
        lax.psum_scatter(
            key_grad_rows.astype(jnp.bfloat16), "wide", scatter_dimension=0, tiled=True
        ).astype(jnp.float32),
        lax.psum_scatter(
            value_grad_rows.astype(jnp.bfloat16), "wide", scatter_dimension=0, tiled=True
        ).astype(jnp.float32),
    )
    grad_values = value_total.astype(jnp.bfloat16)
    grad_key_rot = (
        key_total.astype(jnp.bfloat16).astype(jnp.float32).reshape(tok_rows, kv_heads, HEAD_WIDTH)
    )
    grad_query_rot = (
        grad_query.astype(jnp.bfloat16)
        .astype(jnp.float32)
        .reshape(kv_heads, group_width, tok_rows, HEAD_WIDTH)
        .transpose(2, 0, 1, 3)
        .reshape(tok_rows, local_heads, HEAD_WIDTH)
    )
    grad_query_unit = rope_back(grad_query_rot, cos_table, sin_table)
    grad_key_unit = rope_back(grad_key_rot, cos_table, sin_table)
    query_gain_part = jnp.sum(grad_query_unit * query_unit, axis=(0, 1))
    key_gain_part = jnp.sum(grad_key_unit * key_unit, axis=(0, 1))
    grad_query_pre = (
        norm_back(grad_query_unit, query_pre, inv_query, query_gain)
        .reshape(tok_rows, local_heads * HEAD_WIDTH)
        .astype(jnp.bfloat16)
    )
    grad_key_pre = (
        norm_back(grad_key_unit, key_before_norm, inv_key, key_gain)
        .reshape(tok_rows, kv_heads * HEAD_WIDTH)
        .astype(jnp.bfloat16)
    )
    grad_normed_part = (
        contract_last(grad_query_pre, full_query)
        + contract_last(grad_key_pre, full_key)
        + contract_last(grad_values, full_value)
        + contract_last(grad_gate_pre, full_gate)
    )
    grad_normed = lax.psum(grad_normed_part.astype(jnp.bfloat16), "head").astype(jnp.float32)
    input_grad = (grad_middle + norm_back(grad_normed, hidden32, inv_one, attn_gain)).astype(
        jnp.bfloat16
    )
    attn_gain_part = jnp.sum(grad_normed * hidden32 * inv_one, axis=0)
    ffn_gain_part = jnp.sum(grad_normed_two * middle * inv_two, axis=0)
    weight_grads = lax.psum_scatter(
        jnp.concatenate(
            [
                contract_first(normed_input, grad_query_pre),
                contract_first(normed_input, grad_key_pre),
                contract_first(normed_input, grad_values),
                contract_first(normed_input, grad_gate_pre),
                contract_first(grad_branch, gated),
                contract_first(normed_two, grad_ffn_gate),
                contract_first(normed_two, grad_ffn_up),
                contract_first(out_cotangent, hidden_act),
            ],
            axis=1,
        ).astype(jnp.bfloat16),
        "wide",
        scatter_dimension=0,
        tiled=True,
    ).astype(jnp.float32)
    col_widths = [
        query_weight.shape[1],
        key_matrix.shape[1],
        value_matrix.shape[1],
        gate_weight.shape[1],
        out_weight.shape[1],
        ffn_gate_weight.shape[1],
        ffn_up_weight.shape[1],
        ffn_down_weight.shape[1],
    ]
    pieces = []
    offset = 0
    for width in col_widths:
        pieces.append(weight_grads[:, offset : offset + width])
        offset = offset + width
    head_first = (lax.axis_index("head") == 0).astype(jnp.float32)
    attn_gain_grad, ffn_gain_grad, query_gain_grad, key_gain_grad = lax.psum(
        (attn_gain_part * head_first, ffn_gain_part * head_first, query_gain_part, key_gain_part),
        ("wide", "head"),
    )
    return (
        layer_out,
        input_grad,
        pieces[0],
        pieces[1],
        pieces[2],
        pieces[3],
        pieces[4],
        pieces[5],
        pieces[6],
        pieces[7],
        attn_gain_grad,
        ffn_gain_grad,
        query_gain_grad,
        key_gain_grad,
    )


PLANES = 4
PLANE = ("far", "x")


def pair_swap(values, axis):
    return lax.ppermute(values, axis, [(0, 1), (1, 0)])


def plane_swap(values, step):
    return lax.ppermute(values, PLANE, [(i, i ^ step) for i in range(PLANES)])


def side_swap(values, step):
    return lax.ppermute(values, ("x", "y"), [(i, i ^ step) for i in range(4)])


def after(values, *done):
    return lax.optimization_barrier((values, done))[0]


def gather_chunks(chunk):
    far = pair_swap(chunk, "far")
    near = [side_swap(chunk, step) for step in range(1, 4)]
    away = [side_swap(far, step) for step in range(1, 4)]
    pieces = [chunk, far]
    for pair in zip(near, away):
        pieces.extend(pair)
    return pieces


def sum_sends(parts):
    return [
        [parts[far]] + [side_swap(parts[2 * step + far], step) for step in range(1, 4)]
        for far in (1, 0)
    ]


def sum_pieces(pieces):
    total = pieces[0].astype(jnp.float32)
    for piece in pieces[1:]:
        total = total + piece.astype(jnp.float32)
    return total


def flip_if(values, axis, flag):
    return jnp.where(flag, jnp.flip(values, axis), values)


def to_own_first(values, flag):
    lead = values.shape[:-1]
    width = values.shape[-1]
    split = values.reshape(lead + (2, 2, width // 4))
    zero = split[..., 0, :].reshape(lead + (width // 2,))
    one = split[..., 1, :].reshape(lead + (width // 2,))
    return jnp.concatenate([jnp.where(flag, one, zero), jnp.where(flag, zero, one)], axis=-1)


def from_own_first(values, flag):
    lead = values.shape[:-1]
    width = values.shape[-1]
    own = values[..., : width // 2].reshape(lead + (2, width // 4))
    other = values[..., width // 2 :].reshape(lead + (2, width // 4))
    pair = jnp.stack([jnp.where(flag, other, own), jnp.where(flag, own, other)], axis=-2)
    return pair.reshape(lead + (width,))


def to_plane_owners(local):
    planes, rows, width = local.shape
    return lax.all_to_all(
        local.reshape(planes * rows, width), PLANE, split_axis=0, concat_axis=0, tiled=True
    )


HEADS = ("far", "x", "c")


def head_pairs(a, b, back):
    pairs = []
    for f in range(2):
        for x in range(2):
            for c in range(2):
                pairs.append((4 * f + 2 * x + c, 4 * c + 2 * (x ^ a) + (f ^ b)))
    return [(j, i) for i, j in pairs] if back else pairs


def to_head_owners(columns, far, x, c):
    turned = flip_if(flip_if(columns, 0, x == 1), 1, far == 1)
    sent = [
        [lax.ppermute(turned[a, b], HEADS, head_pairs(a, b, False)) for a in range(2)]
        for b in range(2)
    ]
    pieces = jnp.stack([jnp.stack(row) for row in sent])
    rows = flip_if(flip_if(pieces, 0, c == 1), 1, x == 1)
    return rows.reshape(PLANES * columns.shape[2], columns.shape[3]), sent


def from_head_owners(rows, far, x, c):
    blocks = rows.reshape(2, 2, rows.shape[0] // PLANES, rows.shape[1])
    blocks = flip_if(flip_if(blocks, 0, c == 1), 1, x == 1)
    pieces = jnp.stack(
        [
            jnp.stack(
                [lax.ppermute(blocks[b, a], HEADS, head_pairs(a, b, True)) for b in range(2)]
            )
            for a in range(2)
        ]
    )
    return flip_if(flip_if(pieces, 0, x == 1), 1, far == 1)


def core_sum(mine, other):
    both = mine.astype(jnp.float32) + pair_swap(other, "c").astype(jnp.float32)
    return both.astype(jnp.bfloat16)


def near_add(both, got):
    half = both.shape[0] // 2
    return (both[:half].astype(jnp.float32) + got.astype(jnp.float32)).astype(jnp.bfloat16)


def to_row_owners(rows):
    back = lax.all_to_all(rows, PLANE, split_axis=0, concat_axis=0, tiled=True)
    return back.reshape(PLANES, rows.shape[0] // PLANES, rows.shape[1])


VMEM_BYTES = 56 * 1024 * 1024


def kernel_call(body, operands, outs, scratch=(), flags=None, flops=0, far_operands=0):
    specs = [pl.BlockSpec(memory_space=pltpu.VMEM)] * (len(operands) - far_operands)
    specs += [pl.BlockSpec(memory_space=pl.ANY)] * far_operands
    if flags is not None:
        operands = [flags] + list(operands)
        specs = [pl.BlockSpec(memory_space=pltpu.SMEM)] + specs
    moved = sum(v.size * v.dtype.itemsize for v in operands)
    moved += sum(v.size * v.dtype.itemsize for v in outs)
    return pl.pallas_call(
        body,
        out_shape=outs,
        in_specs=specs,
        out_specs=[pl.BlockSpec(memory_space=pltpu.VMEM)] * len(outs),
        scratch_shapes=list(scratch),
        compiler_params=pltpu.CompilerParams(vmem_limit_bytes=VMEM_BYTES),
        cost_estimate=pl.CostEstimate(flops=flops, bytes_accessed=moved, transcendentals=0),
    )(*operands)


def shaped(shape, dtype):
    return jax.ShapeDtypeStruct(shape, dtype)


def dot_nn(left, right):
    return jnp.dot(left, right, preferred_element_type=jnp.float32)


def turned(values, cosine, signed_sine):
    return values * cosine + pltpu.roll(values, HEAD_WIDTH // 2, 1) * signed_sine


def turned_back(grads, cosine, signed_sine):
    return grads * cosine - pltpu.roll(grads, HEAD_WIDTH // 2, 1) * signed_sine


def sigmoid(values):
    return 1.0 / (1.0 + jnp.exp(-values))


def project_kernel(flag, *refs):
    hidden = refs[:8]
    gain, mine_own, mine_near, other_own, other_near, cosine, sine, qgain, kgain = refs[8:17]
    normed, pair, query_rot, query_pre, key_pre, scratch = refs[17:]
    rows = hidden[0].shape[0]
    for i in range(8):
        h = hidden[i][...].astype(jnp.float32)
        inverse = lax.rsqrt(jnp.mean(h * h, axis=1, keepdims=True) + epsilon)
        normed[i * rows : (i + 1) * rows, :] = (h * inverse * gain[...]).astype(jnp.bfloat16)
    half = normed.shape[1] // 2
    left, right = normed[:, :half], normed[:, half:]
    for i, (own, near) in enumerate(((mine_own, mine_near), (other_own, other_near))):
        scratch[i] = dot_nn(left, own[...]) + dot_nn(right, near[...])
    cos, sin = cosine[...], sine[...]
    swapped = flag[0] == 1
    mine, other = scratch[0, :, HEAD_WIDTH:], scratch[1, :, HEAD_WIDTH:]
    pre = jnp.where(swapped, other, mine)
    key_pre[...] = pre
    pair[:, HEAD_WIDTH:] = jnp.where(swapped, mine, other).astype(jnp.bfloat16)
    unit = pre * lax.rsqrt(jnp.mean(pre * pre, axis=1, keepdims=True) + epsilon)
    pair[:, :HEAD_WIDTH] = turned(unit * kgain[...], cos, sin).astype(jnp.bfloat16)
    for i in range(2):
        pre = scratch[i, :, :HEAD_WIDTH]
        query_pre[i] = pre
        unit = pre * lax.rsqrt(jnp.mean(pre * pre, axis=1, keepdims=True) + epsilon)
        query_rot[i] = turned(unit * qgain[...], cos, sin).astype(jnp.bfloat16)


def attend_kernel(query_rot, first, second, third, fourth, bounds, key_ids, gate_pre, *refs):
    outs_w, gated, attended, log_total, parts, total = refs[:4], *refs[4:7], refs[7:15], refs[15]
    scale = HEAD_WIDTH ** (-0.5)
    pairs = (first, second, third, fourth)
    rows = first.shape[0]
    tile = rows // 2

    def step(i, carry):
        head, at = i // 2, pl.multiple_of(i % 2 * tile, tile)
        query = query_rot[head, pl.ds(at, tile), :]
        start, last = bounds[pl.ds(at, tile), 0:1], bounds[pl.ds(at, tile), 1:2]
        scores = []
        for j, pair in enumerate(pairs):
            ids = key_ids[:, j * rows : (j + 1) * rows]
            allowed = (ids >= start) & (ids <= last)
            score = contract_last(query, pair[:, :HEAD_WIDTH]) * scale
            scores.append(jnp.where(allowed, score, masked_score))
        top = jnp.max(scores[0], axis=1, keepdims=True)
        for score in scores[1:]:
            top = jnp.maximum(top, jnp.max(score, axis=1, keepdims=True))
        total = jnp.zeros_like(top)
        result = jnp.zeros((tile, HEAD_WIDTH), jnp.float32)
        for score, pair in zip(scores, pairs):
            raised = jnp.exp(score - top)
            total = total + jnp.sum(raised, axis=1, keepdims=True)
            result = result + dot_nn(raised.astype(jnp.bfloat16), pair[:, HEAD_WIDTH:])
        result = result / total
        attended[head, pl.ds(at, tile), :] = result
        log_total[head, pl.ds(at, tile), :] = jnp.broadcast_to(top + jnp.log(total), result.shape)
        gate = sigmoid(gate_pre[head, pl.ds(at, tile), :])
        gated[head, pl.ds(at, tile), :] = (result * gate).astype(jnp.bfloat16)
        return carry

    lax.fori_loop(0, 4, step, 0)
    half = total.shape[1] // 2
    for near in range(2):
        total[:, near * half : (near + 1) * half] = contract_last(
            gated[0], outs_w[near][:, HEAD_WIDTH:]
        ) + contract_last(gated[1], outs_w[2 + near][:, HEAD_WIDTH:])
    rows = parts[0].shape[0]
    for i in range(8):
        parts[i][...] = total[i * rows : (i + 1) * rows, :].astype(jnp.bfloat16)


def ffn_kernel(*refs):
    chunks, cotangent, gate_up, down = refs[:8], refs[8:12], refs[12:16], refs[16:20]
    acts, grads, two_parts = refs[20:22], refs[22:24], refs[24:32]
    normed_two, cot, total = refs[32:35]
    gate_up_here, down_here, sems = refs[35:39], refs[39:43], refs[43]
    copies = []
    for side in range(2):
        for i in (2 * side, 2 * side + 1):
            copies.append(pltpu.make_async_copy(gate_up[i], gate_up_here[i], sems.at[len(copies)]))
        for i in (2 * side, 2 * side + 1):
            copies.append(pltpu.make_async_copy(down[i], down_here[i], sems.at[len(copies)]))
    for copy in copies:
        copy.start()
    rows = chunks[0].shape[0]
    for i in range(8):
        normed_two[i * rows : (i + 1) * rows, :] = chunks[i][...]
    rows = cotangent[0].shape[0]
    for i in range(4):
        cot[i * rows : (i + 1) * rows, :] = cotangent[i][...]
    half = cot.shape[1] // 2
    units = down_here[0].shape[1]
    tile = cot.shape[0] // 2
    for side in range(2):
        for copy in copies[4 * side : 4 * side + 4]:
            copy.wait()

        def step(i, carry, side=side):
            rows_at = pl.ds(pl.multiple_of(i * tile, tile), tile)
            own, near = 2 * side, 2 * side + 1
            pre = dot_nn(normed_two[rows_at, :half], gate_up_here[own][...]) + dot_nn(
                normed_two[rows_at, half:], gate_up_here[near][...]
            )
            grad = dot_nn(cot[rows_at, :half], down_here[own][...]) + dot_nn(
                cot[rows_at, half:], down_here[near][...]
            )
            gate, up = pre[:, :units], pre[:, units:]
            act = sigmoid(gate)
            silu = gate * act
            acts[side][rows_at, :] = (silu * up).astype(jnp.bfloat16)
            grads[side][rows_at, :units] = (
                grad * up * act * (1.0 + gate * (1.0 - act))
            ).astype(jnp.bfloat16)
            grads[side][rows_at, units:] = (grad * silu).astype(jnp.bfloat16)
            for i_near in range(2):
                part = contract_last(
                    grads[side][rows_at, :], gate_up_here[2 * side + i_near][...]
                )
                columns = slice(i_near * half, (i_near + 1) * half)
                total[rows_at, columns] = part if side == 0 else total[rows_at, columns] + part
            return carry

        lax.fori_loop(0, 2, step, 0)
    rows = two_parts[0].shape[0]
    for i in range(8):
        two_parts[i][...] = total[i * rows : (i + 1) * rows, :].astype(jnp.bfloat16)


def down_kernel(*refs):
    acts, down, parts, total = refs[:2], refs[2:6], refs[6:10], refs[10]
    half = total.shape[1] // 2
    for near in range(2):
        total[:, near * half : (near + 1) * half] = contract_last(
            acts[0][...], down[near][...]
        ) + contract_last(acts[1][...], down[2 + near][...])
    rows = parts[0].shape[0]
    for i in range(4):
        parts[i][...] = total[i * rows : (i + 1) * rows, :].astype(jnp.bfloat16)


def attend_back_kernel(*refs):
    chunks, outs_w, pairs = refs[:8], refs[8:12], refs[12:16]
    bounds, key_ids, query_rot, query_pre, gate_pre, attended, log_total = refs[16:23]
    cosine, sine, qgain = refs[23:26]
    branch, grad_gate, grad_query, grad_pairs, gain_part = refs[26:31]
    gated_grad, keys_acc, vals_acc = refs[31:]
    scale = HEAD_WIDTH ** (-0.5)
    rows = chunks[0].shape[0]
    for i in range(8):
        branch[i * rows : (i + 1) * rows, :] = chunks[i][...]
    half = branch.shape[1] // 2
    for side in range(2):
        gated_grad[side] = dot_nn(branch[:, :half], outs_w[2 * side][:, HEAD_WIDTH:]) + dot_nn(
            branch[:, half:], outs_w[2 * side + 1][:, HEAD_WIDTH:]
        )
    keys_acc[...] = jnp.zeros_like(keys_acc)
    vals_acc[...] = jnp.zeros_like(vals_acc)
    gain_part[...] = jnp.zeros_like(gain_part)
    rows = pairs[0].shape[0]
    tile = rows // 2

    def step(i, carry):
        head, at = i // 2, pl.multiple_of(i % 2 * tile, tile)
        rows_at = pl.ds(at, tile)
        grad = gated_grad[head, rows_at, :]
        gate = sigmoid(gate_pre[head, rows_at, :])
        out = attended[head, rows_at, :]
        grad_gate[head, rows_at, :] = (grad * out * gate * (1.0 - gate)).astype(jnp.bfloat16)
        grad_out = (grad * gate).astype(jnp.bfloat16)
        delta = jnp.sum(grad_out.astype(jnp.float32) * out, axis=1, keepdims=True)
        query = query_rot[head, rows_at, :]
        start, last = bounds[rows_at, 0:1], bounds[rows_at, 1:2]
        log = log_total[head, rows_at, 0:1]
        grad_rot = jnp.zeros((tile, HEAD_WIDTH), jnp.float32)
        for j, pair in enumerate(pairs):
            ids = key_ids[:, j * rows : (j + 1) * rows]
            allowed = (ids >= start) & (ids <= last)
            keys, vals = pair[:, :HEAD_WIDTH], pair[:, HEAD_WIDTH:]
            score = jnp.where(allowed, contract_last(query, keys) * scale, masked_score)
            weight = jnp.exp(score - log)
            grad_score = (weight * (contract_last(grad_out, vals) - delta)).astype(jnp.bfloat16)
            grad_rot = grad_rot + dot_nn(grad_score, keys)
            at_keys = slice(j * rows, (j + 1) * rows)
            keys_acc[at_keys, :] += contract_first(grad_score, query)
            vals_acc[at_keys, :] += contract_first(weight.astype(jnp.bfloat16), grad_out)
        grad_rot = (grad_rot * scale).astype(jnp.bfloat16).astype(jnp.float32)
        grad_unit = turned_back(grad_rot, cosine[rows_at, :], sine[rows_at, :])
        pre = query_pre[head, rows_at, :]
        inverse = lax.rsqrt(jnp.mean(pre * pre, axis=1, keepdims=True) + epsilon)
        gain_part[...] += jnp.sum(grad_unit * (pre * inverse), axis=0, keepdims=True)
        grad_query[head, rows_at, :] = norm_back(grad_unit, pre, inverse, qgain[...]).astype(
            jnp.bfloat16
        )
        return carry

    lax.fori_loop(0, 4, step, 0)
    grad_pairs[:, :HEAD_WIDTH] = (keys_acc[...] * scale).astype(jnp.bfloat16)
    grad_pairs[:, HEAD_WIDTH:] = vals_acc[...].astype(jnp.bfloat16)


def tables_kernel(lengths, coords, frequency, bounds, key_ids, angles):
    far, near, x, y, c = (coords[i] for i in range(5))
    rows = bounds.shape[0] // 8

    def ids_of(at, near_at, c_at):
        chunk, row = at // rows, at % rows
        x_at, y_at, far_at = x ^ (chunk // 4), y ^ (chunk // 2 % 2), far ^ (chunk % 2)
        return (((far_at * 2 + near_at) * 2 + x_at) * 4 + y_at * 2 + c_at) * rows + row

    at = lax.broadcasted_iota(jnp.int32, bounds.shape, 0)
    lane = lax.broadcasted_iota(jnp.int32, bounds.shape, 1)
    ids = ids_of(at, near, c)
    start = jnp.zeros_like(ids)
    end = jnp.int32(0)
    for i in range(lengths.shape[0]):
        end = end + lengths[i]
        start = jnp.where(ids >= end, end, start)
    bounds[...] = jnp.where(lane == 0, start, ids)
    angles[...] = (ids - start).astype(jnp.float32) * frequency[...]
    at = lax.broadcasted_iota(jnp.int32, key_ids.shape, 1)
    group = at // (8 * rows)
    key_ids[...] = ids_of(at % (8 * rows), near ^ (group % 2), c ^ (group // 2))


def gate_kernel(normed, mine_own, mine_near, other_own, other_near, gate_pre):
    half = normed.shape[1] // 2
    for i, (own, near) in enumerate(((mine_own, mine_near), (other_own, other_near))):
        gate_pre[i] = dot_nn(normed[:, :half], own[:, :HEAD_WIDTH]) + dot_nn(
            normed[:, half:], near[:, :HEAD_WIDTH]
        )


def input_kernel(flag, *refs):
    own_pair, got_pair, key_pre, cosine, sine, kgain, grad_query, grad_gate, normed = refs[:9]
    qk, og = refs[9:13], refs[13:17]
    grad_qk, parts, key_gain, input_gain, total = refs[17:19], refs[19:27], refs[27], refs[28], refs[29]
    pair = own_pair[...].astype(jnp.float32) + got_pair[...].astype(jnp.float32)
    grad_unit = turned_back(
        pair[:, :HEAD_WIDTH].astype(jnp.bfloat16).astype(jnp.float32), cosine[...], sine[...]
    )
    pre = key_pre[...]
    inverse = lax.rsqrt(jnp.mean(pre * pre, axis=1, keepdims=True) + epsilon)
    key_gain[...] = jnp.sum(grad_unit * (pre * inverse), axis=0, keepdims=True)
    grad_key = norm_back(grad_unit, pre, inverse, kgain[...]).astype(jnp.bfloat16)
    grad_value = pair[:, HEAD_WIDTH:].astype(jnp.bfloat16)
    swapped = flag[0] == 1
    for side in range(2):
        grad_qk[side][:, :HEAD_WIDTH] = grad_query[side]
        first, second = (grad_key, grad_value) if side == 0 else (grad_value, grad_key)
        grad_qk[side][:, HEAD_WIDTH:] = jnp.where(swapped, second, first)
    half = total.shape[1] // 2
    tile = total.shape[0] // 2

    def step(i, carry):
        rows_at = pl.ds(pl.multiple_of(i * tile, tile), tile)
        for near in range(2):
            acc = None
            for side in range(2):
                part = contract_last(grad_qk[side][rows_at, :], qk[2 * side + near][...])
                part = part + contract_last(
                    grad_gate[side, rows_at, :], og[2 * side + near][:, :HEAD_WIDTH]
                )
                acc = part if acc is None else acc + part
            total[rows_at, near * half : (near + 1) * half] = acc
        return carry

    lax.fori_loop(0, 2, step, 0)
    rows = parts[0].shape[0]
    gain = jnp.zeros(input_gain.shape, jnp.float32)
    for i in range(8):
        part = total[i * rows : (i + 1) * rows, :]
        parts[i][...] = part.astype(jnp.bfloat16)
        gain = gain + jnp.sum(
            part * normed[i * rows : (i + 1) * rows, :].astype(jnp.float32), axis=0, keepdims=True
        )
    input_gain[...] = gain


def on_slice_device(
    hidden_in,
    out_cotangent,
    doc_lengths,
    query_weight,
    key_matrix,
    value_matrix,
    gate_weight,
    out_weight,
    ffn_gate_weight,
    ffn_up_weight,
    ffn_down_weight,
    attn_gain,
    ffn_gain,
    query_gain,
    key_gain,
):
    bf16, f32 = jnp.bfloat16, jnp.float32
    block_rows, width = hidden_in.shape
    chunk_rows = block_rows // 4
    tokens = 8 * chunk_rows
    low = HEAD_WIDTH
    units = ffn_gate_weight.shape[1] // PLANES
    coords = [lax.axis_index(name) for name in ("far", "near", "x", "y", "c")]
    far, near, x, y, c = coords
    odd_near = near == 1
    core_flag = c.reshape(1)

    def columns(x_at, head):
        at = (2 * x_at + head) * low
        third = (key_matrix if head == 0 else value_matrix)[:, x_at * low : (x_at + 1) * low]
        parts = (query_weight[:, at : at + low], third)
        parts += (gate_weight[:, at : at + low], out_weight[:, at : at + low])
        return jnp.concatenate(parts, axis=1)

    own_hidden = to_own_first(
        lax.dynamic_slice_in_dim(hidden_in, (y * 2 + c) * chunk_rows, chunk_rows, 0), odd_near
    )
    hidden = gather_chunks(own_hidden)
    attn_half, attn_sent = to_head_owners(
        jnp.stack([jnp.stack([columns(i, j) for j in range(2)]) for i in range(2)]), far, x, c
    )
    qk_half, og_half = attn_half[:, : 2 * low], attn_half[:, 2 * low :]
    qk_near = pair_swap(qk_half, "near")
    og_near = pair_swap(after(og_half, qk_near), "near")
    qk = [qk_half, qk_near, pair_swap(qk_half, "c"), pair_swap(after(qk_near, hidden), "c")]
    gain_one = to_own_first(attn_gain, odd_near)
    out_cotangent, ffn_gain = after((out_cotangent, ffn_gain), hidden[1])
    cotangent = to_own_first(
        lax.dynamic_slice_in_dim(out_cotangent, (y * 2 + c) * chunk_rows, chunk_rows, 0), odd_near
    )
    gain_two = to_own_first(ffn_gain, odd_near)
    cotangent_far = pair_swap(cotangent, "far")
    hidden, cotangent_far = after((hidden, cotangent_far))
    ffn_gate_weight, ffn_up_weight, ffn_down_weight = after(
        (ffn_gate_weight, ffn_up_weight, ffn_down_weight), qk_near, hidden, cotangent_far
    )
    cotangent_pair = jnp.concatenate([cotangent, cotangent_far], axis=0)
    cotangents = [cotangent_pair] + [side_swap(cotangent_pair, i) for i in range(1, 4)]

    def by_plane(*weights):
        return jnp.stack(
            [
                jnp.concatenate([w[:, p * units : (p + 1) * units] for w in weights], axis=1)
                for p in range(PLANES)
            ]
        )

    gate_up_half = to_plane_owners(by_plane(ffn_gate_weight, ffn_up_weight))

    half_width = low // 2
    frequency = rope_base ** (-2.0 * jnp.arange(half_width, dtype=f32) / low)
    frequency = jnp.concatenate([frequency, frequency])[None, :]
    bounds, key_ids, angles = pl.pallas_call(
        tables_kernel,
        out_shape=[
            shaped((tokens, low), jnp.int32),
            shaped((1, 4 * tokens), jnp.int32),
            shaped((tokens, low), f32),
        ],
        in_specs=[pl.BlockSpec(memory_space=pltpu.SMEM)] * 2
        + [pl.BlockSpec(memory_space=pltpu.VMEM)],
        out_specs=[pl.BlockSpec(memory_space=pltpu.VMEM)] * 3,
    )(after(doc_lengths, qk_near), jnp.stack(coords), frequency)
    sign = jnp.where(jnp.arange(low) < half_width, -1.0, 1.0).astype(f32)
    cosine, sine = jnp.cos(angles), jnp.sin(angles) * sign[None, :]
    query_gain, key_gain = query_gain[None, :], key_gain[None, :]

    normed, pair, query_rot, query_pre, key_pre = kernel_call(
        project_kernel,
        hidden + [gain_one[None, :]] + qk + [cosine, sine, query_gain, key_gain],
        [
            shaped((tokens, width), bf16),
            shaped((tokens, 2 * low), bf16),
            shaped((2, tokens, low), bf16),
            shaped((2, tokens, low), f32),
            shaped((tokens, low), f32),
        ],
        [pltpu.VMEM((2, tokens, 2 * low), f32)],
        core_flag,
        4 * tokens * width * 2 * low,
    )
    pair_near = pair_swap(pair, "near")
    pairs = [pair, pair_near, pair_swap(pair, "c"), pair_swap(pair_near, "c")]

    og = [og_half, og_near] + [pair_swap(after(part, pair), "c") for part in (og_half, og_near)]
    gate_up_near = pair_swap(after(gate_up_half, pair_near), "near")
    down_half = to_plane_owners(after(by_plane(ffn_down_weight), gate_up_half))
    query_rot, cotangents, gate_up_half = after((query_rot, cotangents, gate_up_half))

    (gate_pre,) = kernel_call(
        gate_kernel,
        [normed] + og,
        [shaped((2, tokens, low), f32)],
        flops=4 * tokens * width * low,
    )
    outs = kernel_call(
        attend_kernel,
        [query_rot] + pairs + [bounds, key_ids, gate_pre] + og,
        [shaped((2, tokens, low), bf16)]
        + [shaped((2, tokens, low), f32)] * 2
        + [shaped((chunk_rows, width), bf16)] * 8,
        [pltpu.VMEM((tokens, width), f32)],
        None,
        8 * tokens * 4 * tokens * low,
    )
    gated, attended, log_total, branch_parts = outs[0], outs[1], outs[2], outs[3:]
    away, own = sum_sends(branch_parts)
    away, gate_up_near, down_half = after((sum_pieces(away).astype(bf16), gate_up_near, down_half))
    hidden32 = own_hidden.astype(f32)
    middle = hidden32 + sum_pieces(own + [pair_swap(away, "far")])
    inv_two = lax.rsqrt(jnp.mean(middle * middle, axis=1, keepdims=True) + epsilon)
    normed_two_chunk = (middle * inv_two * gain_two).astype(bf16)
    normed_two_pieces = gather_chunks(normed_two_chunk)
    gate_up = [
        gate_up_half,
        gate_up_near,
        pair_swap(gate_up_half, "c"),
        pair_swap(gate_up_near, "c"),
    ]
    down_near = pair_swap(after(down_half, gate_up_near), "near")
    down = [down_half, down_near, pair_swap(down_half, "c"), pair_swap(down_near, "c")]

    outs = kernel_call(
        ffn_kernel,
        normed_two_pieces + cotangents + gate_up + down,
        [shaped((tokens, units), bf16)] * 2
        + [shaped((tokens, 2 * units), bf16)] * 2
        + [shaped((chunk_rows, width), bf16)] * 8,
        [pltpu.VMEM((tokens, width), bf16)] * 2
        + [pltpu.VMEM((tokens, width), f32)]
        + [pltpu.VMEM((width // 2, 2 * units), bf16)] * 4
        + [pltpu.VMEM((width // 2, units), bf16)] * 4
        + [pltpu.SemaphoreType.DMA((8,))],
        None,
        20 * tokens * width * units,
        8,
    )
    hidden_acts, grad_ffn, two_parts = outs[:2], outs[2:4], outs[4:12]
    away, own = sum_sends(two_parts)
    two_far = pair_swap(sum_pieces(away).astype(bf16), "far")
    pieces_late, hidden_acts, grad_ffn, cotangents = after(
        (normed_two_pieces, hidden_acts, grad_ffn, cotangents), two_parts[1]
    )
    normed_two = jnp.concatenate(pieces_late, axis=0)
    all_cotangent = jnp.concatenate(cotangents, axis=0)
    down_parts = kernel_call(
        down_kernel,
        list(hidden_acts) + list(down),
        [shaped((2 * chunk_rows, width), bf16)] * 4,
        [pltpu.VMEM((tokens, width), f32)],
        None,
        4 * tokens * width * units,
    )
    two_away = own, two_far
    gate_up_both = core_sum(*(contract_first(normed_two, g).astype(bf16) for g in grad_ffn))
    down_both = core_sum(*(contract_first(all_cotangent, act).astype(bf16) for act in hidden_acts))

    (own, two_far), down_both, gate_up_both = after((two_away, down_both, gate_up_both))
    grad_normed_two = sum_pieces(own + [two_far])

    def whole_block(chunk):
        chunk = from_own_first(chunk, odd_near)
        other = pair_swap(chunk, "y")
        by_y = jnp.stack([chunk, other])
        by_core = jnp.stack([by_y, pair_swap(by_y, "c")], axis=1)
        whole = flip_if(flip_if(by_core, 1, c == 1), 0, y == 1).reshape(block_rows, width)
        return other, whole

    grad_middle = cotangent.astype(f32) + norm_back(grad_normed_two, middle, inv_two, gain_two)
    grad_branch = grad_middle.astype(bf16)
    branch_pieces = gather_chunks(grad_branch)
    down_parts = after(down_parts, branch_pieces)
    down_pieces = [down_parts[0]] + [side_swap(down_parts[i], i) for i in range(1, 4)]
    half = width // 2
    gate_up_got = pair_swap(gate_up_both[half:], "near")

    all_branch, grad_gate, grad_query, grad_pairs, query_gain_part = kernel_call(
        attend_back_kernel,
        branch_pieces
        + og
        + pairs
        + [bounds, key_ids, query_rot, query_pre, gate_pre, attended, log_total]
        + [cosine, sine, query_gain],
        [
            shaped((tokens, width), bf16),
            shaped((2, tokens, low), bf16),
            shaped((2, tokens, low), bf16),
            shaped((4 * tokens, 2 * low), bf16),
            shaped((1, low), f32),
        ],
        [
            pltpu.VMEM((2, tokens, low), f32),
            pltpu.VMEM((4 * tokens, low), f32),
            pltpu.VMEM((4 * tokens, low), f32),
        ],
        None,
        20 * tokens * 4 * tokens * low,
    )
    pair_other = pair_swap(grad_pairs[2 * tokens :], "c")
    gate_up_got, normed_later = after((gate_up_got, normed), grad_pairs)
    near_pairs = grad_pairs[: 2 * tokens].astype(f32) + pair_other.astype(f32)
    near_pairs = near_pairs.astype(bf16)
    pair_got = pair_swap(near_pairs[tokens:], "near")
    gate_up_rows = near_add(gate_up_both, gate_up_got)
    down_got = pair_swap(after(down_both, pair_got)[half:], "near")
    gate_up_grad = to_row_owners(gate_up_rows)
    og_both = core_sum(
        *(
            jnp.concatenate(
                [
                    contract_first(normed_later, grad_gate[i]).astype(bf16),
                    contract_first(all_branch, gated[i]).astype(bf16),
                ],
                axis=1,
            )
            for i in range(2)
        )
    )
    key_pre, gate_up_rows = after((key_pre, gate_up_rows))
    og_got = pair_swap(after(og_both, pair_got)[half:], "near")
    outs = kernel_call(
        input_kernel,
        [near_pairs[:tokens], pair_got, key_pre, cosine, sine, key_gain]
        + [grad_query, grad_gate, normed]
        + qk
        + og,
        [shaped((tokens, 2 * low), bf16)] * 2
        + [shaped((chunk_rows, width), bf16)] * 8
        + [shaped((1, low), f32), shaped((1, width), f32)],
        [pltpu.VMEM((tokens, width), f32)],
        core_flag,
        12 * tokens * width * low,
    )
    grad_qk, normed_parts, key_gain_part, input_gain_part = outs[:2], outs[2:10], outs[10], outs[11]
    away, own = sum_sends(normed_parts)
    away = sum_pieces(away).astype(bf16)
    qk_sides = [contract_first(normed, g).astype(bf16) for g in after(grad_qk, normed_parts[1])]
    qk_other = pair_swap(qk_sides[1], "c")
    away, qk_other, gate_up_grad = after((away, qk_other, gate_up_grad))
    qk_both = (qk_sides[0].astype(f32) + qk_other.astype(f32)).astype(bf16)
    qk_got = pair_swap(qk_both[half:], "near")
    grad_far = pair_swap(away, "far")
    grad_far, down_got = after((grad_far, down_got))
    down_pieces = after(down_pieces, grad_far)
    down_sums = sum_pieces(down_pieces)
    down_far = pair_swap(down_sums[chunk_rows:].astype(bf16), "far")
    down_rows = near_add(down_both, down_got)
    grad_far, qk_got = after((grad_far, qk_got))
    grad_normed = sum_pieces(own + [grad_far])
    inv_one = lax.rsqrt(jnp.mean(hidden32 * hidden32, axis=1, keepdims=True) + epsilon)
    input_chunk = (grad_middle + norm_back(grad_normed, hidden32, inv_one, gain_one)).astype(bf16)
    input_y, input_grad = whole_block(input_chunk)
    og_got = after(og_got, grad_far)
    gain_parts = after((input_gain_part, query_gain_part, key_gain_part), input_y)
    down_far = after(down_far, grad_far)
    attn_rows = jnp.concatenate([near_add(qk_both, qk_got), near_add(og_both, og_got)], axis=1)
    attn_grad = from_head_owners(attn_rows, far, x, c)
    down_grad = to_row_owners(after(down_rows, grad_far, gate_up_grad))
    qk_grad, og_grad = attn_grad[..., : 2 * low], attn_grad[..., 2 * low :]
    layer_y, layer_out = whole_block(
        (middle + down_sums[:chunk_rows] + down_far.astype(f32)).astype(bf16)
    )
    gains = jnp.concatenate(
        [
            from_own_first(gain_parts[0][0] / gain_one, odd_near),
            from_own_first(jnp.sum(grad_normed_two * middle * inv_two, axis=0), odd_near),
            gain_parts[1][0],
            gain_parts[2][0],
        ]
    )
    gains = (gains + plane_swap(gains, 1)) + (plane_swap(gains, 2) + plane_swap(gains, 3))
    for axis in ("y", "c", "near"):
        gains = gains + pair_swap(gains, axis)

    def per_head(grad, start):
        columns = [grad[i, j, :, start : start + low] for i in range(2) for j in range(2)]
        return jnp.concatenate(columns, axis=1).astype(f32)

    def per_group(grad, j):
        return jnp.concatenate([grad[0, j, :, low:], grad[1, j, :, low:]], axis=1).astype(f32)

    def flat(grad):
        return jnp.concatenate([grad[p] for p in range(PLANES)], axis=1).astype(f32)

    return (
        layer_out,
        input_grad,
        per_head(qk_grad, 0),
        per_group(qk_grad, 0),
        per_group(qk_grad, 1),
        per_head(og_grad, 0),
        per_head(og_grad, low),
        flat(gate_up_grad[:, :, :units]),
        flat(gate_up_grad[:, :, units:]),
        flat(down_grad),
        gains[:width],
        gains[width : 2 * width],
        gains[2 * width : 2 * width + low],
        gains[2 * width + low :],
    )


def solution(mesh):
    wide, head = mesh.shape["wide"], mesh.shape["head"]
    if wide == 2 * PLANES and head == 4:
        devices = mesh.devices.reshape(2, 2, 2, 2, 2)
        mesh = Mesh(devices, ("far", "near", "x", "y", "c"))
        program, rows, columns = on_slice_device, ("far", "near", "x"), ("y", "c")
    else:
        program, rows, columns = on_device, "wide", "head"
    tokens, weight = P(rows, None), P(rows, columns)
    return jax.shard_map(
        program,
        mesh=mesh,
        in_specs=(tokens, tokens, P()) + (weight,) * 8 + (P(),) * 4,
        out_specs=(tokens, tokens) + (weight,) * 8 + (P(),) * 4,
        check_vma=False,
    )
```
